256 devices in a mesh: space: 64 (over y, z, core), chan: 4 (over x).
Axes of the slice: x: 4, y: 4, z: 8, core: 2. Of those that a mesh axis runs over, the one named last changes fastest.
Arguments:
- point_feats: bfloat16 [64, 65536], P('chan', 'space'), may hold values from -6 to 6
- point_owner: int32 [65536, 1], P('space'), may hold values from 0 to 63; in each aligned block of 1024 rows (0 to 1023, 1024 to 2047, ...) at most 32 rows name the same one
- point_place: int32 [65536], P('space'), may hold values from 0 to 2047
- neighbors: int32 [256, 6], P('space'), may hold values from -1 to 255, as said below
- weight_in: bfloat16 [64, 27, 96], P('chan'), may hold values from -0.15625 to 0.15625
- weight_mid: bfloat16 [96, 27, 96], P('chan'), may hold values from -0.125 to 0.125
Outputs:
- brick_feats: bfloat16 [96, 256, 512], P('chan', 'space')
- point_out: bfloat16 [96, 65536], P('chan', 'space')
The draws below stay inside these ranges and needn't reach their ends.
Inputs may be any that keep to these rules, and one draw needn't show every extreme that they name: `point_owner`: among the points of one index of space, at most 32 have the same owner, and in some index of space exactly 32 points have one owner. `neighbors`: A listed brick's owner index along space (id // 4) differs from the listing brick's by at most one; if brick a lists b at face f, then b lists a at face f xor 1.
All inputs are finite; a program needn't handle non-finite values.
Results may differ from the reference program's by a relative error of at most 0.01.
Values may be sent and summed in bfloat16 or wider, within the bound.
A program may use at most 384 MiB of HBM per device.

```python
import math
import jax
import jax.numpy as jnp
import numpy as np
from jax import lax

CIN = 64
CH = 96
SIDE = 8
VOX = 512
B_DEV = 4
P_DEV = 1024
BRICKS = 256
POINTS = 65536
CAP = 32
N_SPACE = 64


def draw_neighbors(key, part):
    devices = BRICKS // B_DEV
    half = B_DEV // 2
    scores = jax.random.randint(jax.random.fold_in(key, 11), (devices, B_DEV), 0, 1 << 20) * B_DEV + jnp.arange(B_DEV, dtype=jnp.int32)[None, :]
    stored_slot = jnp.argsort(scores, axis=1).astype(jnp.int32)
    slot_store = jnp.argsort(stored_slot, axis=1).astype(jnp.int32)
    open_x = jax.random.randint(jax.random.fold_in(key, 12), (devices, B_DEV), 0, 4) > 0
    open_y = jax.random.randint(jax.random.fold_in(key, 13), (devices, B_DEV), 0, 4) > 0
    open_z = jax.random.randint(jax.random.fold_in(key, 14), (devices, B_DEV), 0, 4) > 0
    device_ids = jnp.broadcast_to(jnp.arange(devices, dtype=jnp.int32)[:, None], (devices, B_DEV))
    slot_ids = jnp.broadcast_to(jnp.arange(B_DEV, dtype=jnp.int32)[None, :], (devices, B_DEV))
    lat_y = slot_ids % 2
    lat_z = slot_ids // 2

    def lookup_bits(table, dev_at, slot_at):
        return table[jnp.clip(dev_at, 0, devices - 1), jnp.clip(slot_at, 0, B_DEV - 1)]
    options = [(device_ids - 1, slot_ids, (device_ids > 0) & lookup_bits(open_x, device_ids - 1, slot_ids)), (device_ids + 1, slot_ids, (device_ids < devices - 1) & lookup_bits(open_x, device_ids, slot_ids)), (device_ids, slot_ids - 1, (lat_y == 1) & lookup_bits(open_y, device_ids, slot_ids - 1)), (device_ids, slot_ids + 1, (lat_y == 0) & lookup_bits(open_y, device_ids, slot_ids)), (device_ids, slot_ids - 2, (lat_z > 0) & lookup_bits(open_z, device_ids, slot_ids - 2)), (device_ids, slot_ids + 2, (lat_z < half - 1) & lookup_bits(open_z, device_ids, slot_ids))]
    columns = []
    for dev_at, slot_at, usable in options:
        safe_dev = jnp.clip(dev_at, 0, devices - 1)
        safe_slot = jnp.clip(slot_at, 0, B_DEV - 1)
        global_id = safe_dev * B_DEV + slot_store[safe_dev, safe_slot]
        columns.append(jnp.where(usable, global_id, -1))
    lattice = jnp.stack(columns, 2)
    stored = jnp.take_along_axis(lattice, stored_slot[:, :, None], axis=1)
    return stored.reshape(BRICKS, 6).astype(jnp.int32)


def touch_ends(array, key, smallest, high):
    spot = [jax.random.randint(jax.random.fold_in(key, axis), (), 0, length) for axis, length in enumerate(array.shape)]
    longest = array.shape.index(max(array.shape))
    next_to = spot[:longest] + [(spot[longest] + 1) % array.shape[longest]] + spot[longest + 1:]
    return array.at[tuple(spot)].set(smallest).at[tuple(next_to)].set(high)


def level_of(rng, shape, shards, least, high):
    def one(position, parts):
        heights = jax.random.uniform(jax.random.fold_in(jax.random.fold_in(rng, 6), position), (parts,), jnp.float32, least / len(shards), high / len(shards))
        return jnp.repeat(jnp.exp(heights), shape[position] // parts).reshape((-1,) + (1,) * (len(shape) - position - 1))

    gain = one(*shards[0])
    for cut in shards[1:]:
        gain = gain * one(*cut)
    return gain


def shared_out(own_key, own, number, rows, number_of, top, bound, slope):
    sequence = jax.random.permutation(own_key, number_of)
    heavy_load, ordinary = shares(number_of, rows * top, bound, slope, True), shares(number_of, rows * top, bound, slope, False)
    places = jnp.arange(number_of)

    def named(sizes, turn):
        used = int((sizes > 0).sum())
        fixed = max(1, used // 4)
        moved = fixed + (places - fixed + turn * (used - fixed)) % max(1, number_of - fixed)
        return jnp.zeros((number_of,), jnp.int32).at[sequence[jnp.where(places < fixed, places, moved)]].set(jnp.asarray(sizes, jnp.int32))

    sizes = jnp.where(number % 4 == 0, named(heavy_load, number // 4), named(ordinary, number - number // 4 - 1))
    mixed = jax.random.permutation(jax.random.fold_in(own, 3), number_of)
    source_of, taker = mixed[0:number_of // 2 * 2:2], mixed[1:number_of // 2 * 2:2]
    slack = jnp.minimum(sizes[source_of] - 1, bound - sizes[taker]) // 2
    slack = jnp.where((source_of == sequence[0]) | (taker == sequence[0]) | (sizes[taker] == 0), 0, jnp.maximum(slack, 0))
    moved = jax.random.randint(jax.random.fold_in(own, 4), (number_of // 2,), 0, 1 << 20) % (slack + 1)
    sizes = sizes.at[source_of].add(-moved).at[taker].add(moved)
    members = jnp.searchsorted(jnp.cumsum(sizes), jnp.arange(rows * top), side="right").astype(jnp.int32)
    table = members.reshape(top, rows).T
    table = table[jax.random.permutation(jax.random.fold_in(own, 1), rows)]
    turn = jax.random.randint(jax.random.fold_in(own, 2), (rows, 1), 0, top)
    return jnp.take_along_axis(table, (jnp.arange(top)[None, :] + turn) % top, axis=1)


def shares(number_of, total, limit, lean, full):
    loads = [(1 << 20) // math.isqrt(grade ** lean) + 1 for grade in range(1, number_of + 1)]
    largest = limit if full else min(limit, max(-(-total // number_of), total * loads[0] // sum(loads)))
    least = 1 if total - largest >= number_of - 1 else 0
    counts, surplus = [largest] + [least] * (number_of - 1), total - largest - least * (number_of - 1)
    while surplus > 0:
        free = [i for i in range(1, number_of) if counts[i] < largest] or [i for i in range(1, number_of) if counts[i] < limit]
        mass, left = sum([loads[i] for i in free]), surplus
        for i in free:
            addition = min(limit - counts[i], max(1, left * loads[i] // mass), surplus)
            counts[i] = counts[i] + addition
            surplus = surplus - addition
    return np.array(counts)


def noise(stream_key, shape, deviation, limit, cuts=(), held_as=jnp.bfloat16):
    level = level_of(stream_key, shape, cuts, -0.22, 0.18) if cuts else 1.0
    drawn = jax.random.normal(stream_key, shape, jnp.float32) * deviation * level
    return jnp.minimum(jnp.maximum(drawn, -limit), limit).astype(held_as)


def setup_inputs(seed: int = 0) -> dict:
    arg_keys = jax.random.split(jax.random.key(seed), 7)
    point_feats = noise(arg_keys[0], (CIN, POINTS), 1.0, 6.0, ((0, 4), (1, 64)))
    point_owner_keys = jax.random.split(jax.random.fold_in(arg_keys[1], 1), POINTS // P_DEV)
    point_owner_turns = jax.random.permutation(jax.random.fold_in(arg_keys[1], 3), POINTS // P_DEV)
    point_owner = jax.vmap(lambda own, number: shared_out(jax.random.fold_in(arg_keys[1], 2), own, number, P_DEV, N_SPACE, 1, CAP, 2))(point_owner_keys, point_owner_turns).reshape((POINTS, 1))
    point_place = touch_ends(jax.random.randint(arg_keys[2], (POINTS,), 0, B_DEV * VOX), jax.random.fold_in(arg_keys[2], 1), 0, (B_DEV * VOX) - 1).astype(jnp.int32)
    neighbors = draw_neighbors(jax.random.fold_in(arg_keys[6], 71), 0)
    weight_in = noise(arg_keys[4], (CIN, 27, CH), (27 * CIN) ** -0.5, 0.15625, ((0, 4),))
    weight_mid = noise(arg_keys[5], (CH, 27, CH), (27 * CH) ** -0.5, 0.125, ((0, 4),))
    return {"point_feats": point_feats, "point_owner": point_owner, "point_place": point_place, "neighbors": neighbors, "weight_in": weight_in, "weight_mid": weight_mid}


def outbound(voxel_grid):
    chans, bricks = voxel_grid.shape[0], voxel_grid.shape[1]
    layers = [voxel_grid[:, :, 0], voxel_grid[:, :, -1], voxel_grid[:, :, :, 0], voxel_grid[:, :, :, -1], voxel_grid[:, :, :, :, 0], voxel_grid[:, :, :, :, -1]]
    return jnp.stack(layers, 2).reshape(chans, bricks * 6, SIDE * SIDE)


def neighbour_faces(face_table, lookup, present):
    chans = face_table.shape[0]
    bricks = lookup.shape[0]
    fetched = jnp.take(face_table, lookup.reshape(-1), axis=1)
    fetched = fetched * present.reshape(1, -1, 1).astype(fetched.dtype)
    return fetched.reshape(chans, bricks, 6, SIDE, SIDE)


def assemble(voxel_grid, fetched):
    chans, bricks = voxel_grid.shape[0], voxel_grid.shape[1]
    padded = jnp.zeros((chans, bricks, SIDE + 2, SIDE + 2, SIDE + 2), voxel_grid.dtype)
    padded = padded.at[:, :, 1:-1, 1:-1, 1:-1].set(voxel_grid)
    padded = padded.at[:, :, 0, 1:-1, 1:-1].set(fetched[:, :, 0])
    padded = padded.at[:, :, -1, 1:-1, 1:-1].set(fetched[:, :, 1])
    padded = padded.at[:, :, 1:-1, 0, 1:-1].set(fetched[:, :, 2])
    padded = padded.at[:, :, 1:-1, -1, 1:-1].set(fetched[:, :, 3])
    padded = padded.at[:, :, 1:-1, 1:-1, 0].set(fetched[:, :, 4])
    padded = padded.at[:, :, 1:-1, 1:-1, -1].set(fetched[:, :, 5])
    return padded


def conv_ref(padded, weight):
    chans = padded.shape[0]
    weight_wide = weight.astype(jnp.float32)

    def per_brick(brick_id):
        single = lax.dynamic_index_in_dim(padded, brick_id, 1, keepdims=False)
        shifted = jnp.stack([single[:, step_x:step_x + SIDE, step_y:step_y + SIDE, step_z:step_z + SIDE] for step_x in range(3) for step_y in range(3) for step_z in range(3)], 0)
        shifted = shifted.reshape(27, chans, SIDE ** 3).astype(jnp.float32)
        return jnp.einsum("ctk,tcv->kv", weight_wide, shifted, precision=lax.Precision.HIGHEST)

    result = lax.map(per_brick, jnp.arange(BRICKS, dtype=jnp.int32))
    return jnp.transpose(result, (1, 0, 2))


def reference(point_feats, point_owner, point_place, neighbors, weight_in, weight_mid):
    voxels = SIDE ** 3
    target = (point_owner[:, 0] * (B_DEV * voxels) + point_place).astype(jnp.int32)
    totals = jax.ops.segment_sum(point_feats.astype(jnp.float32).T, target, num_segments=BRICKS * voxels)
    grid_in = totals.T.astype(jnp.bfloat16).reshape(CIN, BRICKS, SIDE, SIDE, SIDE)
    facing = jnp.bitwise_xor(jnp.arange(6, dtype=jnp.int32), 1)
    present = neighbors >= 0
    lookup = jnp.where(present, neighbors * 6 + facing[None, :], 0).astype(jnp.int32)

    def conv_layer(voxel_grid, weight):
        fetched = neighbour_faces(outbound(voxel_grid), lookup, present)
        return conv_ref(assemble(voxel_grid, fetched), weight)

    layer_one = jax.nn.relu(conv_layer(grid_in, weight_in)).astype(jnp.bfloat16)
    layer_grid = layer_one.reshape(CH, BRICKS, SIDE, SIDE, SIDE)
    brick_feats = jax.nn.relu(conv_layer(layer_grid, weight_mid) + layer_one.astype(jnp.float32)).astype(jnp.bfloat16)
    flattened = brick_feats.reshape(CH, BRICKS * voxels)
    point_out = jnp.take(flattened, target, axis=1)
    return brick_feats, point_out
```

```python
import functools

import jax
import jax.numpy as jnp
import numpy as np
from jax import lax
from jax.experimental import pallas as pl
from jax.experimental.pallas import tpu as pltpu
from jax.sharding import PartitionSpec as P

DEPTH = 8
PLANE = 8
CHAN = 4
CAP = 32
CELLS = 512
BRICKS = 4
VOX = BRICKS * CELLS
OUT = 24
TAPS = 9
F32 = jnp.float32
BF16 = jnp.bfloat16
MESH = pl.DeviceIdType.MESH


def tap_row(jl):
    return OUT * jl + (8 if jl >= 5 else 0)


ROWS = 224


def face_picker():
    sel = np.zeros((CELLS, 384), np.float32)
    for u in range(8):
        for w in range(8):
            for p in range(3):
                for half, end in ((0, 7), (1, 0)):
                    x, y, z = ((end, u, w), (u, end, w), (u, w, end))[p]
                    sel[(8 * x + y) * 8 + z, 128 * p + 64 * half + 8 * u + w] = 1
    return sel


def plane_spread():
    ec = np.zeros((128, 256), np.float32)
    for x in range(2):
        for y in range(8):
            for z in range(8):
                ec[64 * x + 8 * y + z, 128 * x + 10 * (y + 1) + z + 1] = 1
    return ec


def rim_spread():
    eh = np.zeros((256, 1024), np.float32)
    for x in range(8):
        for w in range(8):
            eh[8 * x + w, 128 * x + w + 1] = 1
            eh[64 + 8 * x + w, 128 * x + 90 + w + 1] = 1
            eh[128 + 8 * x + w, 128 * x + 10 * (w + 1)] = 1
            eh[192 + 8 * x + w, 128 * x + 10 * (w + 1) + 9] = 1
    return eh


def plane_pack():
    cm = np.zeros((256, 128), np.float32)
    for x in range(2):
        for y in range(8):
            for z in range(8):
                cm[128 * x + 10 * y + z, 64 * x + 8 * y + z] = 1
    return cm


def dot(a, b):
    return jnp.dot(a, b, preferred_element_type=F32)


def dot_lanes(a, b):
    return lax.dot_general(a, b, (((1,), (1,)), ((), ())), preferred_element_type=F32)


def one_hot(row, count):
    ids = lax.broadcasted_iota(jnp.int32, (count, row.shape[1]), 0).astype(F32)
    return jnp.where(ids == row, 1.0, 0.0).astype(BF16)


def swap_groups(parts):
    rows = parts[0].shape[0]
    tall = jnp.concatenate([p[:, 128 * m : 128 * m + 128] for p in parts for m in range(2)], 0)
    turned = [tall] + [pltpu.roll(tall, 32 * a, 1) for a in range(1, 4)]
    group = lax.broadcasted_iota(jnp.int32, (rows, 128), 1) // 32
    result = []
    for j in range(8):
        m, g = j // 4, j % 4
        tiles = []
        for t in range(2):
            tile = None
            for u in range(4):
                at = (2 * (4 * t + u) + m) * rows
                piece = turned[(u - g) % 4][at : at + rows]
                tile = piece if tile is None else jnp.where(group == u, piece, tile)
            tiles.append(tile)
        result.append(jnp.concatenate(tiles, 1))
    return result


def body(
    feats, owner, place, nbr, w_in, w_mid, sel, ec, eh, cm,
    grid_out, point_out,
    send_a, recv_a, send_b, recv_b, x_one, x_two, face_one, face_two, w_send_one, w_recv_one, w_send_two, w_recv_two,
    w_one, w_two, lot_p, hi_p, lot_s, hi_s, pad_one, pad_two, keep, ret_a, ret_b, ret_c, ret_v,
    sem_z, sem_j, sem_x, sem_f, sem_w, sem_rj, sem_rz,
):
    s = lax.axis_index("space")
    q = lax.axis_index("chan")
    core = s % 2
    z = (s // 2) % DEPTH
    row = s // (2 * DEPTH)
    plane = row * 2 + core
    spaces = 64

    def z_peer(d):
        return {"space": (row * DEPTH + (z + d) % DEPTH) * 2 + core, "chan": q}

    def j_peer(d):
        other = (plane + d) % PLANE
        return {"space": ((other // 2) * DEPTH + z) * 2 + other % 2, "chan": q}

    def x_peer(d):
        return {"space": s, "chan": (q + d) % CHAN}

    def s_peer(d):
        return {"space": (s + d + spaces) % spaces, "chan": q}

    started = []

    def send(src, dst, sems, at, peer):
        copy = pltpu.make_async_remote_copy(
            src_ref=src, dst_ref=dst, send_sem=sems.at[(0, *at)], recv_sem=sems.at[(1, *at)], device_id=peer, device_id_type=MESH
        )
        copy.start()
        started.append(copy)
        return copy

    peers = (
        [z_peer(d) for d in range(1, DEPTH)]
        + [j_peer(d) for d in range(1, PLANE)]
        + [x_peer(d) for d in range(1, CHAN)]
        + [s_peer(1), s_peer(-1)]
    )
    barrier = pltpu.get_barrier_semaphore()
    for peer in peers:
        pl.semaphore_signal(barrier, inc=1, device_id=peer, device_id_type=MESH)

    own = owner[...]
    where_to = place[...]
    match = jnp.where(lax.broadcasted_iota(jnp.int32, (64, 1024), 0) == own, 1.0, 0.0)
    tall = jnp.concatenate([match[:, 256 * i : 256 * i + 256] for i in range(4)], 0)
    before = jnp.where(
        lax.broadcasted_iota(jnp.int32, (256, 256), 0) < lax.broadcasted_iota(jnp.int32, (256, 256), 1), 1.0, 0.0
    )
    earlier = dot(tall.astype(BF16), before.astype(BF16))
    carry = jnp.zeros((64, 1), F32)
    ranks = []
    for i in range(4):
        mine = tall[64 * i : 64 * i + 64]
        ranks.append(jnp.sum(mine * (earlier[64 * i : 64 * i + 64] + carry), axis=0, keepdims=True))
        carry = carry + jnp.sum(mine, axis=1, keepdims=True)
    rank = jnp.concatenate(ranks, 1)
    to_z = (own // 2) % DEPTH
    to_plane = (own // (2 * DEPTH)) * 2 + own % 2
    hi = (to_z * 2 + to_plane // 4).astype(F32)
    lo = ((to_plane % 4) * CAP).astype(F32) + rank
    hot = one_hot(lo, 128)
    lot_p[...] = hot
    hi_p[...] = jnp.broadcast_to(hi, (8, 1024))
    extra = lax.broadcasted_iota(jnp.int32, (8, 1024), 0)
    extra = jnp.where(
        extra == 0, (where_to // 128).astype(F32), jnp.where(extra == 1, (where_to % 128).astype(F32), 0.0)
    )
    full = jnp.concatenate([feats[...].astype(F32), extra], 0)
    hi_wide = jnp.broadcast_to(hi, (24, 1024))
    spread = jnp.concatenate([jnp.where(hi_wide == float(h), full, 0.0).astype(BF16) for h in range(16)], 0)
    packed = dot_lanes(spread, hot)
    for h in range(16):
        send_a[h // 2, :, 128 * (h % 2) : 128 * (h % 2) + 128] = packed[24 * h : 24 * h + 24].astype(BF16)

    pl.semaphore_wait(barrier, len(peers))

    first = []
    for d in range(1, DEPTH):
        first.append(send(send_a.at[(z + d) % DEPTH], recv_a.at[d], sem_z, (d,), z_peer(d)))

    lane = lax.broadcasted_iota(jnp.int32, (1, 128), 1)
    weight_moves = []
    for n, (w, w_send, w_recv) in enumerate(((w_in, w_send_one, w_recv_one), (w_mid, w_send_two, w_recv_two))):
        width = w.shape[1]
        zero = jnp.zeros((width, 32), F32)
        for i in range(3):
            slabs = [jnp.concatenate([w[9 * i + jl].astype(F32), zero], 1) for jl in range(TAPS)]
            for k in range(CHAN):
                tiles = []
                for group in (range(0, 5), range(5, 9)):
                    tile = jnp.zeros((width, 128), F32)
                    for u, jl in enumerate(group):
                        moved = pltpu.roll(slabs[jl], (24 * u - 24 * k) % 128, 1)
                        tile = jnp.where((lane >= 24 * u) & (lane < 24 * u + 24), moved, tile)
                    tiles.append(tile)
                w_send[k, i] = jnp.concatenate(tiles, 1).astype(BF16)
        for d in range(1, CHAN):
            weight_moves.append(send(w_send.at[(q + d) % CHAN], w_recv.at[d], sem_w, (n, d), x_peer(d)))

    for copy in first:
        copy.wait_recv()
    parts = [send_a[z].astype(F32)] + [recv_a[d].astype(F32) for d in range(1, DEPTH)]
    for j, part in enumerate(swap_groups(parts)):
        send_b[j] = part.astype(BF16)
    second = []
    for d in range(1, PLANE):
        second.append(send(send_b.at[(plane + d) % PLANE], recv_b.at[d], sem_j, (d,), j_peer(d)))

    for copy in weight_moves:
        copy.wait_recv()
    for w_send, w_recv, w_full, width in (
        (w_send_one, w_recv_one, w_one, 16),
        (w_send_two, w_recv_two, w_two, 24),
    ):
        pieces = []
        for i in range(3):
            for r in range(CHAN):
                pieces.append((w_send[q, i] if r == 0 else w_recv[r, i]).astype(F32))
        depth = 12 * width
        fill = (-depth) % 128
        if fill:
            pieces.append(jnp.zeros((fill, 256), F32))
        turned = jnp.concatenate(pieces, 0).T
        w_full[...] = turned[:ROWS].astype(BF16)

    for copy in second:
        copy.wait_recv()
    slots = jnp.concatenate([send_b[plane].astype(F32)] + [recv_b[d].astype(F32) for d in range(1, PLANE)], 1)
    hi = slots[16:17]
    hot = one_hot(slots[17:18], 128)
    lot_s[...] = hot
    hi_s[...] = jnp.broadcast_to(hi, (8, VOX))
    hi_wide = jnp.broadcast_to(hi, (16, VOX))
    spread = jnp.concatenate([jnp.where(hi_wide == float(h), slots[0:16], 0.0).astype(BF16) for h in range(16)], 0)
    cells = dot_lanes(spread, hot)
    for h in range(16):
        x_one[0, :, 128 * h : 128 * h + 128] = cells[16 * h : 16 * h + 16].astype(BF16)

    def halo_index(b, f):
        n = nbr[b, f]
        local = n - BRICKS * s + BRICKS
        return local, (n >= 0) & (local >= 0) & (local < 3 * BRICKS)

    def exchange_and_conv(n, width, x_buf, face, pad, w_full):
        sides = 4 * 12
        none = 3 * sides

        def half(h):
            return slice(1024 * h, 1024 * h + 1024)

        def move(src, dst, h, at, d):
            return send(x_buf.at[src, :, half(h)], x_buf.at[dst, :, half(h)], sem_x, (n, at), x_peer(d))

        right = {h: move(0, 1, h, h, 1) for h in (0, 1)}
        left = {h: move(0, 3, h, 2 + h, -1 + CHAN) for h in (1, 0)}
        face_moves = []

        def faces(r):
            cells = [x_buf[r, :, CELLS * b : CELLS * b + CELLS].astype(F32) for b in range(BRICKS)]
            rims = dot(jnp.concatenate(cells, 0).astype(BF16), sel[...])
            for b in range(BRICKS):
                for p in range(3):
                    face[sides + 12 * r + 3 * b + p] = rims[width * b : width * b + width, 128 * p : 128 * p + 128].astype(BF16)
            src = face.at[sides + 12 * r : sides + 12 * r + 12]
            face_moves.append(send(src, face.at[12 * r : 12 * r + 12], sem_f, (n, r, 0), s_peer(1)))
            face_moves.append(
                send(src, face.at[2 * sides + 12 * r : 2 * sides + 12 * r + 12], sem_f, (n, r, 1), s_peer(-1))
            )

        face[none] = jnp.zeros((width, 128), BF16)
        faces(0)
        right[0].wait_recv()
        relay = [move(1, 2, 0, 4, 1)]
        left[1].wait_recv()
        relay.append(move(3, 2, 1, 5, -1 + CHAN))
        right[1].wait_recv()
        faces(1)
        left[0].wait_recv()
        faces(3)
        for copy in relay:
            copy.wait_recv()
        faces(2)
        tiles = [
            x_buf[r, :, 128 * t : 128 * t + 128].astype(F32) for r in range(CHAN) for t in range(16)
        ]
        inner = dot(jnp.concatenate(tiles, 0).astype(BF16), ec[...])
        for copy in face_moves:
            copy.wait_recv()
        low_half = lax.broadcasted_iota(jnp.int32, (width, 128), 1) < 64

        def rim(r, b, p):
            found = []
            for f in (2 * p, 2 * p + 1):
                local, there = halo_index(b, f)
                local = jnp.where(there, local, 0)
                at = (local // BRICKS) * sides + 12 * r + 3 * (local % BRICKS) + p
                found.append(face[jnp.where(there, at, none)].astype(F32))
            return jnp.where(low_half, found[0], found[1])

        rims = {(r, b, p): rim(r, b, p) for r in range(CHAN) for b in range(BRICKS) for p in range(3)}
        pairs = [(r, b) for r in range(CHAN) for b in range(BRICKS)]
        ends = dot(jnp.concatenate([rims[r, b, 0] for r, b in pairs], 0).astype(BF16), ec[...])
        sides_yz = jnp.concatenate(
            [
                jnp.concatenate([rims[r, b, 1] for r, b in pairs], 0),
                jnp.concatenate([rims[r, b, 2] for r, b in pairs], 0),
            ],
            1,
        )
        outer = dot(sides_yz.astype(BF16), eh[...])
        sums = []
        for b in range(BRICKS):
            at = [(r * BRICKS + b) * width for r in range(CHAN)]
            end = jnp.concatenate([ends[a : a + width] for a in at], 0).astype(BF16)
            pad[b, :, 0:128] = end[:, 0:128]
            pad[b, :, 1152:1280] = end[:, 128:256]
            for p in range(4):
                mid = jnp.concatenate(
                    [
                        inner[(r * 16 + 4 * b + p) * width : (r * 16 + 4 * b + p + 1) * width]
                        + outer[at[r] : at[r] + width, 256 * p : 256 * p + 256]
                        for r in range(CHAN)
                    ],
                    0,
                )
                pad[b, :, 128 + 256 * p : 384 + 256 * p] = mid.astype(BF16)
            deep = jnp.concatenate([pad[b, :, 128 * i : 128 * i + 1024] for i in range(3)], 0)
            full = dot(w_full[:, 0 : deep.shape[0]], deep)
            total = None
            for jl in range(TAPS):
                term = full[tap_row(jl) : tap_row(jl) + OUT]
                term = jnp.concatenate([term[:, 128 * x : 128 * x + 128] for x in range(8)], 0)
                shift = 10 * (jl // 3) + jl % 3
                if shift:
                    term = pltpu.roll(term, 128 - shift, 1)
                total = term if total is None else total + term
            sums.append(total)
        return sums

    def close(layers):
        pieces = []
        for layer in layers:
            for p in range(4):
                pieces.append(
                    jnp.concatenate(
                        [layer[OUT * (2 * p) : OUT * (2 * p) + OUT], layer[OUT * (2 * p + 1) : OUT * (2 * p + 1) + OUT]], 1
                    )
                )
        return dot(jnp.concatenate(pieces, 0).astype(BF16), cm[...])

    sums = exchange_and_conv(0, 16, x_one, face_one, pad_one, w_one)
    layers = []
    for b in range(BRICKS):
        layer = jnp.maximum(sums[b], 0.0).astype(BF16)
        keep[b] = layer
        layers.append(layer.astype(F32))
    cells = close(layers)
    for t in range(16):
        x_two[0, :, 128 * t : 128 * t + 128] = cells[OUT * t : OUT * t + OUT].astype(BF16)

    sums = exchange_and_conv(1, 24, x_two, face_two, pad_two, w_two)
    layers = [jnp.maximum(sums[b] + keep[b].astype(F32), 0.0).astype(BF16).astype(F32) for b in range(BRICKS)]
    cells = close(layers)
    for t in range(16):
        grid_out[:, 128 * t : 128 * t + 128] = cells[OUT * t : OUT * t + OUT].astype(BF16)
    cells = cells.astype(BF16)

    third = []
    for d in [*range(1, PLANE), 0]:
        at = slice(256 * d, 256 * d + 256)
        found = dot(cells, lot_s[:, at])
        hi_wide = jnp.broadcast_to(hi_s[0:1, at], (OUT, 256))
        value = found[0:OUT]
        for h in range(1, 16):
            value = jnp.where(hi_wide == float(h), found[OUT * h : OUT * h + OUT], value)
        if d == 0:
            ret_b[plane] = value.astype(BF16)
        else:
            ret_a[d] = value.astype(BF16)
            third.append(send(ret_a.at[d], ret_b.at[plane], sem_rj, (d,), j_peer(PLANE - d)))
    for copy in third:
        copy.wait_recv()
    fourth = []
    for d, part in enumerate(swap_groups([ret_b[j].astype(F32) for j in range(PLANE)])):
        if d == 0:
            ret_v[z] = part.astype(BF16)
        else:
            ret_c[d] = part.astype(BF16)
            fourth.append(send(ret_c.at[d], ret_v.at[z], sem_rz, (d,), z_peer(DEPTH - d)))
    for copy in fourth:
        copy.wait_recv()
    lines = [ret_v[h // 2, :, 128 * (h % 2) : 128 * (h % 2) + 128].astype(F32) for h in range(16)]
    found = dot(jnp.concatenate(lines, 0).astype(BF16), lot_p[...])
    hi_wide = jnp.broadcast_to(hi_p[0:1], (OUT, 1024))
    value = found[0:OUT]
    for h in range(1, 16):
        value = jnp.where(hi_wide == float(h), found[OUT * h : OUT * h + OUT], value)
    point_out[...] = value.astype(BF16)
    for copy in started:
        copy.wait_send()


def per_device(point_feats, point_owner, point_place, neighbors, weight_in, weight_mid):
    vmem = pl.BlockSpec(memory_space=pltpu.VMEM)
    smem = pl.BlockSpec(memory_space=pltpu.SMEM)
    constants = [jnp.asarray(c(), BF16) for c in (face_picker, plane_spread, rim_spread, plane_pack)]
    points = point_feats.shape[1]
    grid, values = pl.pallas_call(
        body,
        out_shape=(
            jax.ShapeDtypeStruct((OUT, VOX), BF16),
            jax.ShapeDtypeStruct((OUT, points), BF16),
        ),
        in_specs=[vmem, vmem, vmem, smem] + [vmem] * 6,
        out_specs=(vmem, vmem),
        scratch_shapes=[
            pltpu.VMEM((8, 24, 256), BF16),
            pltpu.VMEM((8, 24, 256), BF16),
            pltpu.VMEM((8, 24, 256), BF16),
            pltpu.VMEM((8, 24, 256), BF16),
            pltpu.VMEM((4, 16, VOX), BF16),
            pltpu.VMEM((4, 24, VOX), BF16),
            pltpu.VMEM((145, 16, 128), BF16),
            pltpu.VMEM((145, 24, 128), BF16),
            pltpu.VMEM((4, 3, 16, 256), BF16),
            pltpu.VMEM((4, 3, 16, 256), BF16),
            pltpu.VMEM((4, 3, 24, 256), BF16),
            pltpu.VMEM((4, 3, 24, 256), BF16),
            pltpu.VMEM((ROWS, 256), BF16),
            pltpu.VMEM((ROWS, 384), BF16),
            pltpu.VMEM((128, points), BF16),
            pltpu.VMEM((8, points), F32),
            pltpu.VMEM((128, VOX), BF16),
            pltpu.VMEM((8, VOX), F32),
            pltpu.VMEM((4, 64, 1280), BF16),
            pltpu.VMEM((4, 96, 1280), BF16),
            pltpu.VMEM((4, 192, 128), BF16),
            pltpu.VMEM((8, 24, 256), BF16),
            pltpu.VMEM((8, 24, 256), BF16),
            pltpu.VMEM((8, 24, 256), BF16),
            pltpu.VMEM((8, 24, 256), BF16),
            pltpu.SemaphoreType.DMA((2, 8)),
            pltpu.SemaphoreType.DMA((2, 8)),
            pltpu.SemaphoreType.DMA((2, 2, 6)),
            pltpu.SemaphoreType.DMA((2, 2, 4, 2)),
            pltpu.SemaphoreType.DMA((2, 2, 4)),
            pltpu.SemaphoreType.DMA((2, 8)),
            pltpu.SemaphoreType.DMA((2, 8)),
        ],
        compiler_params=pltpu.CompilerParams(collective_id=0, has_side_effects=True),
    )(
        point_feats,
        point_owner.reshape(1, points),
        point_place.reshape(1, points),
        neighbors,
        jnp.transpose(weight_in, (1, 0, 2)),
        jnp.transpose(weight_mid, (1, 0, 2)),
        *constants,
    )
    return grid.reshape(OUT, BRICKS, CELLS), values


def solution(mesh):
    return jax.shard_map(
        per_device,
        mesh=mesh,
        in_specs=(
            P("chan", "space"),
            P("space", None),
            P("space"),
            P("space", None),
            P("chan", None, None),
            P("chan", None, None),
        ),
        out_specs=(P("chan", "space", None), P("chan", "space")),
        check_vma=False,
    )
```

```python
import functools

import jax
import jax.numpy as jnp
import numpy as np
from jax import lax
from jax.experimental import pallas as pl
from jax.experimental.pallas import tpu as pltpu
from jax.sharding import PartitionSpec as P

DEPTH = 8
PLANE = 8
CHAN = 4
CAP = 32
CELLS = 512
BRICKS = 4
VOX = BRICKS * CELLS
OUT = 24
TAPS = 9
F32 = jnp.float32
BF16 = jnp.bfloat16
MESH = pl.DeviceIdType.MESH


def tap_row(jl):
    return OUT * jl + (8 if jl >= 5 else 0)


ROWS = 224


def face_picker():
    sel = np.zeros((CELLS, 384), np.float32)
    for u in range(8):
        for w in range(8):
            for p in range(3):
                for half, end in ((0, 7), (1, 0)):
                    x, y, z = ((end, u, w), (u, end, w), (u, w, end))[p]
                    sel[(8 * x + y) * 8 + z, 128 * p + 64 * half + 8 * u + w] = 1
    return sel


def plane_spread():
    ec = np.zeros((128, 256), np.float32)
    for x in range(2):
        for y in range(8):
            for z in range(8):
                ec[64 * x + 8 * y + z, 128 * x + 10 * (y + 1) + z + 1] = 1
    return ec


def rim_spread():
    eh = np.zeros((256, 1024), np.float32)
    for x in range(8):
        for w in range(8):
            eh[8 * x + w, 128 * x + w + 1] = 1
            eh[64 + 8 * x + w, 128 * x + 90 + w + 1] = 1
            eh[128 + 8 * x + w, 128 * x + 10 * (w + 1)] = 1
            eh[192 + 8 * x + w, 128 * x + 10 * (w + 1) + 9] = 1
    return eh


def plane_pack():
    cm = np.zeros((256, 128), np.float32)
    for x in range(2):
        for y in range(8):
            for z in range(8):
                cm[128 * x + 10 * y + z, 64 * x + 8 * y + z] = 1
    return cm


def dot(a, b):
    return jnp.dot(a, b, preferred_element_type=F32)


def dot_lanes(a, b):
    return lax.dot_general(a, b, (((1,), (1,)), ((), ())), preferred_element_type=F32)


def one_hot(row, count):
    ids = lax.broadcasted_iota(jnp.int32, (count, row.shape[1]), 0).astype(F32)
    return jnp.where(ids == row, 1.0, 0.0).astype(BF16)


def swap_groups(parts):
    rows = parts[0].shape[0]
    tall = jnp.concatenate([p[:, 128 * m : 128 * m + 128] for p in parts for m in range(2)], 0)
    turned = [tall] + [pltpu.roll(tall, 32 * a, 1) for a in range(1, 4)]
    group = lax.broadcasted_iota(jnp.int32, (rows, 128), 1) // 32
    result = []
    for j in range(8):
        m, g = j // 4, j % 4
        tiles = []
        for t in range(2):
            tile = None
            for u in range(4):
                at = (2 * (4 * t + u) + m) * rows
                piece = turned[(u - g) % 4][at : at + rows]
                tile = piece if tile is None else jnp.where(group == u, piece, tile)
            tiles.append(tile)
        result.append(jnp.concatenate(tiles, 1))
    return result


def body(
    feats_in, owner_in, place_in, nbr_in, w_in_in, w_mid_in, sel_in, ec_in, eh_in, cm_in,
    grid_out, point_out,
    feats, owner, place, nbr, w_in, w_mid, sel, ec, eh, cm, grid_stage, point_stage, sem_in, sem_out,
    send_a, recv_a, send_b, recv_b, x_one, x_two, face_one, face_two, w_send_one, w_recv_one, w_send_two, w_recv_two,
    w_one, w_two, lot_p, hi_p, lot_s, hi_s, pad_one, pad_two, keep, ret_a, ret_b, ret_c, ret_v,
    sem_z, sem_j, sem_x, sem_f, sem_w, sem_rj, sem_rz,
):
    s = lax.axis_index("space")
    q = lax.axis_index("chan")
    core = s % 2
    z = (s // 2) % DEPTH
    row = s // (2 * DEPTH)
    plane = row * 2 + core
    spaces = 64

    def z_peer(d):
        return {"space": (row * DEPTH + (z + d) % DEPTH) * 2 + core, "chan": q}

    def j_peer(d):
        other = (plane + d) % PLANE
        return {"space": ((other // 2) * DEPTH + z) * 2 + other % 2, "chan": q}

    def x_peer(d):
        return {"space": s, "chan": (q + d) % CHAN}

    def s_peer(d):
        return {"space": (s + d + spaces) % spaces, "chan": q}

    started = []

    def send(src, dst, sems, at, peer):
        copy = pltpu.make_async_remote_copy(
            src_ref=src, dst_ref=dst, send_sem=sems.at[(0, *at)], recv_sem=sems.at[(1, *at)], device_id=peer, device_id_type=MESH
        )
        copy.start()
        started.append(copy)
        return copy

    peers = (
        [z_peer(d) for d in range(1, DEPTH)]
        + [j_peer(d) for d in range(1, PLANE)]
        + [x_peer(d) for d in range(1, CHAN)]
        + [s_peer(1), s_peer(-1)]
    )
    barrier = pltpu.get_barrier_semaphore()
    for peer in peers:
        pl.semaphore_signal(barrier, inc=1, device_id=peer, device_id_type=MESH)

    fetches = [
        pltpu.make_async_copy(src, dst, sem_in.at[i])
        for i, (src, dst) in enumerate(
            (
                (owner_in, owner), (place_in, place), (feats_in, feats), (w_in_in, w_in), (w_mid_in, w_mid),
                (nbr_in, nbr), (sel_in, sel), (ec_in, ec), (eh_in, eh), (cm_in, cm),
            )
        )
    ]
    for copy in fetches:
        copy.start()
    for copy in fetches[:3]:
        copy.wait()

    own = owner[...]
    where_to = place[...]
    match = jnp.where(lax.broadcasted_iota(jnp.int32, (64, 1024), 0) == own, 1.0, 0.0)
    tall = jnp.concatenate([match[:, 256 * i : 256 * i + 256] for i in range(4)], 0)
    before = jnp.where(
        lax.broadcasted_iota(jnp.int32, (256, 256), 0) < lax.broadcasted_iota(jnp.int32, (256, 256), 1), 1.0, 0.0
    )
    earlier = dot(tall.astype(BF16), before.astype(BF16))
    carry = jnp.zeros((64, 1), F32)
    ranks = []
    for i in range(4):
        mine = tall[64 * i : 64 * i + 64]
        ranks.append(jnp.sum(mine * (earlier[64 * i : 64 * i + 64] + carry), axis=0, keepdims=True))
        carry = carry + jnp.sum(mine, axis=1, keepdims=True)
    rank = jnp.concatenate(ranks, 1)
    to_z = (own // 2) % DEPTH
    to_plane = (own // (2 * DEPTH)) * 2 + own % 2
    hi = (to_plane * 2 + to_z // 4).astype(F32)
    lo = ((to_z % 4) * CAP).astype(F32) + rank
    hot = one_hot(lo, 128)
    lot_p[...] = hot
    hi_p[...] = jnp.broadcast_to(hi, (8, 1024))
    extra = lax.broadcasted_iota(jnp.int32, (8, 1024), 0)
    extra = jnp.where(
        extra == 0, (where_to // 128).astype(F32), jnp.where(extra == 1, (where_to % 128).astype(F32), 0.0)
    )
    full = jnp.concatenate([feats[...].astype(F32), extra], 0)
    hi_wide = jnp.broadcast_to(hi, (24, 1024))
    spread = jnp.concatenate([jnp.where(hi_wide == float(h), full, 0.0).astype(BF16) for h in range(16)], 0)
    packed = dot_lanes(spread, hot)
    for h in range(16):
        send_a[h // 2, :, 128 * (h % 2) : 128 * (h % 2) + 128] = packed[24 * h : 24 * h + 24].astype(BF16)

    pl.semaphore_wait(barrier, len(peers))

    first = []
    for d in range(1, PLANE):
        first.append(send(send_a.at[(plane + d) % PLANE], recv_a.at[d], sem_j, (d,), j_peer(d)))
    for copy in fetches[3:]:
        copy.wait()

    lane = lax.broadcasted_iota(jnp.int32, (1, 128), 1)
    weight_moves = []
    for n, (w, w_send, w_recv) in enumerate(((w_in, w_send_one, w_recv_one), (w_mid, w_send_two, w_recv_two))):
        width = w.shape[1]
        zero = jnp.zeros((width, 32), F32)
        for i in range(3):
            slabs = [jnp.concatenate([w[9 * i + jl].astype(F32), zero], 1) for jl in range(TAPS)]
            for k in range(CHAN):
                tiles = []
                for group in (range(0, 5), range(5, 9)):
                    tile = jnp.zeros((width, 128), F32)
                    for u, jl in enumerate(group):
                        moved = pltpu.roll(slabs[jl], (24 * u - 24 * k) % 128, 1)
                        tile = jnp.where((lane >= 24 * u) & (lane < 24 * u + 24), moved, tile)
                    tiles.append(tile)
                w_send[k, i] = jnp.concatenate(tiles, 1).astype(BF16)
        for d in range(1, CHAN):
            weight_moves.append(send(w_send.at[(q + d) % CHAN], w_recv.at[d], sem_w, (n, d), x_peer(d)))

    for copy in first:
        copy.wait_recv()
    parts = [send_a[plane].astype(F32)] + [recv_a[d].astype(F32) for d in range(1, PLANE)]
    for j, part in enumerate(swap_groups(parts)):
        send_b[j] = part.astype(BF16)
    second = []
    for d in range(1, DEPTH):
        second.append(send(send_b.at[(z + d) % DEPTH], recv_b.at[d], sem_z, (d,), z_peer(d)))

    for copy in weight_moves:
        copy.wait_recv()
    for w_send, w_recv, w_full, width in (
        (w_send_one, w_recv_one, w_one, 16),
        (w_send_two, w_recv_two, w_two, 24),
    ):
        pieces = []
        for i in range(3):
            for r in range(CHAN):
                pieces.append((w_send[q, i] if r == 0 else w_recv[r, i]).astype(F32))
        depth = 12 * width
        fill = (-depth) % 128
        if fill:
            pieces.append(jnp.zeros((fill, 256), F32))
        turned = jnp.concatenate(pieces, 0).T
        w_full[...] = turned[:ROWS].astype(BF16)

    for copy in second:
        copy.wait_recv()
    slots = jnp.concatenate([send_b[z].astype(F32)] + [recv_b[d].astype(F32) for d in range(1, DEPTH)], 1)
    hi = slots[16:17]
    hot = one_hot(slots[17:18], 128)
    lot_s[...] = hot
    hi_s[...] = jnp.broadcast_to(hi, (8, VOX))
    hi_wide = jnp.broadcast_to(hi, (16, VOX))
    spread = jnp.concatenate([jnp.where(hi_wide == float(h), slots[0:16], 0.0).astype(BF16) for h in range(16)], 0)
    cells = dot_lanes(spread, hot)
    for h in range(16):
        x_one[0, :, 128 * h : 128 * h + 128] = cells[16 * h : 16 * h + 16].astype(BF16)

    def halo_index(b, f):
        n = nbr[b, f]
        local = n - BRICKS * s + BRICKS
        return local, (n >= 0) & (local >= 0) & (local < 3 * BRICKS)

    def exchange_and_conv(n, width, x_buf, face, pad, w_full):
        sides = 4 * 12
        none = 3 * sides

        def half(h):
            return slice(1024 * h, 1024 * h + 1024)

        def move(src, dst, h, at, d):
            return send(x_buf.at[src, :, half(h)], x_buf.at[dst, :, half(h)], sem_x, (n, at), x_peer(d))

        right = {h: move(0, 1, h, h, 1) for h in (0, 1)}
        left = {h: move(0, 3, h, 2 + h, -1 + CHAN) for h in (1, 0)}
        face_moves = []

        def faces(r):
            cells = [x_buf[r, :, CELLS * b : CELLS * b + CELLS].astype(F32) for b in range(BRICKS)]
            rims = dot(jnp.concatenate(cells, 0).astype(BF16), sel[...])
            for b in range(BRICKS):
                for p in range(3):
                    face[sides + 12 * r + 3 * b + p] = rims[width * b : width * b + width, 128 * p : 128 * p + 128].astype(BF16)
            src = face.at[sides + 12 * r : sides + 12 * r + 12]
            face_moves.append(send(src, face.at[12 * r : 12 * r + 12], sem_f, (n, r, 0), s_peer(1)))
            face_moves.append(
                send(src, face.at[2 * sides + 12 * r : 2 * sides + 12 * r + 12], sem_f, (n, r, 1), s_peer(-1))
            )

        face[none] = jnp.zeros((width, 128), BF16)
        faces(0)
        right[0].wait_recv()
        relay = [move(1, 2, 0, 4, 1)]
        left[1].wait_recv()
        relay.append(move(3, 2, 1, 5, -1 + CHAN))
        right[1].wait_recv()
        faces(1)
        left[0].wait_recv()
        faces(3)
        for copy in relay:
            copy.wait_recv()
        faces(2)
        tiles = [
            x_buf[r, :, 128 * t : 128 * t + 128].astype(F32) for r in range(CHAN) for t in range(16)
        ]
        inner = dot(jnp.concatenate(tiles, 0).astype(BF16), ec[...])
        for copy in face_moves:
            copy.wait_recv()
        low_half = lax.broadcasted_iota(jnp.int32, (width, 128), 1) < 64

        def rim(r, b, p):
            found = []
            for f in (2 * p, 2 * p + 1):
                local, there = halo_index(b, f)
                local = jnp.where(there, local, 0)
                at = (local // BRICKS) * sides + 12 * r + 3 * (local % BRICKS) + p
                found.append(face[jnp.where(there, at, none)].astype(F32))
            return jnp.where(low_half, found[0], found[1])

        rims = {(r, b, p): rim(r, b, p) for r in range(CHAN) for b in range(BRICKS) for p in range(3)}
        pairs = [(r, b) for r in range(CHAN) for b in range(BRICKS)]
        ends = dot(jnp.concatenate([rims[r, b, 0] for r, b in pairs], 0).astype(BF16), ec[...])
        sides_yz = jnp.concatenate(
            [
                jnp.concatenate([rims[r, b, 1] for r, b in pairs], 0),
                jnp.concatenate([rims[r, b, 2] for r, b in pairs], 0),
            ],
            1,
        )
        outer = dot(sides_yz.astype(BF16), eh[...])
        sums = []
        for b in range(BRICKS):
            at = [(r * BRICKS + b) * width for r in range(CHAN)]
            end = jnp.concatenate([ends[a : a + width] for a in at], 0).astype(BF16)
            pad[b, :, 0:128] = end[:, 0:128]
            pad[b, :, 1152:1280] = end[:, 128:256]
            for p in range(4):
                mid = jnp.concatenate(
                    [
                        inner[(r * 16 + 4 * b + p) * width : (r * 16 + 4 * b + p + 1) * width]
                        + outer[at[r] : at[r] + width, 256 * p : 256 * p + 256]
                        for r in range(CHAN)
                    ],
                    0,
                )
                pad[b, :, 128 + 256 * p : 384 + 256 * p] = mid.astype(BF16)
            deep = jnp.concatenate([pad[b, :, 128 * i : 128 * i + 1024] for i in range(3)], 0)
            full = dot(w_full[:, 0 : deep.shape[0]], deep)
            total = None
            for jl in range(TAPS):
                term = full[tap_row(jl) : tap_row(jl) + OUT]
                term = jnp.concatenate([term[:, 128 * x : 128 * x + 128] for x in range(8)], 0)
                shift = 10 * (jl // 3) + jl % 3
                if shift:
                    term = pltpu.roll(term, 128 - shift, 1)
                total = term if total is None else total + term
            sums.append(total)
        return sums

    def close(layers):
        pieces = []
        for layer in layers:
            for p in range(4):
                pieces.append(
                    jnp.concatenate(
                        [layer[OUT * (2 * p) : OUT * (2 * p) + OUT], layer[OUT * (2 * p + 1) : OUT * (2 * p + 1) + OUT]], 1
                    )
                )
        return dot(jnp.concatenate(pieces, 0).astype(BF16), cm[...])

    sums = exchange_and_conv(0, 16, x_one, face_one, pad_one, w_one)
    layers = []
    for b in range(BRICKS):
        layer = jnp.maximum(sums[b], 0.0).astype(BF16)
        keep[b] = layer
        layers.append(layer.astype(F32))
    cells = close(layers)
    for t in range(16):
        x_two[0, :, 128 * t : 128 * t + 128] = cells[OUT * t : OUT * t + OUT].astype(BF16)

    sums = exchange_and_conv(1, 24, x_two, face_two, pad_two, w_two)
    layers = [jnp.maximum(sums[b] + keep[b].astype(F32), 0.0).astype(BF16).astype(F32) for b in range(BRICKS)]
    cells = close(layers)
    closed = cells
    cells = cells.astype(BF16)

    third = []
    for d in [*range(1, DEPTH), 0]:
        at = slice(256 * d, 256 * d + 256)
        found = dot(cells, lot_s[:, at])
        hi_wide = jnp.broadcast_to(hi_s[0:1, at], (OUT, 256))
        value = found[0:OUT]
        for h in range(1, 16):
            value = jnp.where(hi_wide == float(h), found[OUT * h : OUT * h + OUT], value)
        if d == 0:
            ret_b[z] = value.astype(BF16)
        else:
            ret_a[d] = value.astype(BF16)
            third.append(send(ret_a.at[d], ret_b.at[z], sem_rz, (d,), z_peer(DEPTH - d)))
    for p in range(4):
        tiles = [closed[OUT * (4 * b + p) : OUT * (4 * b + p) + OUT] for b in range(BRICKS)]
        grid_stage[:, :, 128 * p : 128 * p + 128] = jnp.stack(tiles, 1).astype(BF16)
    grid_copy = pltpu.make_async_copy(grid_stage, grid_out, sem_out.at[0])
    grid_copy.start()
    for copy in third:
        copy.wait_recv()
    fourth = []
    for d, part in enumerate(swap_groups([ret_b[j].astype(F32) for j in range(DEPTH)])):
        if d == 0:
            ret_v[plane] = part.astype(BF16)
        else:
            ret_c[d] = part.astype(BF16)
            fourth.append(send(ret_c.at[d], ret_v.at[plane], sem_rj, (d,), j_peer(PLANE - d)))
    for copy in fourth:
        copy.wait_recv()
    lines = [ret_v[h // 2, :, 128 * (h % 2) : 128 * (h % 2) + 128].astype(F32) for h in range(16)]
    found = dot(jnp.concatenate(lines, 0).astype(BF16), lot_p[...])
    hi_wide = jnp.broadcast_to(hi_p[0:1], (OUT, 1024))
    value = found[0:OUT]
    for h in range(1, 16):
        value = jnp.where(hi_wide == float(h), found[OUT * h : OUT * h + OUT], value)
    point_stage[...] = value.astype(BF16)
    point_copy = pltpu.make_async_copy(point_stage, point_out, sem_out.at[1])
    point_copy.start()
    grid_copy.wait()
    point_copy.wait()
    for copy in started:
        copy.wait_send()


def per_device(point_feats, point_owner, point_place, neighbors, weight_in, weight_mid):
    anywhere = pl.BlockSpec(memory_space=pl.ANY)
    constants = [jnp.asarray(c(), BF16) for c in (face_picker, plane_spread, rim_spread, plane_pack)]
    points = point_feats.shape[1]
    grid, values = pl.pallas_call(
        body,
        out_shape=(
            jax.ShapeDtypeStruct((OUT, BRICKS, CELLS), BF16),
            jax.ShapeDtypeStruct((OUT, points), BF16),
        ),
        in_specs=[anywhere] * 10,
        out_specs=(anywhere, anywhere),
        scratch_shapes=[
            pltpu.VMEM((16, points), BF16),
            pltpu.VMEM((1, points), jnp.int32),
            pltpu.VMEM((1, points), jnp.int32),
            pltpu.SMEM((4, 6), jnp.int32),
            pltpu.VMEM((27, 16, 96), BF16),
            pltpu.VMEM((27, 24, 96), BF16),
            *[pltpu.VMEM(c.shape, BF16) for c in constants],
            pltpu.VMEM((OUT, BRICKS, CELLS), BF16),
            pltpu.VMEM((OUT, points), BF16),
            pltpu.SemaphoreType.DMA((10,)),
            pltpu.SemaphoreType.DMA((2,)),
            pltpu.VMEM((8, 24, 256), BF16),
            pltpu.VMEM((8, 24, 256), BF16),
            pltpu.VMEM((8, 24, 256), BF16),
            pltpu.VMEM((8, 24, 256), BF16),
            pltpu.VMEM((4, 16, VOX), BF16),
            pltpu.VMEM((4, 24, VOX), BF16),
            pltpu.VMEM((145, 16, 128), BF16),
            pltpu.VMEM((145, 24, 128), BF16),
            pltpu.VMEM((4, 3, 16, 256), BF16),
            pltpu.VMEM((4, 3, 16, 256), BF16),
            pltpu.VMEM((4, 3, 24, 256), BF16),
            pltpu.VMEM((4, 3, 24, 256), BF16),
            pltpu.VMEM((ROWS, 256), BF16),
            pltpu.VMEM((ROWS, 384), BF16),
            pltpu.VMEM((128, points), BF16),
            pltpu.VMEM((8, points), F32),
            pltpu.VMEM((128, VOX), BF16),
            pltpu.VMEM((8, VOX), F32),
            pltpu.VMEM((4, 64, 1280), BF16),
            pltpu.VMEM((4, 96, 1280), BF16),
            pltpu.VMEM((4, 192, 128), BF16),
            pltpu.VMEM((8, 24, 256), BF16),
            pltpu.VMEM((8, 24, 256), BF16),
            pltpu.VMEM((8, 24, 256), BF16),
            pltpu.VMEM((8, 24, 256), BF16),
            pltpu.SemaphoreType.DMA((2, 8)),
            pltpu.SemaphoreType.DMA((2, 8)),
            pltpu.SemaphoreType.DMA((2, 2, 6)),
            pltpu.SemaphoreType.DMA((2, 2, 4, 2)),
            pltpu.SemaphoreType.DMA((2, 2, 4)),
            pltpu.SemaphoreType.DMA((2, 8)),
            pltpu.SemaphoreType.DMA((2, 8)),
        ],
        compiler_params=pltpu.CompilerParams(collective_id=0, has_side_effects=True),
    )(
        point_feats,
        point_owner.reshape(1, points),
        point_place.reshape(1, points),
        neighbors,
        jnp.transpose(weight_in, (1, 0, 2)),
        jnp.transpose(weight_mid, (1, 0, 2)),
        *constants,
    )
    return grid, values


def solution(mesh):
    return jax.shard_map(
        per_device,
        mesh=mesh,
        in_specs=(
            P("chan", "space"),
            P("space", None),
            P("space"),
            P("space", None),
            P("chan", None, None),
            P("chan", None, None),
        ),
        out_specs=(P("chan", "space", None), P("chan", "space")),
        check_vma=False,
    )
```

```python
import functools

import jax
import jax.numpy as jnp
import numpy as np
from jax import lax
from jax.experimental import pallas as pl
from jax.experimental.pallas import tpu as pltpu
from jax.sharding import PartitionSpec as P

DEPTH = 8
PLANE = 8
CHAN = 4
CAP = 32
CELLS = 512
BRICKS = 4
VOX = BRICKS * CELLS
OUT = 24
TAPS = 9
F32 = jnp.float32
BF16 = jnp.bfloat16
MESH = pl.DeviceIdType.MESH


def tap_row(jl):
    return OUT * jl + (8 if jl >= 5 else 0)


ROWS = 224
ALL = 96
FAR_FIRST = (4, 3, 5, 2, 6, 1, 7)


def face_picker():
    sel = np.zeros((CELLS, 384), np.float32)
    for u in range(8):
        for w in range(8):
            for p in range(3):
                for half, end in ((0, 7), (1, 0)):
                    x, y, z = ((end, u, w), (u, end, w), (u, w, end))[p]
                    sel[(8 * x + y) * 8 + z, 128 * p + 64 * half + 8 * u + w] = 1
    return sel


def plane_spread():
    ec = np.zeros((128, 256), np.float32)
    for x in range(2):
        for y in range(8):
            for z in range(8):
                ec[64 * x + 8 * y + z, 128 * x + 10 * (y + 1) + z + 1] = 1
    return ec


def rim_spread():
    eh = np.zeros((256, 1024), np.float32)
    for x in range(8):
        for w in range(8):
            eh[8 * x + w, 128 * x + w + 1] = 1
            eh[64 + 8 * x + w, 128 * x + 90 + w + 1] = 1
            eh[128 + 8 * x + w, 128 * x + 10 * (w + 1)] = 1
            eh[192 + 8 * x + w, 128 * x + 10 * (w + 1) + 9] = 1
    return eh


def plane_pack():
    cm = np.zeros((256, 128), np.float32)
    for x in range(2):
        for y in range(8):
            for z in range(8):
                cm[128 * x + 10 * y + z, 64 * x + 8 * y + z] = 1
    return cm


def dot(a, b):
    return jnp.dot(a, b, preferred_element_type=F32)


def dot_lanes(a, b):
    return lax.dot_general(a, b, (((1,), (1,)), ((), ())), preferred_element_type=F32)


def one_hot(row, count):
    ids = lax.broadcasted_iota(jnp.int32, (count, row.shape[1]), 0).astype(F32)
    return jnp.where(ids == row, 1.0, 0.0).astype(BF16)


def swap_groups(parts):
    rows = parts[0].shape[0]
    tall = jnp.concatenate([p[:, 128 * m : 128 * m + 128] for p in parts for m in range(2)], 0)
    turned = [tall] + [pltpu.roll(tall, 32 * a, 1) for a in range(1, 4)]
    group = lax.broadcasted_iota(jnp.int32, (rows, 128), 1) // 32
    result = []
    for j in range(8):
        m, g = j // 4, j % 4
        tiles = []
        for t in range(2):
            tile = None
            for u in range(4):
                at = (2 * (4 * t + u) + m) * rows
                piece = turned[(u - g) % 4][at : at + rows]
                tile = piece if tile is None else jnp.where(group == u, piece, tile)
            tiles.append(tile)
        result.append(jnp.concatenate(tiles, 1))
    return result


def body(
    feats_in, owner_in, place_in, nbr_in, w_in_in, w_mid_in, sel_in, ec_in, eh_in, cm_in,
    grid_out, point_out,
    feats, owner, place, nbr, w_in, w_mid, sel, ec, eh, cm, grid_stage, point_stage, sem_in, sem_out,
    send_a, recv_a, send_b, recv_b, x_one, c_one, h_send, h_recv, x_two, face_one, face_two, w_all, w_send_two, w_recv_two,
    w_one, w_two, lot_p, hi_p, lot_s, hi_s, pad_one, pad_two, ret_a, ret_b, ret_c, ret_v,
    sem_z, sem_j, sem_x, sem_p, sem_f, sem_g, sem_w, sem_rj, sem_rz,
):
    s = lax.axis_index("space")
    q = lax.axis_index("chan")
    core = s % 2
    z = (s // 2) % DEPTH
    row = s // (2 * DEPTH)
    plane = row * 2 + core
    spaces = 64

    def z_peer(d):
        return {"space": (row * DEPTH + (z + d) % DEPTH) * 2 + core, "chan": q}

    def j_peer(d):
        other = (plane + d) % PLANE
        return {"space": ((other // 2) * DEPTH + z) * 2 + other % 2, "chan": q}

    def x_peer(d):
        return {"space": s, "chan": (q + d) % CHAN}

    def s_peer(d):
        return {"space": (s + d + spaces) % spaces, "chan": q}

    started = []

    def send(src, dst, sems, at, peer):
        copy = pltpu.make_async_remote_copy(
            src_ref=src, dst_ref=dst, send_sem=sems.at[(0, *at)], recv_sem=sems.at[(1, *at)], device_id=peer, device_id_type=MESH
        )
        copy.start()
        started.append(copy)
        return copy

    peers = (
        [z_peer(d) for d in range(1, DEPTH)]
        + [j_peer(d) for d in range(1, PLANE)]
        + [x_peer(d) for d in range(1, CHAN)]
        + [s_peer(1), s_peer(-1)]
    )
    barrier = pltpu.get_barrier_semaphore()
    for peer in peers:
        pl.semaphore_signal(barrier, inc=1, device_id=peer, device_id_type=MESH)

    fetches = [
        pltpu.make_async_copy(src, dst, sem_in.at[i])
        for i, (src, dst) in enumerate(
            (
                (owner_in, owner), (place_in, place), (feats_in, feats), (w_in_in, w_in), (w_mid_in, w_mid),
                (nbr_in, nbr), (sel_in, sel), (ec_in, ec), (eh_in, eh), (cm_in, cm),
            )
        )
    ]
    for copy in fetches:
        copy.start()
    for copy in fetches[:3]:
        copy.wait()

    own = owner[...]
    where_to = place[...]
    match = jnp.where(lax.broadcasted_iota(jnp.int32, (64, 1024), 0) == own, 1.0, 0.0)
    tall = jnp.concatenate([match[:, 256 * i : 256 * i + 256] for i in range(4)], 0)
    before = jnp.where(
        lax.broadcasted_iota(jnp.int32, (256, 256), 0) < lax.broadcasted_iota(jnp.int32, (256, 256), 1), 1.0, 0.0
    )
    earlier = dot(tall.astype(BF16), before.astype(BF16))
    carry = jnp.zeros((64, 1), F32)
    ranks = []
    for i in range(4):
        mine = tall[64 * i : 64 * i + 64]
        ranks.append(jnp.sum(mine * (earlier[64 * i : 64 * i + 64] + carry), axis=0, keepdims=True))
        carry = carry + jnp.sum(mine, axis=1, keepdims=True)
    rank = jnp.concatenate(ranks, 1)
    to_z = (own // 2) % DEPTH
    to_plane = (own // (2 * DEPTH)) * 2 + own % 2
    hi = (to_plane * 2 + to_z // 4).astype(F32)
    lo = ((to_z % 4) * CAP).astype(F32) + rank
    hot = one_hot(lo, 128)
    lot_p[...] = hot
    hi_p[...] = jnp.broadcast_to(hi, (8, 1024))
    extra = lax.broadcasted_iota(jnp.int32, (8, 1024), 0)
    extra = jnp.where(
        extra == 0, (where_to // 128).astype(F32), jnp.where(extra == 1, (where_to % 128).astype(F32), 0.0)
    )
    full = jnp.concatenate([feats[...].astype(F32), extra], 0)
    hi_wide = jnp.broadcast_to(hi, (24, 1024))
    spread = jnp.concatenate([jnp.where(hi_wide == float(h), full, 0.0).astype(BF16) for h in range(16)], 0)
    packed = dot_lanes(spread, hot)
    for h in range(16):
        send_a[h // 2, :, 128 * (h % 2) : 128 * (h % 2) + 128] = packed[24 * h : 24 * h + 24].astype(BF16)

    pl.semaphore_wait(barrier, len(peers))

    first = []
    for d in FAR_FIRST:
        first.append(send(send_a.at[(plane + d) % PLANE], recv_a.at[d], sem_j, (d,), j_peer(d)))
    for copy in fetches[3:]:
        copy.wait()

    lane = lax.broadcasted_iota(jnp.int32, (1, 128), 1)
    weight_moves = [send(w_in, w_all.at[d], sem_w, (0, d), x_peer(d)) for d in range(1, CHAN)]
    zero = jnp.zeros((24, 32), F32)
    for i in range(3):
        slabs = [jnp.concatenate([w_mid[9 * i + jl].astype(F32), zero], 1) for jl in range(TAPS)]
        for k in range(CHAN):
            tiles = []
            for group in (range(0, 5), range(5, 9)):
                tile = jnp.zeros((24, 128), F32)
                for u, jl in enumerate(group):
                    moved = pltpu.roll(slabs[jl], (24 * u - 24 * k) % 128, 1)
                    tile = jnp.where((lane >= 24 * u) & (lane < 24 * u + 24), moved, tile)
                tiles.append(tile)
            w_send_two[k, i] = jnp.concatenate(tiles, 1).astype(BF16)
    for d in range(1, CHAN):
        weight_moves.append(send(w_send_two.at[(q + d) % CHAN], w_recv_two.at[d], sem_w, (1, d), x_peer(d)))

    for copy in first:
        copy.wait_recv()
    parts = [send_a[plane].astype(F32)] + [recv_a[d].astype(F32) for d in range(1, PLANE)]
    for j, part in enumerate(swap_groups(parts)):
        send_b[j] = part.astype(BF16)
    second = []
    for d in FAR_FIRST:
        second.append(send(send_b.at[(z + d) % DEPTH], recv_b.at[d], sem_z, (d,), z_peer(d)))

    for copy in weight_moves:
        copy.wait_recv()
    zero = jnp.zeros((192, 32), F32)
    for jl in range(TAPS):
        pieces = [(w_in if r == 0 else w_all.at[r])[9 * i + jl].astype(F32) for i in range(3) for r in range(CHAN)]
        tall = jnp.concatenate([jnp.concatenate(pieces, 0), zero], 1)
        w_one[ALL * jl : ALL * jl + ALL, 0:192] = tall.T[0:ALL].astype(BF16)
    w_recv_two[0] = w_send_two[q]
    pieces = [w_recv_two[(q - k + CHAN) % CHAN, i].astype(F32) for i in range(3) for k in range(CHAN)]
    turned = jnp.concatenate(pieces + [jnp.zeros((ALL, 256), F32)], 0).T[:ROWS]
    out_id = lax.broadcasted_iota(jnp.int32, (ROWS, 384), 0) - tap_row(4)
    in_id = lax.broadcasted_iota(jnp.int32, (ROWS, 384), 1) - 3 * ALL - OUT * q
    same = (out_id == in_id) & (out_id >= 0) & (out_id < OUT)
    w_two[...] = jnp.where(same, 1.0, turned).astype(BF16)

    for copy in second:
        copy.wait_recv()
    slots = jnp.concatenate([send_b[z].astype(F32)] + [recv_b[d].astype(F32) for d in range(1, DEPTH)], 1)
    hi = slots[16:17]
    hot = one_hot(slots[17:18], 128)
    lot_s[...] = hot
    hi_s[...] = jnp.broadcast_to(hi, (8, VOX))
    hi_wide = jnp.broadcast_to(hi, (16, VOX))
    spread = jnp.concatenate([jnp.where(hi_wide == float(h), slots[0:16], 0.0).astype(BF16) for h in range(16)], 0)
    cells = dot_lanes(spread, hot)
    for h in range(16):
        x_one[h // 4, :, 128 * (h % 4) : 128 * (h % 4) + 128] = cells[16 * h : 16 * h + 16].astype(BF16)

    none = 36

    def face_index(b, f, relative):
        local = nbr[b, f] - BRICKS * s + BRICKS
        there = (nbr[b, f] >= 0) & (local >= 0) & (local < 3 * BRICKS)
        local = jnp.where(there, local, 0)
        brick = local % BRICKS
        if relative:
            brick = (q - brick + CHAN) % CHAN
        return jnp.where(there, (local // BRICKS) * 12 + 3 * brick + f // 2, none)

    def rim(face, b, p, relative):
        low, high = (face[face_index(b, f, relative)].astype(F32) for f in (2 * p, 2 * p + 1))
        return jnp.where(lax.broadcasted_iota(jnp.int32, low.shape, 1) < 64, low, high)

    def tap_sum(full, count, row_of):
        total = None
        for jl in range(TAPS):
            term = full[row_of(jl) : row_of(jl) + count]
            term = jnp.concatenate([term[:, 128 * x : 128 * x + 128] for x in range(8)], 0)
            shift = 10 * (jl // 3) + jl % 3
            if shift:
                term = pltpu.roll(term, 128 - shift, 1)
            total = term if total is None else total + term
        return total

    def pack_planes(layer, count):
        return [
            jnp.concatenate(
                [layer[count * (2 * p) : count * (2 * p + 1)], layer[count * (2 * p + 1) : count * (2 * p + 2)]], 1
            )
            for p in range(4)
        ]

    rims = dot(jnp.concatenate([x_one[b] for b in range(BRICKS)], 0), sel[...])
    for b in range(BRICKS):
        for p in range(3):
            face_one[12 + 3 * b + p] = rims[16 * b : 16 * b + 16, 128 * p : 128 * p + 128].astype(BF16)
    face_one[none] = jnp.zeros((16, 128), BF16)
    face_two[none] = jnp.zeros((ALL, 128), BF16)
    beside = [
        send(face_one.at[12:24], face_one.at[24 * e : 24 * e + 12], sem_f, (3, e), s_peer(1 - 2 * e)) for e in (0, 1)
    ]
    centers = [send(x_one.at[(q + d) % CHAN], c_one.at[d], sem_x, (0, d), x_peer(d)) for d in (2, 1, 3)]
    for copy in beside:
        copy.wait_recv()
    for b in range(BRICKS):
        for p in range(3):
            h_send[b, p] = rim(face_one, b, p, False).astype(BF16)
    halos = [send(h_send.at[(q + d) % CHAN], h_recv.at[d], sem_x, (1, d), x_peer(d)) for d in (2, 1, 3)]
    for copy in centers:
        copy.wait_recv()
    parts = [x_one[q].astype(F32)] + [c_one[r].astype(F32) for r in range(1, CHAN)]
    tiles = [part[:, 128 * p : 128 * p + 128] for part in parts for p in range(4)]
    inner = dot(jnp.concatenate(tiles, 0).astype(BF16), ec[...])
    for copy in halos:
        copy.wait_recv()
    edges = [jnp.concatenate([h_send[q, p]] + [h_recv[r, p] for r in range(1, CHAN)], 0) for p in range(3)]
    ends = dot(edges[0], ec[...]).astype(BF16)
    outer = dot(jnp.concatenate(edges[1:], 1), eh[...])
    pad_one[:, 0:128] = ends[:, 0:128]
    pad_one[:, 1152:1280] = ends[:, 128:256]
    for p in range(4):
        mid = jnp.concatenate([inner[(4 * r + p) * 16 : (4 * r + p + 1) * 16] for r in range(CHAN)], 0)
        pad_one[:, 128 + 256 * p : 384 + 256 * p] = (mid + outer[:, 256 * p : 256 * p + 256]).astype(BF16)
    deep = jnp.concatenate([pad_one[:, 128 * i : 128 * i + 1024] for i in range(3)], 0)
    layer = tap_sum(dot(w_one[:, 0:192], deep), ALL, lambda jl: ALL * jl)
    layer = jnp.maximum(layer, 0.0).astype(BF16).astype(F32)
    cells = dot(jnp.concatenate(pack_planes(layer, ALL), 0).astype(BF16), cm[...])
    for p in range(4):
        x_two[0, :, 128 * p : 128 * p + 128] = cells[ALL * p : ALL * p + ALL].astype(BF16)

    def piece(slot, t):
        return x_two.at[slot, 16 * t : 16 * t + 16]

    right, left = {}, {}
    for t in range(6):
        right[t] = send(piece(0, t), piece(1, t), sem_p, (0, t), x_peer(1))
        u = (t + 3) % 6
        left[u] = send(piece(0, u), piece(3, u), sem_p, (1, u), x_peer(3))
    face_moves = []

    def send_faces(r, at, sems, which):
        for e in (0, 1):
            src = face_two.at[12 + 3 * r : 15 + 3 * r, at]
            dst = face_two.at[24 * e + 3 * r : 24 * e + 3 * r + 3, at]
            face_moves.append(send(src, dst, sems, (*which, e), s_peer(1 - 2 * e)))

    def faces(r):
        rims = dot(x_two[r], sel[...])
        for p in range(3):
            face_two[12 + 3 * r + p] = rims[:, 128 * p : 128 * p + 128].astype(BF16)
        send_faces(r, slice(0, ALL), sem_f, (r if r < 2 else 2,))

    faces(0)
    relay = {}
    for t in range(3):
        right[t].wait_recv()
        relay[t] = send(piece(1, t), piece(2, t), sem_p, (2, t), x_peer(1))
        left[3 + t].wait_recv()
        relay[3 + t] = send(piece(3, 3 + t), piece(2, 3 + t), sem_p, (2, 3 + t), x_peer(3))
    for t in range(3, 6):
        right[t].wait_recv()
    faces(1)
    for t in range(3):
        left[t].wait_recv()
    faces(3)
    for t in range(3):
        relay[t].wait_recv()
        relay[3 + t].wait_recv()
        rows = [slice(16 * u, 16 * u + 16) for u in (t, 3 + t)]
        rims = dot(jnp.concatenate([x_two[2, at] for at in rows], 0), sel[...])
        for half, at in enumerate(rows):
            for p in range(3):
                face_two[18 + p, at] = rims[16 * half : 16 * half + 16, 128 * p : 128 * p + 128].astype(BF16)
            send_faces(2, at, sem_g, (t, half))
    bricks = [x_two[(q - b + CHAN) % CHAN] for b in range(BRICKS)]
    tiles = [brick[:, 128 * p : 128 * p + 128] for brick in bricks for p in range(4)]
    inner = dot(jnp.concatenate(tiles, 0), ec[...])
    for copy in face_moves:
        copy.wait_recv()
    edges = [
        jnp.concatenate([rim(face_two, b, p, True).astype(BF16) for b in range(BRICKS)], 0) for p in range(3)
    ]
    ends = dot(edges[0], ec[...]).astype(BF16)
    outer = dot(jnp.concatenate(edges[1:], 1), eh[...])
    layers = []
    for b in range(BRICKS):
        pad_two[b, :, 0:128] = ends[ALL * b : ALL * b + ALL, 0:128]
        pad_two[b, :, 1152:1280] = ends[ALL * b : ALL * b + ALL, 128:256]
        for p in range(4):
            mid = inner[(4 * b + p) * ALL : (4 * b + p + 1) * ALL]
            mid = mid + outer[ALL * b : ALL * b + ALL, 256 * p : 256 * p + 256]
            pad_two[b, :, 128 + 256 * p : 384 + 256 * p] = mid.astype(BF16)
        deep = jnp.concatenate([pad_two[b, :, 128 * i : 128 * i + 1024] for i in (0, 1, 2, 1)], 0)
        layer = tap_sum(dot(w_two[...], deep), OUT, tap_row)
        layers += pack_planes(jnp.maximum(layer, 0.0), OUT)
    closed = dot(jnp.concatenate(layers, 0).astype(BF16), cm[...])
    cells = closed.astype(BF16)

    third = []
    for d in [*FAR_FIRST, 0]:
        at = slice(256 * d, 256 * d + 256)
        found = dot(cells, lot_s[:, at])
        hi_wide = jnp.broadcast_to(hi_s[0:1, at], (OUT, 256))
        value = found[0:OUT]
        for h in range(1, 16):
            value = jnp.where(hi_wide == float(h), found[OUT * h : OUT * h + OUT], value)
        if d == 0:
            ret_b[z] = value.astype(BF16)
        else:
            ret_a[d] = value.astype(BF16)
            third.append(send(ret_a.at[d], ret_b.at[z], sem_rz, (d,), z_peer(DEPTH - d)))
    for p in range(4):
        tiles = [closed[OUT * (4 * b + p) : OUT * (4 * b + p) + OUT] for b in range(BRICKS)]
        grid_stage[:, :, 128 * p : 128 * p + 128] = jnp.stack(tiles, 1).astype(BF16)
    grid_copy = pltpu.make_async_copy(grid_stage, grid_out, sem_out.at[0])
    grid_copy.start()
    for copy in third:
        copy.wait_recv()
    fourth = []
    parts = swap_groups([ret_b[j].astype(F32) for j in range(DEPTH)])
    for d in [*FAR_FIRST, 0]:
        if d == 0:
            ret_v[plane] = parts[d].astype(BF16)
        else:
            ret_c[d] = parts[d].astype(BF16)
            fourth.append(send(ret_c.at[d], ret_v.at[plane], sem_rj, (d,), j_peer(PLANE - d)))
    for copy in fourth:
        copy.wait_recv()
    lines = [ret_v[h // 2, :, 128 * (h % 2) : 128 * (h % 2) + 128].astype(F32) for h in range(16)]
    found = dot(jnp.concatenate(lines, 0).astype(BF16), lot_p[...])
    hi_wide = jnp.broadcast_to(hi_p[0:1], (OUT, 1024))
    value = found[0:OUT]
    for h in range(1, 16):
        value = jnp.where(hi_wide == float(h), found[OUT * h : OUT * h + OUT], value)
    point_stage[...] = value.astype(BF16)
    point_copy = pltpu.make_async_copy(point_stage, point_out, sem_out.at[1])
    point_copy.start()
    grid_copy.wait()
    point_copy.wait()
    for copy in started:
        copy.wait_send()


def per_device(point_feats, point_owner, point_place, neighbors, weight_in, weight_mid):
    anywhere = pl.BlockSpec(memory_space=pl.ANY)
    constants = [jnp.asarray(c(), BF16) for c in (face_picker, plane_spread, rim_spread, plane_pack)]
    points = point_feats.shape[1]
    grid, values = pl.pallas_call(
        body,
        out_shape=(
            jax.ShapeDtypeStruct((OUT, BRICKS, CELLS), BF16),
            jax.ShapeDtypeStruct((OUT, points), BF16),
        ),
        in_specs=[anywhere] * 10,
        out_specs=(anywhere, anywhere),
        scratch_shapes=[
            pltpu.VMEM((16, points), BF16),
            pltpu.VMEM((1, points), jnp.int32),
            pltpu.VMEM((1, points), jnp.int32),
            pltpu.SMEM((4, 6), jnp.int32),
            pltpu.VMEM((27, 16, 96), BF16),
            pltpu.VMEM((27, 24, 96), BF16),
            *[pltpu.VMEM(c.shape, BF16) for c in constants],
            pltpu.VMEM((OUT, BRICKS, CELLS), BF16),
            pltpu.VMEM((OUT, points), BF16),
            pltpu.SemaphoreType.DMA((10,)),
            pltpu.SemaphoreType.DMA((2,)),
            pltpu.VMEM((8, 24, 256), BF16),
            pltpu.VMEM((8, 24, 256), BF16),
            pltpu.VMEM((8, 24, 256), BF16),
            pltpu.VMEM((8, 24, 256), BF16),
            pltpu.VMEM((4, 16, CELLS), BF16),
            pltpu.VMEM((4, 16, CELLS), BF16),
            pltpu.VMEM((4, 3, 16, 128), BF16),
            pltpu.VMEM((4, 3, 16, 128), BF16),
            pltpu.VMEM((4, ALL, CELLS), BF16),
            pltpu.VMEM((37, 16, 128), BF16),
            pltpu.VMEM((37, ALL, 128), BF16),
            pltpu.VMEM((4, 27, 16, 96), BF16),
            pltpu.VMEM((4, 3, 24, 256), BF16),
            pltpu.VMEM((4, 3, 24, 256), BF16),
            pltpu.VMEM((TAPS * ALL, 256), BF16),
            pltpu.VMEM((ROWS, 384), BF16),
            pltpu.VMEM((128, points), BF16),
            pltpu.VMEM((8, points), F32),
            pltpu.VMEM((128, VOX), BF16),
            pltpu.VMEM((8, VOX), F32),
            pltpu.VMEM((64, 1280), BF16),
            pltpu.VMEM((4, ALL, 1280), BF16),
            pltpu.VMEM((8, 24, 256), BF16),
            pltpu.VMEM((8, 24, 256), BF16),
            pltpu.VMEM((8, 24, 256), BF16),
            pltpu.VMEM((8, 24, 256), BF16),
            pltpu.SemaphoreType.DMA((2, 8)),
            pltpu.SemaphoreType.DMA((2, 8)),
            pltpu.SemaphoreType.DMA((2, 2, 4)),
            pltpu.SemaphoreType.DMA((2, 3, 6)),
            pltpu.SemaphoreType.DMA((2, 4, 2)),
            pltpu.SemaphoreType.DMA((2, 3, 2, 2)),
            pltpu.SemaphoreType.DMA((2, 2, 4)),
            pltpu.SemaphoreType.DMA((2, 8)),
            pltpu.SemaphoreType.DMA((2, 8)),
        ],
        compiler_params=pltpu.CompilerParams(collective_id=0, has_side_effects=True),
    )(
        point_feats,
        point_owner.reshape(1, points),
        point_place.reshape(1, points),
        neighbors,
        jnp.transpose(weight_in, (1, 0, 2)),
        jnp.transpose(weight_mid, (1, 0, 2)),
        *constants,
    )
    return grid, values


def solution(mesh):
    return jax.shard_map(
        per_device,
        mesh=mesh,
        in_specs=(
            P("chan", "space"),
            P("space", None),
            P("space"),
            P("space", None),
            P("chan", None, None),
            P("chan", None, None),
        ),
        out_specs=(P("chan", "space", None), P("chan", "space")),
        check_vma=False,
    )
```

```python
import functools

import jax
import jax.numpy as jnp
import numpy as np
from jax import lax
from jax.experimental import pallas as pl
from jax.experimental.pallas import tpu as pltpu
from jax.sharding import PartitionSpec as P

DEPTH = 8
PLANE = 8
CHAN = 4
CAP = 32
CELLS = 512
BRICKS = 4
VOX = BRICKS * CELLS
OUT = 24
TAPS = 9
F32 = jnp.float32
BF16 = jnp.bfloat16
MESH = pl.DeviceIdType.MESH


def tap_row(jl):
    return OUT * jl + (8 if jl >= 5 else 0)


ROWS = 224
ALL = 96
FAR_FIRST = (4, 3, 5, 2, 6, 1, 7)


def face_picker():
    sel = np.zeros((CELLS, 384), np.float32)
    for u in range(8):
        for w in range(8):
            for p in range(3):
                for half, end in ((0, 7), (1, 0)):
                    x, y, z = ((end, u, w), (u, end, w), (u, w, end))[p]
                    sel[(8 * x + y) * 8 + z, 128 * p + 64 * half + 8 * u + w] = 1
    return sel


def plane_spread():
    ec = np.zeros((128, 256), np.float32)
    for x in range(2):
        for y in range(8):
            for z in range(8):
                ec[64 * x + 8 * y + z, 128 * x + 10 * (y + 1) + z + 1] = 1
    return ec


def rim_spread():
    eh = np.zeros((256, 1024), np.float32)
    for x in range(8):
        for w in range(8):
            eh[8 * x + w, 128 * x + w + 1] = 1
            eh[64 + 8 * x + w, 128 * x + 90 + w + 1] = 1
            eh[128 + 8 * x + w, 128 * x + 10 * (w + 1)] = 1
            eh[192 + 8 * x + w, 128 * x + 10 * (w + 1) + 9] = 1
    return eh


def plane_pack():
    cm = np.zeros((256, 128), np.float32)
    for x in range(2):
        for y in range(8):
            for z in range(8):
                cm[128 * x + 10 * y + z, 64 * x + 8 * y + z] = 1
    return cm


def dot(a, b):
    return jnp.dot(a, b, preferred_element_type=F32)


def dot_lanes(a, b):
    return lax.dot_general(a, b, (((1,), (1,)), ((), ())), preferred_element_type=F32)


def one_hot(row, count):
    ids = lax.broadcasted_iota(jnp.int32, (count, row.shape[1]), 0).astype(F32)
    return jnp.where(ids == row, 1.0, 0.0).astype(BF16)


def swap_groups(parts):
    rows = parts[0].shape[0]
    tall = jnp.concatenate([p[:, 128 * m : 128 * m + 128] for p in parts for m in range(2)], 0)
    turned = [tall] + [pltpu.roll(tall, 32 * a, 1) for a in range(1, 4)]
    group = lax.broadcasted_iota(jnp.int32, (rows, 128), 1) // 32
    result = []
    for j in range(8):
        m, g = j // 4, j % 4
        tiles = []
        for t in range(2):
            tile = None
            for u in range(4):
                at = (2 * (4 * t + u) + m) * rows
                piece = turned[(u - g) % 4][at : at + rows]
                tile = piece if tile is None else jnp.where(group == u, piece, tile)
            tiles.append(tile)
        result.append(jnp.concatenate(tiles, 1))
    return result


def body(
    feats_in, owner_in, place_in, nbr_in, w_in_in, w_mid_in, sel_in, ec_in, eh_in, cm_in,
    grid_out, point_out,
    feats, owner, place, nbr, w_in, w_mid, sel, ec, eh, cm, sem_in, index,
    send_a, recv_a, send_b, recv_b, x_one, c_one, h_send, h_recv, x_two, face_one, face_two, w_all, w_send_two, w_recv_two,
    w_one, w_two, lot_p, hi_p, lot_s, hi_s, pad_one, pad_two, ret_a, ret_b, ret_c, ret_v,
    sem_z, sem_j, sem_x, sem_p, sem_f, sem_g, sem_w, sem_rj, sem_rz,
):
    s = lax.axis_index("space")
    q = lax.axis_index("chan")
    core = s % 2
    z = (s // 2) % DEPTH
    row = s // (2 * DEPTH)
    plane = row * 2 + core
    spaces = 64

    def z_peer(d):
        return {"space": (row * DEPTH + (z + d) % DEPTH) * 2 + core, "chan": q}

    def j_peer(d):
        other = (plane + d) % PLANE
        return {"space": ((other // 2) * DEPTH + z) * 2 + other % 2, "chan": q}

    def x_peer(d):
        return {"space": s, "chan": (q + d) % CHAN}

    def s_peer(d):
        return {"space": (s + d + spaces) % spaces, "chan": q}

    started = []

    def send(src, dst, sems, at, peer):
        copy = pltpu.make_async_remote_copy(
            src_ref=src, dst_ref=dst, send_sem=sems.at[(0, *at)], recv_sem=sems.at[(1, *at)], device_id=peer, device_id_type=MESH
        )
        copy.start()
        started.append(copy)
        return copy

    fetches = [
        pltpu.make_async_copy(src, dst, sem_in.at[i])
        for i, (src, dst) in enumerate(
            (
                (owner_in, owner), (place_in, place), (feats_in, feats), (w_in_in, w_in), (w_mid_in, w_mid),
                (nbr_in, nbr), (sel_in, sel), (ec_in, ec), (eh_in, eh), (cm_in, cm),
            )
        )
    ]
    for copy in fetches:
        copy.start()
    peers = (
        [z_peer(d) for d in range(1, DEPTH)]
        + [j_peer(d) for d in range(1, PLANE)]
        + [x_peer(d) for d in range(1, CHAN)]
        + [s_peer(1), s_peer(-1)]
    )
    barrier = pltpu.get_barrier_semaphore()
    for peer in peers:
        pl.semaphore_signal(barrier, inc=1, device_id=peer, device_id_type=MESH)

    for copy in fetches[:3]:
        copy.wait()

    own = owner[...]
    where_to = place[...]
    match = jnp.where(lax.broadcasted_iota(jnp.int32, (64, 1024), 0) == own, 1.0, 0.0)
    tall = jnp.concatenate([match[:, 256 * i : 256 * i + 256] for i in range(4)], 0)
    before = jnp.where(
        lax.broadcasted_iota(jnp.int32, (256, 256), 0) < lax.broadcasted_iota(jnp.int32, (256, 256), 1), 1.0, 0.0
    )
    earlier = dot(tall.astype(BF16), before.astype(BF16))
    carry = jnp.zeros((64, 1), F32)
    ranks = []
    for i in range(4):
        mine = tall[64 * i : 64 * i + 64]
        ranks.append(jnp.sum(mine * (earlier[64 * i : 64 * i + 64] + carry), axis=0, keepdims=True))
        carry = carry + jnp.sum(mine, axis=1, keepdims=True)
    rank = jnp.concatenate(ranks, 1)
    to_z = (own // 2) % DEPTH
    to_plane = (own // (2 * DEPTH)) * 2 + own % 2
    hi = (to_plane * 2 + to_z // 4).astype(F32)
    lo = ((to_z % 4) * CAP).astype(F32) + rank
    hot = one_hot(lo, 128)
    lot_p[...] = hot
    hi_p[...] = jnp.broadcast_to(hi, (8, 1024))
    extra = lax.broadcasted_iota(jnp.int32, (8, 1024), 0)
    extra = jnp.where(
        extra == 0, (where_to // 128).astype(F32), jnp.where(extra == 1, (where_to % 128).astype(F32), 0.0)
    )
    full = jnp.concatenate([feats[...].astype(F32), extra], 0)
    hi_wide = jnp.broadcast_to(hi, (24, 1024))
    spread = jnp.concatenate([jnp.where(hi_wide == float(h), full, 0.0).astype(BF16) for h in range(16)], 0)
    packed = dot_lanes(spread, hot)
    for h in range(16):
        send_a[h // 2, :, 128 * (h % 2) : 128 * (h % 2) + 128] = packed[24 * h : 24 * h + 24].astype(BF16)

    pl.semaphore_wait(barrier, len(peers))

    first = []
    for d in FAR_FIRST:
        first.append(send(send_a.at[(plane + d) % PLANE], recv_a.at[d], sem_j, (d,), j_peer(d)))
    for copy in fetches[3:]:
        copy.wait()

    lane = lax.broadcasted_iota(jnp.int32, (1, 128), 1)
    weight_moves = [send(w_in, w_all.at[d], sem_w, (0, d), x_peer(d)) for d in range(1, CHAN)]
    zero = jnp.zeros((24, 32), F32)
    for i in range(3):
        slabs = [jnp.concatenate([w_mid[9 * i + jl].astype(F32), zero], 1) for jl in range(TAPS)]
        for k in range(CHAN):
            tiles = []
            for group in (range(0, 5), range(5, 9)):
                tile = jnp.zeros((24, 128), F32)
                for u, jl in enumerate(group):
                    moved = pltpu.roll(slabs[jl], (24 * u - 24 * k) % 128, 1)
                    tile = jnp.where((lane >= 24 * u) & (lane < 24 * u + 24), moved, tile)
                tiles.append(tile)
            w_send_two[k, i] = jnp.concatenate(tiles, 1).astype(BF16)
    for d in range(1, CHAN):
        weight_moves.append(send(w_send_two.at[(q + d) % CHAN], w_recv_two.at[d], sem_w, (1, d), x_peer(d)))

    for copy in first:
        copy.wait_recv()
    parts = [send_a[plane].astype(F32)] + [recv_a[d].astype(F32) for d in range(1, PLANE)]
    for j, part in enumerate(swap_groups(parts)):
        send_b[j] = part.astype(BF16)
    second = []
    for d in FAR_FIRST:
        second.append(send(send_b.at[(z + d) % DEPTH], recv_b.at[d], sem_z, (d,), z_peer(d)))

    for copy in weight_moves:
        copy.wait_recv()
    zero = jnp.zeros((192, 32), F32)
    for jl in range(TAPS):
        pieces = [(w_in if r == 0 else w_all.at[r])[9 * i + jl].astype(F32) for i in range(3) for r in range(CHAN)]
        tall = jnp.concatenate([jnp.concatenate(pieces, 0), zero], 1)
        w_one[ALL * jl : ALL * jl + ALL, 0:192] = tall.T[0:ALL].astype(BF16)
    w_recv_two[0] = w_send_two[q]
    pieces = [w_recv_two[(q - k + CHAN) % CHAN, i].astype(F32) for i in range(3) for k in range(CHAN)]
    turned = jnp.concatenate(pieces + [jnp.zeros((ALL, 256), F32)], 0).T[:ROWS]
    out_id = lax.broadcasted_iota(jnp.int32, (ROWS, 384), 0) - tap_row(4)
    in_id = lax.broadcasted_iota(jnp.int32, (ROWS, 384), 1) - 3 * ALL - OUT * q
    same = (out_id == in_id) & (out_id >= 0) & (out_id < OUT)
    w_two[...] = jnp.where(same, 1.0, turned).astype(BF16)

    none = 36
    for b in range(BRICKS):
        for f in range(6):
            local = nbr[b, f] - BRICKS * s + BRICKS
            there = (nbr[b, f] >= 0) & (local >= 0) & (local < 3 * BRICKS)
            base = (local >> 2) * 12 + f // 2
            index[0, 6 * b + f] = jnp.where(there, base + 3 * (local & 3), none)
            index[1, 6 * b + f] = jnp.where(there, base + 3 * ((q - local) & 3), none)

    for copy in second:
        copy.wait_recv()
    slots = jnp.concatenate([send_b[z].astype(F32)] + [recv_b[d].astype(F32) for d in range(1, DEPTH)], 1)
    hi = slots[16:17]
    hot = one_hot(slots[17:18], 128)
    lot_s[...] = hot
    hi_s[...] = jnp.broadcast_to(hi, (8, VOX))
    hi_wide = jnp.broadcast_to(hi, (16, VOX))
    spread = jnp.concatenate([jnp.where(hi_wide == float(h), slots[0:16], 0.0).astype(BF16) for h in range(16)], 0)
    cells = dot_lanes(spread, hot)
    for h in range(16):
        x_one[h // 4, :, 128 * (h % 4) : 128 * (h % 4) + 128] = cells[16 * h : 16 * h + 16].astype(BF16)

    def rim(face, b, p, relative):
        low, high = (face[index[relative, 6 * b + f]].astype(F32) for f in (2 * p, 2 * p + 1))
        return jnp.where(lax.broadcasted_iota(jnp.int32, low.shape, 1) < 64, low, high)

    def tap_sum(full, count, row_of):
        total = None
        for jl in range(TAPS):
            term = full[row_of(jl) : row_of(jl) + count]
            term = jnp.concatenate([term[:, 128 * x : 128 * x + 128] for x in range(8)], 0)
            shift = 10 * (jl // 3) + jl % 3
            if shift:
                term = pltpu.roll(term, 128 - shift, 1)
            total = term if total is None else total + term
        return total

    def pack_planes(layer, count):
        return [
            jnp.concatenate(
                [layer[count * (2 * p) : count * (2 * p + 1)], layer[count * (2 * p + 1) : count * (2 * p + 2)]], 1
            )
            for p in range(4)
        ]

    rims = dot(jnp.concatenate([x_one[b] for b in range(BRICKS)], 0), sel[...])
    for b in range(BRICKS):
        for p in range(3):
            face_one[12 + 3 * b + p] = rims[16 * b : 16 * b + 16, 128 * p : 128 * p + 128].astype(BF16)
    face_one[none] = jnp.zeros((16, 128), BF16)
    face_two[none] = jnp.zeros((ALL, 128), BF16)
    beside = [
        send(face_one.at[12:24], face_one.at[24 * e : 24 * e + 12], sem_f, (3, e), s_peer(1 - 2 * e)) for e in (0, 1)
    ]
    centers = [send(x_one.at[(q + d) % CHAN], c_one.at[d], sem_x, (0, d), x_peer(d)) for d in (2, 1, 3)]
    for copy in beside:
        copy.wait_recv()
    for b in range(BRICKS):
        for p in range(3):
            h_send[b, p] = rim(face_one, b, p, 0).astype(BF16)
    halos = [send(h_send.at[(q + d) % CHAN], h_recv.at[d], sem_x, (1, d), x_peer(d)) for d in (2, 1, 3)]
    for copy in centers:
        copy.wait_recv()
    parts = [x_one[q].astype(F32)] + [c_one[r].astype(F32) for r in range(1, CHAN)]
    tiles = [part[:, 128 * p : 128 * p + 128] for part in parts for p in range(4)]
    inner = dot(jnp.concatenate(tiles, 0).astype(BF16), ec[...])
    for copy in halos:
        copy.wait_recv()
    edges = [jnp.concatenate([h_send[q, p]] + [h_recv[r, p] for r in range(1, CHAN)], 0) for p in range(3)]
    ends = dot(edges[0], ec[...]).astype(BF16)
    outer = dot(jnp.concatenate(edges[1:], 1), eh[...])
    pad_one[:, 0:128] = ends[:, 0:128]
    pad_one[:, 1152:1280] = ends[:, 128:256]
    for p in range(4):
        mid = jnp.concatenate([inner[(4 * r + p) * 16 : (4 * r + p + 1) * 16] for r in range(CHAN)], 0)
        pad_one[:, 128 + 256 * p : 384 + 256 * p] = (mid + outer[:, 256 * p : 256 * p + 256]).astype(BF16)
    deep = jnp.concatenate([pad_one[:, 128 * i : 128 * i + 1024] for i in range(3)], 0)
    layer = tap_sum(dot(w_one[:, 0:192], deep), ALL, lambda jl: ALL * jl)
    layer = jnp.maximum(layer, 0.0).astype(BF16).astype(F32)
    cells = dot(jnp.concatenate(pack_planes(layer, ALL), 0).astype(BF16), cm[...])
    for p in range(4):
        x_two[0, :, 128 * p : 128 * p + 128] = cells[ALL * p : ALL * p + ALL].astype(BF16)

    def piece(slot, t):
        return x_two.at[slot, 16 * t : 16 * t + 16]

    right, left = {}, {}
    for t in range(6):
        right[t] = send(piece(0, t), piece(1, t), sem_p, (0, t), x_peer(1))
        u = (t + 3) % 6
        left[u] = send(piece(0, u), piece(3, u), sem_p, (1, u), x_peer(3))
    face_moves = []

    def send_faces(r, at, sems, which):
        for e in (0, 1):
            src = face_two.at[12 + 3 * r : 15 + 3 * r, at]
            dst = face_two.at[24 * e + 3 * r : 24 * e + 3 * r + 3, at]
            face_moves.append(send(src, dst, sems, (*which, e), s_peer(1 - 2 * e)))

    def faces(r):
        rims = dot(x_two[r], sel[...])
        for p in range(3):
            face_two[12 + 3 * r + p] = rims[:, 128 * p : 128 * p + 128].astype(BF16)
        send_faces(r, slice(0, ALL), sem_f, (r if r < 2 else 2,))

    faces(0)
    relay = {}
    for t in range(3):
        right[t].wait_recv()
        relay[t] = send(piece(1, t), piece(2, t), sem_p, (2, t), x_peer(1))
        left[3 + t].wait_recv()
        relay[3 + t] = send(piece(3, 3 + t), piece(2, 3 + t), sem_p, (2, 3 + t), x_peer(3))
    for t in range(3, 6):
        right[t].wait_recv()
    faces(1)
    for t in range(3):
        left[t].wait_recv()
    faces(3)
    for t in range(3):
        relay[t].wait_recv()
        relay[3 + t].wait_recv()
        rows = [slice(16 * u, 16 * u + 16) for u in (t, 3 + t)]
        rims = dot(jnp.concatenate([x_two[2, at] for at in rows], 0), sel[...])
        for half, at in enumerate(rows):
            for p in range(3):
                face_two[18 + p, at] = rims[16 * half : 16 * half + 16, 128 * p : 128 * p + 128].astype(BF16)
            send_faces(2, at, sem_g, (t, half))
    bricks = [x_two[(q - b + CHAN) % CHAN] for b in range(BRICKS)]
    tiles = [brick[:, 128 * p : 128 * p + 128] for brick in bricks for p in range(4)]
    inner = dot(jnp.concatenate(tiles, 0), ec[...])
    for copy in face_moves:
        copy.wait_recv()
    edges = [
        jnp.concatenate([rim(face_two, b, p, 1).astype(BF16) for b in range(BRICKS)], 0) for p in range(3)
    ]
    ends = dot(edges[0], ec[...]).astype(BF16)
    outer = dot(jnp.concatenate(edges[1:], 1), eh[...])
    layers = []
    for b in range(BRICKS):
        pad_two[b, :, 0:128] = ends[ALL * b : ALL * b + ALL, 0:128]
        pad_two[b, :, 1152:1280] = ends[ALL * b : ALL * b + ALL, 128:256]
        for p in range(4):
            mid = inner[(4 * b + p) * ALL : (4 * b + p + 1) * ALL]
            mid = mid + outer[ALL * b : ALL * b + ALL, 256 * p : 256 * p + 256]
            pad_two[b, :, 128 + 256 * p : 384 + 256 * p] = mid.astype(BF16)
        deep = jnp.concatenate([pad_two[b, :, 128 * i : 128 * i + 1024] for i in (0, 1, 2, 1)], 0)
        layer = tap_sum(dot(w_two[...], deep), OUT, tap_row)
        layers += pack_planes(jnp.maximum(layer, 0.0), OUT)
    closed = dot(jnp.concatenate(layers, 0).astype(BF16), cm[...])
    cells = closed.astype(BF16)

    third = []
    for d in [*FAR_FIRST, 0]:
        at = slice(256 * d, 256 * d + 256)
        found = dot(cells, lot_s[:, at])
        hi_wide = jnp.broadcast_to(hi_s[0:1, at], (OUT, 256))
        value = found[0:OUT]
        for h in range(1, 16):
            value = jnp.where(hi_wide == float(h), found[OUT * h : OUT * h + OUT], value)
        if d == 0:
            ret_b[z] = value.astype(BF16)
        else:
            ret_a[d] = value.astype(BF16)
            third.append(send(ret_a.at[d], ret_b.at[z], sem_rz, (d,), z_peer(DEPTH - d)))
    for p in range(4):
        tiles = [closed[OUT * (4 * b + p) : OUT * (4 * b + p) + OUT] for b in range(BRICKS)]
        grid_out[:, :, 128 * p : 128 * p + 128] = jnp.stack(tiles, 1).astype(BF16)
    for copy in third:
        copy.wait_recv()
    fourth = []
    parts = swap_groups([ret_b[j].astype(F32) for j in range(DEPTH)])
    for d in [*FAR_FIRST, 0]:
        if d == 0:
            ret_v[plane] = parts[d].astype(BF16)
        else:
            ret_c[d] = parts[d].astype(BF16)
            fourth.append(send(ret_c.at[d], ret_v.at[plane], sem_rj, (d,), j_peer(PLANE - d)))
    for copy in fourth:
        copy.wait_recv()
    lines = [ret_v[h // 2, :, 128 * (h % 2) : 128 * (h % 2) + 128].astype(F32) for h in range(16)]
    found = dot(jnp.concatenate(lines, 0).astype(BF16), lot_p[...])
    hi_wide = jnp.broadcast_to(hi_p[0:1], (OUT, 1024))
    value = found[0:OUT]
    for h in range(1, 16):
        value = jnp.where(hi_wide == float(h), found[OUT * h : OUT * h + OUT], value)
    point_out[...] = value.astype(BF16)
    for copy in started:
        copy.wait_send()


def per_device(point_feats, point_owner, point_place, neighbors, weight_in, weight_mid):
    anywhere = pl.BlockSpec(memory_space=pl.ANY)
    constants = [jnp.asarray(c(), BF16) for c in (face_picker, plane_spread, rim_spread, plane_pack)]
    points = point_feats.shape[1]
    grid, values = pl.pallas_call(
        body,
        out_shape=(
            pltpu.VMEM((OUT, BRICKS, CELLS), BF16),
            pltpu.VMEM((OUT, points), BF16),
        ),
        in_specs=[anywhere] * 10,
        out_specs=(pl.BlockSpec(memory_space=pltpu.VMEM), pl.BlockSpec(memory_space=pltpu.VMEM)),
        scratch_shapes=[
            pltpu.VMEM((16, points), BF16),
            pltpu.VMEM((1, points), jnp.int32),
            pltpu.VMEM((1, points), jnp.int32),
            pltpu.SMEM((4, 6), jnp.int32),
            pltpu.VMEM((27, 16, 96), BF16),
            pltpu.VMEM((27, 24, 96), BF16),
            *[pltpu.VMEM(c.shape, BF16) for c in constants],
            pltpu.SemaphoreType.DMA((10,)),
            pltpu.SMEM((2, 24), jnp.int32),
            pltpu.VMEM((8, 24, 256), BF16),
            pltpu.VMEM((8, 24, 256), BF16),
            pltpu.VMEM((8, 24, 256), BF16),
            pltpu.VMEM((8, 24, 256), BF16),
            pltpu.VMEM((4, 16, CELLS), BF16),
            pltpu.VMEM((4, 16, CELLS), BF16),
            pltpu.VMEM((4, 3, 16, 128), BF16),
            pltpu.VMEM((4, 3, 16, 128), BF16),
            pltpu.VMEM((4, ALL, CELLS), BF16),
            pltpu.VMEM((37, 16, 128), BF16),
            pltpu.VMEM((37, ALL, 128), BF16),
            pltpu.VMEM((4, 27, 16, 96), BF16),
            pltpu.VMEM((4, 3, 24, 256), BF16),
            pltpu.VMEM((4, 3, 24, 256), BF16),
            pltpu.VMEM((TAPS * ALL, 256), BF16),
            pltpu.VMEM((ROWS, 384), BF16),
            pltpu.VMEM((128, points), BF16),
            pltpu.VMEM((8, points), F32),
            pltpu.VMEM((128, VOX), BF16),
            pltpu.VMEM((8, VOX), F32),
            pltpu.VMEM((64, 1280), BF16),
            pltpu.VMEM((4, ALL, 1280), BF16),
            pltpu.VMEM((8, 24, 256), BF16),
            pltpu.VMEM((8, 24, 256), BF16),
            pltpu.VMEM((8, 24, 256), BF16),
            pltpu.VMEM((8, 24, 256), BF16),
            pltpu.SemaphoreType.DMA((2, 8)),
            pltpu.SemaphoreType.DMA((2, 8)),
            pltpu.SemaphoreType.DMA((2, 2, 4)),
            pltpu.SemaphoreType.DMA((2, 3, 6)),
            pltpu.SemaphoreType.DMA((2, 4, 2)),
            pltpu.SemaphoreType.DMA((2, 3, 2, 2)),
            pltpu.SemaphoreType.DMA((2, 2, 4)),
            pltpu.SemaphoreType.DMA((2, 8)),
            pltpu.SemaphoreType.DMA((2, 8)),
        ],
        compiler_params=pltpu.CompilerParams(collective_id=0, has_side_effects=True),
    )(
        point_feats,
        point_owner.reshape(1, points),
        point_place.reshape(1, points),
        neighbors,
        jnp.transpose(weight_in, (1, 0, 2)),
        jnp.transpose(weight_mid, (1, 0, 2)),
        *constants,
    )
    return grid, values


def solution(mesh):
    return jax.shard_map(
        per_device,
        mesh=mesh,
        in_specs=(
            P("chan", "space"),
            P("space", None),
            P("space"),
            P("space", None),
            P("chan", None, None),
            P("chan", None, None),
        ),
        out_specs=(P("chan", "space", None), P("chan", "space")),
        check_vma=False,
    )
```

```python
import functools

import jax
import jax.numpy as jnp
import numpy as np
from jax import lax
from jax.experimental import pallas as pl
from jax.experimental.pallas import tpu as pltpu
from jax.sharding import PartitionSpec as P

DEPTH = 8
PLANE = 8
CHAN = 4
CAP = 32
CELLS = 512
BRICKS = 4
VOX = BRICKS * CELLS
OUT = 24
TAPS = 9
F32 = jnp.float32
BF16 = jnp.bfloat16
MESH = pl.DeviceIdType.MESH


def tap_row(jl):
    return OUT * jl + (8 if jl >= 5 else 0)


ROWS = 224
ALL = 96
FAR_FIRST = (4, 3, 5, 2, 6, 1, 7)


def face_picker():
    sel = np.zeros((CELLS, 384), np.float32)
    for u in range(8):
        for w in range(8):
            for p in range(3):
                for half, end in ((0, 7), (1, 0)):
                    x, y, z = ((end, u, w), (u, end, w), (u, w, end))[p]
                    sel[(8 * x + y) * 8 + z, 128 * p + 64 * half + 8 * u + w] = 1
    return sel


def plane_spread():
    ec = np.zeros((128, 256), np.float32)
    for x in range(2):
        for y in range(8):
            for z in range(8):
                ec[64 * x + 8 * y + z, 128 * x + 10 * (y + 1) + z + 1] = 1
    return ec


def rim_spread():
    eh = np.zeros((256, 1024), np.float32)
    for x in range(8):
        for w in range(8):
            eh[8 * x + w, 128 * x + w + 1] = 1
            eh[64 + 8 * x + w, 128 * x + 90 + w + 1] = 1
            eh[128 + 8 * x + w, 128 * x + 10 * (w + 1)] = 1
            eh[192 + 8 * x + w, 128 * x + 10 * (w + 1) + 9] = 1
    return eh


def plane_pack():
    cm = np.zeros((256, 128), np.float32)
    for x in range(2):
        for y in range(8):
            for z in range(8):
                cm[128 * x + 10 * y + z, 64 * x + 8 * y + z] = 1
    return cm


def dot(a, b):
    return jnp.dot(a, b, preferred_element_type=F32)


def dot_lanes(a, b):
    return lax.dot_general(a, b, (((1,), (1,)), ((), ())), preferred_element_type=F32)


def one_hot(row, count):
    ids = lax.broadcasted_iota(jnp.int32, (count, row.shape[1]), 0).astype(F32)
    return jnp.where(ids == row, 1.0, 0.0).astype(BF16)


def swap_groups(parts):
    rows = parts[0].shape[0]
    tall = jnp.concatenate([p[:, 128 * m : 128 * m + 128] for p in parts for m in range(2)], 0)
    turned = [tall] + [pltpu.roll(tall, 32 * a, 1) for a in range(1, 4)]
    group = lax.broadcasted_iota(jnp.int32, (rows, 128), 1) // 32
    result = []
    for j in range(8):
        m, g = j // 4, j % 4
        tiles = []
        for t in range(2):
            tile = None
            for u in range(4):
                at = (2 * (4 * t + u) + m) * rows
                piece = turned[(u - g) % 4][at : at + rows]
                tile = piece if tile is None else jnp.where(group == u, piece, tile)
            tiles.append(tile)
        result.append(jnp.concatenate(tiles, 1))
    return result


def body(
    feats_in, owner_in, place_in, nbr_in, w_in_in, w_mid_in, sel_in, ec_in, eh_in, cm_in,
    grid_out, point_out,
    feats, owner, place, nbr, w_in, w_mid, sel, ec, eh, cm, sem_in, index,
    send_a, recv_a, send_b, recv_b, x_one, c_one, h_send, h_recv, x_two, face_one, face_two, w_all, w_send_two, w_recv_two,
    w_one, w_two, lot_p, hi_p, lot_s, hi_s, pad_one, pad_two, ret_a, ret_v,
    sem_z, sem_j, sem_x, sem_p, sem_f, sem_g, sem_w, sem_ret,
):
    s = lax.axis_index("space")
    q = lax.axis_index("chan")
    core = s % 2
    z = (s // 2) % DEPTH
    row = s // (2 * DEPTH)
    plane = row * 2 + core
    spaces = 64

    def z_peer(d):
        return {"space": (row * DEPTH + (z + d) % DEPTH) * 2 + core, "chan": q}

    def j_peer(d):
        other = (plane + d) % PLANE
        return {"space": ((other // 2) * DEPTH + z) * 2 + other % 2, "chan": q}

    def x_peer(d):
        return {"space": s, "chan": (q + d) % CHAN}

    def s_peer(d):
        return {"space": (s + d + spaces) % spaces, "chan": q}

    started = []

    def send(src, dst, sems, at, peer):
        copy = pltpu.make_async_remote_copy(
            src_ref=src, dst_ref=dst, send_sem=sems.at[(0, *at)], recv_sem=sems.at[(1, *at)], device_id=peer, device_id_type=MESH
        )
        copy.start()
        started.append(copy)
        return copy

    fetches = [
        pltpu.make_async_copy(src, dst, sem_in.at[i])
        for i, (src, dst) in enumerate(
            (
                (owner_in, owner), (place_in, place), (feats_in, feats), (w_in_in, w_in), (w_mid_in, w_mid),
                (nbr_in, nbr), (sel_in, sel), (ec_in, ec), (eh_in, eh), (cm_in, cm),
            )
        )
    ]
    for copy in fetches:
        copy.start()
    peers = (
        [z_peer(d) for d in range(1, DEPTH)]
        + [j_peer(d) for d in range(1, PLANE)]
        + [x_peer(d) for d in range(1, CHAN)]
        + [s_peer(1), s_peer(-1)]
    )
    barrier = pltpu.get_barrier_semaphore()
    for peer in peers:
        pl.semaphore_signal(barrier, inc=1, device_id=peer, device_id_type=MESH)

    for copy in fetches[:3]:
        copy.wait()

    own = owner[...]
    where_to = place[...]
    match = jnp.where(lax.broadcasted_iota(jnp.int32, (64, 1024), 0) == own, 1.0, 0.0)
    tall = jnp.concatenate([match[:, 256 * i : 256 * i + 256] for i in range(4)], 0)
    before = jnp.where(
        lax.broadcasted_iota(jnp.int32, (256, 256), 0) < lax.broadcasted_iota(jnp.int32, (256, 256), 1), 1.0, 0.0
    )
    earlier = dot(tall.astype(BF16), before.astype(BF16))
    carry = jnp.zeros((64, 1), F32)
    ranks = []
    for i in range(4):
        mine = tall[64 * i : 64 * i + 64]
        ranks.append(jnp.sum(mine * (earlier[64 * i : 64 * i + 64] + carry), axis=0, keepdims=True))
        carry = carry + jnp.sum(mine, axis=1, keepdims=True)
    rank = jnp.concatenate(ranks, 1)
    to_z = (own // 2) % DEPTH
    to_plane = (own // (2 * DEPTH)) * 2 + own % 2
    hi = (to_plane * 2 + to_z // 4).astype(F32)
    lo = ((to_z % 4) * CAP).astype(F32) + rank
    hot = one_hot(lo, 128)
    lot_p[...] = hot
    hi_p[...] = jnp.broadcast_to(hi, (8, 1024))
    extra = lax.broadcasted_iota(jnp.int32, (8, 1024), 0)
    extra = jnp.where(
        extra == 0, (where_to // 128).astype(F32), jnp.where(extra == 1, (where_to % 128).astype(F32), 0.0)
    )
    full = jnp.concatenate([feats[...].astype(F32), extra], 0)
    hi_wide = jnp.broadcast_to(hi, (24, 1024))
    spread = jnp.concatenate([jnp.where(hi_wide == float(h), full, 0.0).astype(BF16) for h in range(16)], 0)
    packed = dot_lanes(spread, hot)
    for h in range(16):
        send_a[h // 2, :, 128 * (h % 2) : 128 * (h % 2) + 128] = packed[24 * h : 24 * h + 24].astype(BF16)

    pl.semaphore_wait(barrier, len(peers))

    first = []
    for d in FAR_FIRST:
        first.append(send(send_a.at[(plane + d) % PLANE], recv_a.at[d], sem_j, (d,), j_peer(d)))
    for copy in fetches[3:]:
        copy.wait()

    lane = lax.broadcasted_iota(jnp.int32, (1, 128), 1)
    weight_moves = [send(w_in, w_all.at[d], sem_w, (0, d), x_peer(d)) for d in range(1, CHAN)]
    zero = jnp.zeros((24, 32), F32)
    for i in range(3):
        slabs = [jnp.concatenate([w_mid[9 * i + jl].astype(F32), zero], 1) for jl in range(TAPS)]
        for k in range(CHAN):
            tiles = []
            for group in (range(0, 5), range(5, 9)):
                tile = jnp.zeros((24, 128), F32)
                for u, jl in enumerate(group):
                    moved = pltpu.roll(slabs[jl], (24 * u - 24 * k) % 128, 1)
                    tile = jnp.where((lane >= 24 * u) & (lane < 24 * u + 24), moved, tile)
                tiles.append(tile)
            w_send_two[k, i] = jnp.concatenate(tiles, 1).astype(BF16)
    for d in range(1, CHAN):
        weight_moves.append(send(w_send_two.at[(q + d) % CHAN], w_recv_two.at[d], sem_w, (1, d), x_peer(d)))

    for copy in first:
        copy.wait_recv()
    parts = [send_a[plane].astype(F32)] + [recv_a[d].astype(F32) for d in range(1, PLANE)]
    for j, part in enumerate(swap_groups(parts)):
        send_b[j] = part.astype(BF16)
    second = []
    for d in FAR_FIRST:
        second.append(send(send_b.at[(z + d) % DEPTH], recv_b.at[d], sem_z, (d,), z_peer(d)))

    for copy in weight_moves:
        copy.wait_recv()
    zero = jnp.zeros((192, 32), F32)
    for jl in range(TAPS):
        pieces = [(w_in if r == 0 else w_all.at[r])[9 * i + jl].astype(F32) for i in range(3) for r in range(CHAN)]
        tall = jnp.concatenate([jnp.concatenate(pieces, 0), zero], 1)
        w_one[ALL * jl : ALL * jl + ALL, 0:192] = tall.T[0:ALL].astype(BF16)
    w_recv_two[0] = w_send_two[q]
    pieces = [w_recv_two[(q - k + CHAN) % CHAN, i].astype(F32) for i in range(3) for k in range(CHAN)]
    turned = jnp.concatenate(pieces + [jnp.zeros((ALL, 256), F32)], 0).T[:ROWS]
    out_id = lax.broadcasted_iota(jnp.int32, (ROWS, 384), 0) - tap_row(4)
    in_id = lax.broadcasted_iota(jnp.int32, (ROWS, 384), 1) - 3 * ALL - OUT * q
    same = (out_id == in_id) & (out_id >= 0) & (out_id < OUT)
    w_two[...] = jnp.where(same, 1.0, turned).astype(BF16)

    none = 36
    for b in range(BRICKS):
        for f in range(6):
            local = nbr[b, f] - BRICKS * s + BRICKS
            there = (nbr[b, f] >= 0) & (local >= 0) & (local < 3 * BRICKS)
            base = (local >> 2) * 12 + f // 2
            index[0, 6 * b + f] = jnp.where(there, base + 3 * (local & 3), none)
            index[1, 6 * b + f] = jnp.where(there, base + 3 * ((q - local) & 3), none)

    for copy in second:
        copy.wait_recv()
    slots = jnp.concatenate([send_b[z].astype(F32)] + [recv_b[d].astype(F32) for d in range(1, DEPTH)], 1)
    hi = slots[16:17]
    hot = one_hot(slots[17:18], 128)
    lot_s[...] = hot
    hi_s[...] = jnp.broadcast_to(hi, (8, VOX))
    hi_wide = jnp.broadcast_to(hi, (16, VOX))
    spread = jnp.concatenate([jnp.where(hi_wide == float(h), slots[0:16], 0.0).astype(BF16) for h in range(16)], 0)
    cells = dot_lanes(spread, hot)
    for h in range(16):
        x_one[h // 4, :, 128 * (h % 4) : 128 * (h % 4) + 128] = cells[16 * h : 16 * h + 16].astype(BF16)

    def rim(face, b, p, relative):
        low, high = (face[index[relative, 6 * b + f]].astype(F32) for f in (2 * p, 2 * p + 1))
        return jnp.where(lax.broadcasted_iota(jnp.int32, low.shape, 1) < 64, low, high)

    def tap_sum(full, count, row_of):
        total = None
        for jl in range(TAPS):
            term = full[row_of(jl) : row_of(jl) + count]
            term = jnp.concatenate([term[:, 128 * x : 128 * x + 128] for x in range(8)], 0)
            shift = 10 * (jl // 3) + jl % 3
            if shift:
                term = pltpu.roll(term, 128 - shift, 1)
            total = term if total is None else total + term
        return total

    def pack_planes(layer, count):
        return [
            jnp.concatenate(
                [layer[count * (2 * p) : count * (2 * p + 1)], layer[count * (2 * p + 1) : count * (2 * p + 2)]], 1
            )
            for p in range(4)
        ]

    rims = dot(jnp.concatenate([x_one[b] for b in range(BRICKS)], 0), sel[...])
    for b in range(BRICKS):
        for p in range(3):
            face_one[12 + 3 * b + p] = rims[16 * b : 16 * b + 16, 128 * p : 128 * p + 128].astype(BF16)
    face_one[none] = jnp.zeros((16, 128), BF16)
    face_two[none] = jnp.zeros((ALL, 128), BF16)
    beside = [
        send(face_one.at[12:24], face_one.at[24 * e : 24 * e + 12], sem_f, (3, e), s_peer(1 - 2 * e)) for e in (0, 1)
    ]
    centers = [send(x_one.at[(q + d) % CHAN], c_one.at[d], sem_x, (0, d), x_peer(d)) for d in (2, 1, 3)]
    for copy in beside:
        copy.wait_recv()
    for b in range(BRICKS):
        for p in range(3):
            h_send[b, p] = rim(face_one, b, p, 0).astype(BF16)
    halos = [send(h_send.at[(q + d) % CHAN], h_recv.at[d], sem_x, (1, d), x_peer(d)) for d in (2, 1, 3)]
    for copy in centers:
        copy.wait_recv()
    parts = [x_one[q].astype(F32)] + [c_one[r].astype(F32) for r in range(1, CHAN)]
    tiles = [part[:, 128 * p : 128 * p + 128] for part in parts for p in range(4)]
    inner = dot(jnp.concatenate(tiles, 0).astype(BF16), ec[...])
    for copy in halos:
        copy.wait_recv()
    edges = [jnp.concatenate([h_send[q, p]] + [h_recv[r, p] for r in range(1, CHAN)], 0) for p in range(3)]
    ends = dot(edges[0], ec[...]).astype(BF16)
    outer = dot(jnp.concatenate(edges[1:], 1), eh[...])
    pad_one[:, 0:128] = ends[:, 0:128]
    pad_one[:, 1152:1280] = ends[:, 128:256]
    for p in range(4):
        mid = jnp.concatenate([inner[(4 * r + p) * 16 : (4 * r + p + 1) * 16] for r in range(CHAN)], 0)
        pad_one[:, 128 + 256 * p : 384 + 256 * p] = (mid + outer[:, 256 * p : 256 * p + 256]).astype(BF16)
    deep = jnp.concatenate([pad_one[:, 128 * i : 128 * i + 1024] for i in range(3)], 0)
    layer = tap_sum(dot(w_one[:, 0:192], deep), ALL, lambda jl: ALL * jl)
    layer = jnp.maximum(layer, 0.0).astype(BF16).astype(F32)
    cells = dot(jnp.concatenate(pack_planes(layer, ALL), 0).astype(BF16), cm[...])
    for p in range(4):
        x_two[0, :, 128 * p : 128 * p + 128] = cells[ALL * p : ALL * p + ALL].astype(BF16)

    def piece(slot, t):
        return x_two.at[slot, 16 * t : 16 * t + 16]

    right, left = {}, {}
    for t in range(6):
        right[t] = send(piece(0, t), piece(1, t), sem_p, (0, t), x_peer(1))
        u = (t + 3) % 6
        left[u] = send(piece(0, u), piece(3, u), sem_p, (1, u), x_peer(3))
    face_moves = []

    def send_faces(r, at, sems, which):
        for e in (0, 1):
            src = face_two.at[12 + 3 * r : 15 + 3 * r, at]
            dst = face_two.at[24 * e + 3 * r : 24 * e + 3 * r + 3, at]
            face_moves.append(send(src, dst, sems, (*which, e), s_peer(1 - 2 * e)))

    def faces(r):
        rims = dot(x_two[r], sel[...])
        for p in range(3):
            face_two[12 + 3 * r + p] = rims[:, 128 * p : 128 * p + 128].astype(BF16)
        send_faces(r, slice(0, ALL), sem_f, (r if r < 2 else 2,))

    faces(0)
    relay = {}
    for t in range(3):
        right[t].wait_recv()
        relay[t] = send(piece(1, t), piece(2, t), sem_p, (2, t), x_peer(1))
        left[3 + t].wait_recv()
        relay[3 + t] = send(piece(3, 3 + t), piece(2, 3 + t), sem_p, (2, 3 + t), x_peer(3))
    for t in range(3, 6):
        right[t].wait_recv()
    faces(1)
    for t in range(3):
        left[t].wait_recv()
    faces(3)
    for t in range(3):
        relay[t].wait_recv()
        relay[3 + t].wait_recv()
        rows = [slice(16 * u, 16 * u + 16) for u in (t, 3 + t)]
        rims = dot(jnp.concatenate([x_two[2, at] for at in rows], 0), sel[...])
        for half, at in enumerate(rows):
            for p in range(3):
                face_two[18 + p, at] = rims[16 * half : 16 * half + 16, 128 * p : 128 * p + 128].astype(BF16)
            send_faces(2, at, sem_g, (t, half))
    bricks = [x_two[(q - b + CHAN) % CHAN] for b in range(BRICKS)]
    tiles = [brick[:, 128 * p : 128 * p + 128] for brick in bricks for p in range(4)]
    inner = dot(jnp.concatenate(tiles, 0), ec[...])
    for copy in face_moves:
        copy.wait_recv()
    edges = [
        jnp.concatenate([rim(face_two, b, p, 1).astype(BF16) for b in range(BRICKS)], 0) for p in range(3)
    ]
    ends = dot(edges[0], ec[...]).astype(BF16)
    outer = dot(jnp.concatenate(edges[1:], 1), eh[...])
    layers = []
    for b in range(BRICKS):
        pad_two[b, :, 0:128] = ends[ALL * b : ALL * b + ALL, 0:128]
        pad_two[b, :, 1152:1280] = ends[ALL * b : ALL * b + ALL, 128:256]
        for p in range(4):
            mid = inner[(4 * b + p) * ALL : (4 * b + p + 1) * ALL]
            mid = mid + outer[ALL * b : ALL * b + ALL, 256 * p : 256 * p + 256]
            pad_two[b, :, 128 + 256 * p : 384 + 256 * p] = mid.astype(BF16)
        deep = jnp.concatenate([pad_two[b, :, 128 * i : 128 * i + 1024] for i in (0, 1, 2, 1)], 0)
        layer = tap_sum(dot(w_two[...], deep), OUT, tap_row)
        layers += pack_planes(jnp.maximum(layer, 0.0), OUT)
    closed = dot(jnp.concatenate(layers, 0).astype(BF16), cm[...])
    cells = closed.astype(BF16)

    group = lax.broadcasted_iota(jnp.int32, (8, 128), 1) // 32
    back = []
    for d in [*FAR_FIRST, 0]:
        at = slice(256 * d, 256 * d + 256)
        found = dot(cells, lot_s[:, at])
        hi_wide = jnp.broadcast_to(hi_s[0:1, at], (OUT, 256))
        value = found[0:OUT]
        for h in range(1, 16):
            value = jnp.where(hi_wide == float(h), found[OUT * h : OUT * h + OUT], value)
        tiles = {}
        for t in range(2):
            half = value[:, 128 * t : 128 * t + 128]
            turned = [half] + [pltpu.roll(half, 32 * a, 1) for a in range(1, 4)]
            for u in range(4):
                low, mid, high = (turned[(m - u) % 4][8 * m : 8 * m + 8] for m in range(3))
                tiles[4 * t + u] = jnp.where(group == 0, low, jnp.where(group == 1, mid, high)).astype(BF16)
        for e in [*FAR_FIRST, 0]:
            if d == 0 and e == 0:
                ret_v[plane * DEPTH + z] = tiles[e]
            else:
                ret_a[PLANE * d + e] = tiles[e]
        for e in [*FAR_FIRST, 0]:
            if d or e:
                other = (plane - e + PLANE) % PLANE
                peer = {"space": ((other // 2) * DEPTH + (z - d + DEPTH) % DEPTH) * 2 + other % 2, "chan": q}
                back.append(
                    send(ret_a.at[PLANE * d + e], ret_v.at[plane * DEPTH + z], sem_ret, (PLANE * d + e,), peer)
                )
    for p in range(4):
        tiles = [closed[OUT * (4 * b + p) : OUT * (4 * b + p) + OUT] for b in range(BRICKS)]
        grid_out[:, :, 128 * p : 128 * p + 128] = jnp.stack(tiles, 1).astype(BF16)
    for copy in started:
        copy.wait_send()
    for copy in back:
        copy.wait_recv()
    tall = jnp.concatenate([ret_v[i] for i in range(64)], 0).astype(F32)
    turned = [tall] + [pltpu.roll(tall, 32 * a, 1) for a in range(1, 4)]
    lines = []
    for h in range(16):
        for m in range(3):
            line = None
            for u in range(4):
                piece = turned[(u - m) % 4][8 * (4 * h + u) : 8 * (4 * h + u) + 8]
                line = piece if line is None else jnp.where(group == u, piece, line)
            lines.append(line)
    found = dot(jnp.concatenate(lines, 0).astype(BF16), lot_p[...])
    hi_wide = jnp.broadcast_to(hi_p[0:1], (OUT, 1024))
    value = found[0:OUT]
    for h in range(1, 16):
        value = jnp.where(hi_wide == float(h), found[OUT * h : OUT * h + OUT], value)
    point_out[...] = value.astype(BF16)


def deliver(grid, values, grid_out, point_out, sems):
    copies = [pltpu.make_async_copy(a, b, sems.at[i]) for i, (a, b) in enumerate(((grid, grid_out), (values, point_out)))]
    for copy in copies:
        copy.start()
    for copy in copies:
        copy.wait()


def per_device(point_feats, point_owner, point_place, neighbors, weight_in, weight_mid):
    anywhere = pl.BlockSpec(memory_space=pl.ANY)
    constants = [jnp.asarray(c(), BF16) for c in (face_picker, plane_spread, rim_spread, plane_pack)]
    points = point_feats.shape[1]
    grid, values = pl.pallas_call(
        body,
        out_shape=(
            pltpu.VMEM((OUT, BRICKS, CELLS), BF16),
            pltpu.VMEM((OUT, points), BF16),
        ),
        in_specs=[anywhere] * 10,
        out_specs=(pl.BlockSpec(memory_space=pltpu.VMEM), pl.BlockSpec(memory_space=pltpu.VMEM)),
        scratch_shapes=[
            pltpu.VMEM((16, points), BF16),
            pltpu.VMEM((1, points), jnp.int32),
            pltpu.VMEM((1, points), jnp.int32),
            pltpu.SMEM((4, 6), jnp.int32),
            pltpu.VMEM((27, 16, 96), BF16),
            pltpu.VMEM((27, 24, 96), BF16),
            *[pltpu.VMEM(c.shape, BF16) for c in constants],
            pltpu.SemaphoreType.DMA((10,)),
            pltpu.SMEM((2, 24), jnp.int32),
            pltpu.VMEM((8, 24, 256), BF16),
            pltpu.VMEM((8, 24, 256), BF16),
            pltpu.VMEM((8, 24, 256), BF16),
            pltpu.VMEM((8, 24, 256), BF16),
            pltpu.VMEM((4, 16, CELLS), BF16),
            pltpu.VMEM((4, 16, CELLS), BF16),
            pltpu.VMEM((4, 3, 16, 128), BF16),
            pltpu.VMEM((4, 3, 16, 128), BF16),
            pltpu.VMEM((4, ALL, CELLS), BF16),
            pltpu.VMEM((37, 16, 128), BF16),
            pltpu.VMEM((37, ALL, 128), BF16),
            pltpu.VMEM((4, 27, 16, 96), BF16),
            pltpu.VMEM((4, 3, 24, 256), BF16),
            pltpu.VMEM((4, 3, 24, 256), BF16),
            pltpu.VMEM((TAPS * ALL, 256), BF16),
            pltpu.VMEM((ROWS, 384), BF16),
            pltpu.VMEM((128, points), BF16),
            pltpu.VMEM((8, points), F32),
            pltpu.VMEM((128, VOX), BF16),
            pltpu.VMEM((8, VOX), F32),
            pltpu.VMEM((64, 1280), BF16),
            pltpu.VMEM((4, ALL, 1280), BF16),
            pltpu.VMEM((64, 8, 128), BF16),
            pltpu.VMEM((64, 8, 128), BF16),
            pltpu.SemaphoreType.DMA((2, 8)),
            pltpu.SemaphoreType.DMA((2, 8)),
            pltpu.SemaphoreType.DMA((2, 2, 4)),
            pltpu.SemaphoreType.DMA((2, 3, 6)),
            pltpu.SemaphoreType.DMA((2, 4, 2)),
            pltpu.SemaphoreType.DMA((2, 3, 2, 2)),
            pltpu.SemaphoreType.DMA((2, 2, 4)),
            pltpu.SemaphoreType.DMA((2, 64)),
        ],
        compiler_params=pltpu.CompilerParams(collective_id=0, has_side_effects=True),
    )(
        point_feats,
        point_owner.reshape(1, points),
        point_place.reshape(1, points),
        neighbors,
        jnp.transpose(weight_in, (1, 0, 2)),
        jnp.transpose(weight_mid, (1, 0, 2)),
        *constants,
    )
    grid, values = (pltpu.with_memory_space_constraint(a, pltpu.VMEM) for a in (grid, values))
    return pl.pallas_call(
        deliver,
        out_shape=(
            jax.ShapeDtypeStruct((OUT, BRICKS, CELLS), BF16),
            jax.ShapeDtypeStruct((OUT, points), BF16),
        ),
        in_specs=[pl.BlockSpec(memory_space=pltpu.VMEM)] * 2,
        out_specs=(anywhere, anywhere),
        scratch_shapes=[pltpu.SemaphoreType.DMA((2,))],
    )(grid, values)


def solution(mesh):
    return jax.shard_map(
        per_device,
        mesh=mesh,
        in_specs=(
            P("chan", "space"),
            P("space", None),
            P("space"),
            P("space", None),
            P("chan", None, None),
            P("chan", None, None),
        ),
        out_specs=(P("chan", "space", None), P("chan", "space")),
        check_vma=False,
    )
```

```python
import functools

import jax
import jax.numpy as jnp
import numpy as np
from jax import lax
from jax.experimental import pallas as pl
from jax.experimental.pallas import tpu as pltpu
from jax.sharding import PartitionSpec as P

DEPTH = 8
PLANE = 8
CHAN = 4
CAP = 32
CELLS = 512
BRICKS = 4
VOX = BRICKS * CELLS
OUT = 24
TAPS = 9
F32 = jnp.float32
BF16 = jnp.bfloat16
MESH = pl.DeviceIdType.MESH


def tap_row(jl):
    return OUT * jl + (8 if jl >= 5 else 0)


ROWS = 224
ALL = 96
FAR_FIRST = (4, 3, 5, 2, 6, 1, 7)


def face_picker():
    sel = np.zeros((CELLS, 384), np.float32)
    for u in range(8):
        for w in range(8):
            for p in range(3):
                for half, end in ((0, 7), (1, 0)):
                    x, y, z = ((end, u, w), (u, end, w), (u, w, end))[p]
                    sel[(8 * x + y) * 8 + z, 128 * p + 64 * half + 8 * u + w] = 1
    return sel


def plane_spread():
    ec = np.zeros((128, 256), np.float32)
    for x in range(2):
        for y in range(8):
            for z in range(8):
                ec[64 * x + 8 * y + z, 128 * x + 10 * (y + 1) + z + 1] = 1
    return ec


def rim_spread():
    eh = np.zeros((256, 1024), np.float32)
    for x in range(8):
        for w in range(8):
            eh[8 * x + w, 128 * x + w + 1] = 1
            eh[64 + 8 * x + w, 128 * x + 90 + w + 1] = 1
            eh[128 + 8 * x + w, 128 * x + 10 * (w + 1)] = 1
            eh[192 + 8 * x + w, 128 * x + 10 * (w + 1) + 9] = 1
    return eh


def plane_pack():
    cm = np.zeros((256, 128), np.float32)
    for x in range(2):
        for y in range(8):
            for z in range(8):
                cm[128 * x + 10 * y + z, 64 * x + 8 * y + z] = 1
    return cm


def dot(a, b):
    return jnp.dot(a, b, preferred_element_type=F32)


def dot_lanes(a, b):
    return lax.dot_general(a, b, (((1,), (1,)), ((), ())), preferred_element_type=F32)


def one_hot(row, count):
    ids = lax.broadcasted_iota(jnp.int32, (count, row.shape[1]), 0).astype(F32)
    return jnp.where(ids == row, 1.0, 0.0).astype(BF16)


def pick(choices):
    group = lax.broadcasted_iota(jnp.int32, (8, 128), 1) // 32
    result = choices[-1]
    for i in reversed(range(len(choices) - 1)):
        result = jnp.where(group == i, choices[i], result)
    return result


def split_tiles(tall):
    turned = [tall] + [pltpu.roll(tall, 32 * a, 1) for a in range(1, 4)]
    return [
        pick([turned[(m - u) % 4][24 * h + 8 * m : 24 * h + 8 * m + 8] for m in range(3)])
        for h in range(tall.shape[0] // 24)
        for u in range(4)
    ]


def join_tiles(tiles):
    tall = jnp.concatenate(tiles, 0)
    turned = [tall] + [pltpu.roll(tall, 32 * a, 1) for a in range(1, 4)]
    return jnp.concatenate(
        [
            pick([turned[(u - m) % 4][8 * (4 * h + u) : 8 * (4 * h + u) + 8] for u in range(4)])
            for h in range(len(tiles) // 4)
            for m in range(3)
        ],
        0,
    )


def body(
    feats_in, owner_in, place_in, nbr_in, w_in_in, w_mid_in, sel_in, ec_in, eh_in, cm_in,
    grid_out, point_out,
    feats, owner, place, nbr, w_in, w_mid, sel, ec, eh, cm, sem_in, index,
    send_a, recv_a, x_one, c_one, h_send, h_recv, x_two, face_one, face_two, w_all, w_send_two, w_recv_two,
    w_one, w_two, lot_p, hi_p, lot_s, hi_s, pad_one, pad_two, ret_a, ret_v,
    sem_out, sem_x, sem_p, sem_f, sem_g, sem_w, sem_ret,
):
    s = lax.axis_index("space")
    q = lax.axis_index("chan")
    core = s % 2
    z = (s // 2) % DEPTH
    row = s // (2 * DEPTH)
    plane = row * 2 + core
    spaces = 64

    def far_peer(d, e):
        other = (plane + e + PLANE) % PLANE
        return {"space": ((other // 2) * DEPTH + (z + d + DEPTH) % DEPTH) * 2 + other % 2, "chan": q}

    def x_peer(d):
        return {"space": s, "chan": (q + d) % CHAN}

    def s_peer(d):
        return {"space": (s + d + spaces) % spaces, "chan": q}

    started = []

    def send(src, dst, sems, at, peer):
        copy = pltpu.make_async_remote_copy(
            src_ref=src, dst_ref=dst, send_sem=sems.at[(0, *at)], recv_sem=sems.at[(1, *at)], device_id=peer, device_id_type=MESH
        )
        copy.start()
        started.append(copy)
        return copy

    fetches = [
        pltpu.make_async_copy(src, dst, sem_in.at[i])
        for i, (src, dst) in enumerate(
            (
                (owner_in, owner), (place_in, place), (feats_in, feats), (w_in_in, w_in), (w_mid_in, w_mid),
                (nbr_in, nbr), (sel_in, sel), (ec_in, ec), (eh_in, eh), (cm_in, cm),
            )
        )
    ]
    for copy in fetches:
        copy.start()
    pairs = [(d, e) for d in (*FAR_FIRST, 0) for e in (*FAR_FIRST, 0) if d or e]
    peers = [far_peer(d, e) for d, e in pairs] + [x_peer(d) for d in range(1, CHAN)]
    barrier = pltpu.get_barrier_semaphore()
    for peer in peers:
        pl.semaphore_signal(barrier, inc=1, device_id=peer, device_id_type=MESH)

    for copy in fetches[:3]:
        copy.wait()

    own = owner[...]
    where_to = place[...]
    match = jnp.where(lax.broadcasted_iota(jnp.int32, (64, 1024), 0) == own, 1.0, 0.0)
    tall = jnp.concatenate([match[:, 256 * i : 256 * i + 256] for i in range(4)], 0)
    before = jnp.where(
        lax.broadcasted_iota(jnp.int32, (256, 256), 0) < lax.broadcasted_iota(jnp.int32, (256, 256), 1), 1.0, 0.0
    )
    earlier = dot(tall.astype(BF16), before.astype(BF16))
    carry = jnp.zeros((64, 1), F32)
    ranks = []
    for i in range(4):
        mine = tall[64 * i : 64 * i + 64]
        ranks.append(jnp.sum(mine * (earlier[64 * i : 64 * i + 64] + carry), axis=0, keepdims=True))
        carry = carry + jnp.sum(mine, axis=1, keepdims=True)
    rank = jnp.concatenate(ranks, 1)
    to_z = ((own // 2) - z) & 7
    to_plane = ((own // (2 * DEPTH)) * 2 + (own & 1) - plane) & 7
    hi = (to_z * 2 + to_plane // 4).astype(F32)
    lo = ((to_plane & 3) * CAP).astype(F32) + rank
    hot = one_hot(lo, 128)
    lot_p[...] = hot
    hi_p[...] = jnp.broadcast_to(hi, (8, 1024))
    extra = lax.broadcasted_iota(jnp.int32, (8, 1024), 0)
    extra = jnp.where(
        extra == 0, (where_to // 128).astype(F32), jnp.where(extra == 1, (where_to % 128).astype(F32), 0.0)
    )
    full = jnp.concatenate([feats[...].astype(F32), extra], 0)
    hi_wide = jnp.broadcast_to(hi, (24, 1024))
    spread = jnp.concatenate([jnp.where(hi_wide == float(h), full, 0.0).astype(BF16) for h in range(16)], 0)
    packed = dot_lanes(spread, hot)
    for i, tile in enumerate(split_tiles(packed)):
        send_a[i] = tile.astype(BF16)

    pl.semaphore_wait(barrier, len(peers))

    away = {}
    for d, e in pairs:
        at = PLANE * d + e
        away[at] = send(send_a.at[at], recv_a.at[at], sem_out, (at,), far_peer(d, e))
    for copy in fetches[3:]:
        copy.wait()

    lane = lax.broadcasted_iota(jnp.int32, (1, 128), 1)
    weight_moves = [send(w_in, w_all.at[d], sem_w, (0, d), x_peer(d)) for d in range(1, CHAN)]
    zero = jnp.zeros((24, 32), F32)
    for i in range(3):
        slabs = [jnp.concatenate([w_mid[9 * i + jl].astype(F32), zero], 1) for jl in range(TAPS)]
        for k in range(CHAN):
            tiles = []
            for group in (range(0, 5), range(5, 9)):
                tile = jnp.zeros((24, 128), F32)
                for u, jl in enumerate(group):
                    moved = pltpu.roll(slabs[jl], (24 * u - 24 * k) % 128, 1)
                    tile = jnp.where((lane >= 24 * u) & (lane < 24 * u + 24), moved, tile)
                tiles.append(tile)
            w_send_two[k, i] = jnp.concatenate(tiles, 1).astype(BF16)
    for d in range(1, CHAN):
        weight_moves.append(send(w_send_two.at[(q + d) % CHAN], w_recv_two.at[d], sem_w, (1, d), x_peer(d)))

    none = 36
    for b in range(BRICKS):
        for f in range(6):
            local = nbr[b, f] - BRICKS * s + BRICKS
            there = (nbr[b, f] >= 0) & (local >= 0) & (local < 3 * BRICKS)
            base = (local >> 2) * 12 + f // 2
            index[0, 6 * b + f] = jnp.where(there, base + 3 * (local & 3), none)
            index[1, 6 * b + f] = jnp.where(there, base + 3 * ((q - local) & 3), none)

    cells = jnp.zeros((256, 128), F32)
    for d in (0, 1, 7, 2, 6, 3, 5, 4):
        at = slice(256 * d, 256 * d + 256)
        for e in range(PLANE):
            if d or e:
                away[PLANE * d + e].wait_recv()
        tiles = [(recv_a if d or e else send_a)[PLANE * d + e].astype(F32) for e in range(PLANE)]
        slots = join_tiles(tiles)
        slots = jnp.concatenate([slots[0:24], slots[24:48]], 1)
        hi = slots[16:17]
        hot = one_hot(slots[17:18], 128)
        lot_s[:, at] = hot
        hi_s[:, at] = jnp.broadcast_to(hi, (8, 256))
        hi_wide = jnp.broadcast_to(hi, (16, 256))
        spread = [jnp.where(hi_wide == float(h), slots[0:16], 0.0).astype(BF16) for h in range(16)]
        cells = cells + dot_lanes(jnp.concatenate(spread, 0), hot)
    for h in range(16):
        x_one[h // 4, :, 128 * (h % 4) : 128 * (h % 4) + 128] = cells[16 * h : 16 * h + 16].astype(BF16)

    def rim(face, b, p, relative):
        low, high = (face[index[relative, 6 * b + f]].astype(F32) for f in (2 * p, 2 * p + 1))
        return jnp.where(lax.broadcasted_iota(jnp.int32, low.shape, 1) < 64, low, high)

    def tap_sum(full, count, row_of):
        total = None
        for jl in range(TAPS):
            term = full[row_of(jl) : row_of(jl) + count]
            term = jnp.concatenate([term[:, 128 * x : 128 * x + 128] for x in range(8)], 0)
            shift = 10 * (jl // 3) + jl % 3
            if shift:
                term = pltpu.roll(term, 128 - shift, 1)
            total = term if total is None else total + term
        return total

    def pack_planes(layer, count):
        return [
            jnp.concatenate(
                [layer[count * (2 * p) : count * (2 * p + 1)], layer[count * (2 * p + 1) : count * (2 * p + 2)]], 1
            )
            for p in range(4)
        ]

    rims = dot(jnp.concatenate([x_one[b] for b in range(BRICKS)], 0), sel[...])
    for b in range(BRICKS):
        for p in range(3):
            face_one[12 + 3 * b + p] = rims[16 * b : 16 * b + 16, 128 * p : 128 * p + 128].astype(BF16)
    face_one[none] = jnp.zeros((16, 128), BF16)
    face_two[none] = jnp.zeros((ALL, 128), BF16)
    beside = [
        send(face_one.at[12:24], face_one.at[24 * e : 24 * e + 12], sem_f, (3, e), s_peer(1 - 2 * e)) for e in (0, 1)
    ]
    centers = [send(x_one.at[(q + d) % CHAN], c_one.at[d], sem_x, (0, d), x_peer(d)) for d in (2, 1, 3)]
    for copy in weight_moves:
        copy.wait_recv()
    zero = jnp.zeros((192, 32), F32)
    for jl in range(TAPS):
        pieces = [(w_in if r == 0 else w_all.at[r])[9 * i + jl].astype(F32) for i in range(3) for r in range(CHAN)]
        tall = jnp.concatenate([jnp.concatenate(pieces, 0), zero], 1)
        w_one[ALL * jl : ALL * jl + ALL, 0:192] = tall.T[0:ALL].astype(BF16)
    w_recv_two[0] = w_send_two[q]
    pieces = [w_recv_two[(q - k + CHAN) % CHAN, i].astype(F32) for i in range(3) for k in range(CHAN)]
    turned = jnp.concatenate(pieces + [jnp.zeros((ALL, 256), F32)], 0).T[:ROWS]
    out_id = lax.broadcasted_iota(jnp.int32, (ROWS, 384), 0) - tap_row(4)
    in_id = lax.broadcasted_iota(jnp.int32, (ROWS, 384), 1) - 3 * ALL - OUT * q
    same = (out_id == in_id) & (out_id >= 0) & (out_id < OUT)
    w_two[...] = jnp.where(same, 1.0, turned).astype(BF16)

    for copy in beside:
        copy.wait_recv()
    for b in range(BRICKS):
        for p in range(3):
            h_send[b, p] = rim(face_one, b, p, 0).astype(BF16)
    halos = [send(h_send.at[(q + d) % CHAN], h_recv.at[d], sem_x, (1, d), x_peer(d)) for d in (2, 1, 3)]
    for copy in centers:
        copy.wait_recv()
    parts = [x_one[q].astype(F32)] + [c_one[r].astype(F32) for r in range(1, CHAN)]
    tiles = [part[:, 128 * p : 128 * p + 128] for part in parts for p in range(4)]
    inner = dot(jnp.concatenate(tiles, 0).astype(BF16), ec[...])
    for copy in halos:
        copy.wait_recv()
    edges = [jnp.concatenate([h_send[q, p]] + [h_recv[r, p] for r in range(1, CHAN)], 0) for p in range(3)]
    ends = dot(edges[0], ec[...]).astype(BF16)
    outer = dot(jnp.concatenate(edges[1:], 1), eh[...])
    pad_one[:, 0:128] = ends[:, 0:128]
    pad_one[:, 1152:1280] = ends[:, 128:256]
    for p in range(4):
        mid = jnp.concatenate([inner[(4 * r + p) * 16 : (4 * r + p + 1) * 16] for r in range(CHAN)], 0)
        pad_one[:, 128 + 256 * p : 384 + 256 * p] = (mid + outer[:, 256 * p : 256 * p + 256]).astype(BF16)
    deep = jnp.concatenate([pad_one[:, 128 * i : 128 * i + 1024] for i in range(3)], 0)
    layer = tap_sum(dot(w_one[:, 0:192], deep), ALL, lambda jl: ALL * jl)
    layer = jnp.maximum(layer, 0.0).astype(BF16).astype(F32)
    cells = dot(jnp.concatenate(pack_planes(layer, ALL), 0).astype(BF16), cm[...])
    for p in range(4):
        x_two[0, :, 128 * p : 128 * p + 128] = cells[ALL * p : ALL * p + ALL].astype(BF16)

    def piece(slot, t):
        return x_two.at[slot, 16 * t : 16 * t + 16]

    right, left = {}, {}
    for t in range(6):
        right[t] = send(piece(0, t), piece(1, t), sem_p, (0, t), x_peer(1))
        u = (t + 3) % 6
        left[u] = send(piece(0, u), piece(3, u), sem_p, (1, u), x_peer(3))
    face_moves = []

    def send_faces(r, at, sems, which):
        for e in (0, 1):
            src = face_two.at[12 + 3 * r : 15 + 3 * r, at]
            dst = face_two.at[24 * e + 3 * r : 24 * e + 3 * r + 3, at]
            face_moves.append(send(src, dst, sems, (*which, e), s_peer(1 - 2 * e)))

    def faces(r):
        rims = dot(x_two[r], sel[...])
        for p in range(3):
            face_two[12 + 3 * r + p] = rims[:, 128 * p : 128 * p + 128].astype(BF16)
        send_faces(r, slice(0, ALL), sem_f, (r if r < 2 else 2,))

    faces(0)
    relay = {}
    for t in range(3):
        right[t].wait_recv()
        relay[t] = send(piece(1, t), piece(2, t), sem_p, (2, t), x_peer(1))
        left[3 + t].wait_recv()
        relay[3 + t] = send(piece(3, 3 + t), piece(2, 3 + t), sem_p, (2, 3 + t), x_peer(3))
    for t in range(3, 6):
        right[t].wait_recv()
    faces(1)
    for t in range(3):
        left[t].wait_recv()
    faces(3)
    for t in range(3):
        relay[t].wait_recv()
        relay[3 + t].wait_recv()
        rows = [slice(16 * u, 16 * u + 16) for u in (t, 3 + t)]
        rims = dot(jnp.concatenate([x_two[2, at] for at in rows], 0), sel[...])
        for half, at in enumerate(rows):
            for p in range(3):
                face_two[18 + p, at] = rims[16 * half : 16 * half + 16, 128 * p : 128 * p + 128].astype(BF16)
            send_faces(2, at, sem_g, (t, half))
    bricks = [x_two[(q - b + CHAN) % CHAN] for b in range(BRICKS)]
    tiles = [brick[:, 128 * p : 128 * p + 128] for brick in bricks for p in range(4)]
    inner = dot(jnp.concatenate(tiles, 0), ec[...])
    for copy in face_moves:
        copy.wait_recv()
    edges = [
        jnp.concatenate([rim(face_two, b, p, 1).astype(BF16) for b in range(BRICKS)], 0) for p in range(3)
    ]
    ends = dot(edges[0], ec[...]).astype(BF16)
    outer = dot(jnp.concatenate(edges[1:], 1), eh[...])
    layers = []
    for b in range(BRICKS):
        pad_two[b, :, 0:128] = ends[ALL * b : ALL * b + ALL, 0:128]
        pad_two[b, :, 1152:1280] = ends[ALL * b : ALL * b + ALL, 128:256]
        for p in range(4):
            mid = inner[(4 * b + p) * ALL : (4 * b + p + 1) * ALL]
            mid = mid + outer[ALL * b : ALL * b + ALL, 256 * p : 256 * p + 256]
            pad_two[b, :, 128 + 256 * p : 384 + 256 * p] = mid.astype(BF16)
        deep = jnp.concatenate([pad_two[b, :, 128 * i : 128 * i + 1024] for i in (0, 1, 2, 1)], 0)
        layer = tap_sum(dot(w_two[...], deep), OUT, tap_row)
        layers += pack_planes(jnp.maximum(layer, 0.0), OUT)
    closed = dot(jnp.concatenate(layers, 0).astype(BF16), cm[...])
    cells = closed.astype(BF16)

    back = {}
    for d in [*FAR_FIRST, 0]:
        at = slice(256 * d, 256 * d + 256)
        found = dot(cells, lot_s[:, at])
        hi_wide = jnp.broadcast_to(hi_s[0:1, at], (OUT, 256))
        value = found[0:OUT]
        for h in range(1, 16):
            value = jnp.where(hi_wide == float(h), found[OUT * h : OUT * h + OUT], value)
        tiles = split_tiles(jnp.concatenate([value[:, 0:128], value[:, 128:256]], 0))
        for e in range(PLANE):
            (ret_a if d or e else ret_v)[PLANE * d + e] = tiles[e].astype(BF16)
        for e in [*FAR_FIRST, 0]:
            if d or e:
                at = PLANE * d + e
                back[at] = send(ret_a.at[at], ret_v.at[at], sem_ret, (at,), far_peer(-d, -e))
    for p in range(4):
        tiles = [closed[OUT * (4 * b + p) : OUT * (4 * b + p) + OUT] for b in range(BRICKS)]
        grid_out[:, :, 128 * p : 128 * p + 128] = jnp.stack(tiles, 1).astype(BF16)
    for copy in started:
        copy.wait_send()
    hi_wide = jnp.broadcast_to(hi_p[0:1], (OUT, 1024))
    value = jnp.zeros((OUT, 1024), F32)
    for near in ((0, 1, 7), (2, 6), (3, 5, 4)):
        ids = [PLANE * d + e for d in near for e in range(PLANE)]
        for at in ids:
            if at:
                back[at].wait_recv()
        lines = join_tiles([ret_v[at].astype(F32) for at in ids])
        found = dot(lines.astype(BF16), lot_p[...])
        for i, h in enumerate(2 * d + half for d in near for half in (0, 1)):
            value = jnp.where(hi_wide == float(h), found[OUT * i : OUT * i + OUT], value)
    point_out[...] = value.astype(BF16)


def deliver(grid, values, grid_out, point_out, sems):
    copies = [pltpu.make_async_copy(a, b, sems.at[i]) for i, (a, b) in enumerate(((grid, grid_out), (values, point_out)))]
    for copy in copies:
        copy.start()
    for copy in copies:
        copy.wait()


def per_device(point_feats, point_owner, point_place, neighbors, weight_in, weight_mid):
    anywhere = pl.BlockSpec(memory_space=pl.ANY)
    constants = [jnp.asarray(c(), BF16) for c in (face_picker, plane_spread, rim_spread, plane_pack)]
    points = point_feats.shape[1]
    grid, values = pl.pallas_call(
        body,
        out_shape=(
            pltpu.VMEM((OUT, BRICKS, CELLS), BF16),
            pltpu.VMEM((OUT, points), BF16),
        ),
        in_specs=[anywhere] * 10,
        out_specs=(pl.BlockSpec(memory_space=pltpu.VMEM), pl.BlockSpec(memory_space=pltpu.VMEM)),
        scratch_shapes=[
            pltpu.VMEM((16, points), BF16),
            pltpu.VMEM((1, points), jnp.int32),
            pltpu.VMEM((1, points), jnp.int32),
            pltpu.SMEM((4, 6), jnp.int32),
            pltpu.VMEM((27, 16, 96), BF16),
            pltpu.VMEM((27, 24, 96), BF16),
            *[pltpu.VMEM(c.shape, BF16) for c in constants],
            pltpu.SemaphoreType.DMA((10,)),
            pltpu.SMEM((2, 24), jnp.int32),
            pltpu.VMEM((64, 8, 128), BF16),
            pltpu.VMEM((64, 8, 128), BF16),
            pltpu.VMEM((4, 16, CELLS), BF16),
            pltpu.VMEM((4, 16, CELLS), BF16),
            pltpu.VMEM((4, 3, 16, 128), BF16),
            pltpu.VMEM((4, 3, 16, 128), BF16),
            pltpu.VMEM((4, ALL, CELLS), BF16),
            pltpu.VMEM((37, 16, 128), BF16),
            pltpu.VMEM((37, ALL, 128), BF16),
            pltpu.VMEM((4, 27, 16, 96), BF16),
            pltpu.VMEM((4, 3, 24, 256), BF16),
            pltpu.VMEM((4, 3, 24, 256), BF16),
            pltpu.VMEM((TAPS * ALL, 256), BF16),
            pltpu.VMEM((ROWS, 384), BF16),
            pltpu.VMEM((128, points), BF16),
            pltpu.VMEM((8, points), F32),
            pltpu.VMEM((128, VOX), BF16),
            pltpu.VMEM((8, VOX), F32),
            pltpu.VMEM((64, 1280), BF16),
            pltpu.VMEM((4, ALL, 1280), BF16),
            pltpu.VMEM((64, 8, 128), BF16),
            pltpu.VMEM((64, 8, 128), BF16),
            pltpu.SemaphoreType.DMA((2, 64)),
            pltpu.SemaphoreType.DMA((2, 2, 4)),
            pltpu.SemaphoreType.DMA((2, 3, 6)),
            pltpu.SemaphoreType.DMA((2, 4, 2)),
            pltpu.SemaphoreType.DMA((2, 3, 2, 2)),
            pltpu.SemaphoreType.DMA((2, 2, 4)),
            pltpu.SemaphoreType.DMA((2, 64)),
        ],
        compiler_params=pltpu.CompilerParams(collective_id=0, has_side_effects=True),
    )(
        point_feats,
        point_owner.reshape(1, points),
        point_place.reshape(1, points),
        neighbors,
        jnp.transpose(weight_in, (1, 0, 2)),
        jnp.transpose(weight_mid, (1, 0, 2)),
        *constants,
    )
    grid, values = (pltpu.with_memory_space_constraint(a, pltpu.VMEM) for a in (grid, values))
    return pl.pallas_call(
        deliver,
        out_shape=(
            jax.ShapeDtypeStruct((OUT, BRICKS, CELLS), BF16),
            jax.ShapeDtypeStruct((OUT, points), BF16),
        ),
        in_specs=[pl.BlockSpec(memory_space=pltpu.VMEM)] * 2,
        out_specs=(anywhere, anywhere),
        scratch_shapes=[pltpu.SemaphoreType.DMA((2,))],
    )(grid, values)


def solution(mesh):
    return jax.shard_map(
        per_device,
        mesh=mesh,
        in_specs=(
            P("chan", "space"),
            P("space", None),
            P("space"),
            P("space", None),
            P("chan", None, None),
            P("chan", None, None),
        ),
        out_specs=(P("chan", "space", None), P("chan", "space")),
        check_vma=False,
    )
```

```python
import functools

import jax
import jax.numpy as jnp
import numpy as np
from jax import lax
from jax.experimental import pallas as pl
from jax.experimental.pallas import tpu as pltpu
from jax.sharding import PartitionSpec as P

DEPTH = 8
PLANE = 8
CHAN = 4
CAP = 32
CELLS = 512
BRICKS = 4
VOX = BRICKS * CELLS
OUT = 24
TAPS = 9
F32 = jnp.float32
BF16 = jnp.bfloat16
MESH = pl.DeviceIdType.MESH


def tap_row(jl):
    return OUT * jl + (8 if jl >= 5 else 0)


ROWS = 224
ALL = 96
FAR_FIRST = (4, 3, 5, 2, 6, 1, 7)


def face_picker():
    sel = np.zeros((CELLS, 384), np.float32)
    for u in range(8):
        for w in range(8):
            for p in range(3):
                for half, end in ((0, 7), (1, 0)):
                    x, y, z = ((end, u, w), (u, end, w), (u, w, end))[p]
                    sel[(8 * x + y) * 8 + z, 128 * p + 64 * half + 8 * u + w] = 1
    return sel


def plane_spread():
    ec = np.zeros((128, 256), np.float32)
    for x in range(2):
        for y in range(8):
            for z in range(8):
                ec[64 * x + 8 * y + z, 128 * x + 10 * (y + 1) + z + 1] = 1
    return ec


def rim_spread():
    eh = np.zeros((256, 1024), np.float32)
    for x in range(8):
        for w in range(8):
            eh[8 * x + w, 128 * x + w + 1] = 1
            eh[64 + 8 * x + w, 128 * x + 90 + w + 1] = 1
            eh[128 + 8 * x + w, 128 * x + 10 * (w + 1)] = 1
            eh[192 + 8 * x + w, 128 * x + 10 * (w + 1) + 9] = 1
    return eh


def plane_pack():
    cm = np.zeros((256, 128), np.float32)
    for x in range(2):
        for y in range(8):
            for z in range(8):
                cm[128 * x + 10 * y + z, 64 * x + 8 * y + z] = 1
    return cm


def dot(a, b):
    return jnp.dot(a, b, preferred_element_type=F32)


def dot_lanes(a, b):
    return lax.dot_general(a, b, (((1,), (1,)), ((), ())), preferred_element_type=F32)


def one_hot(row, count):
    ids = lax.broadcasted_iota(jnp.int32, (count, row.shape[1]), 0).astype(F32)
    return jnp.where(ids == row, 1.0, 0.0).astype(BF16)


def pick(choices):
    group = lax.broadcasted_iota(jnp.int32, (8, 128), 1) // 32
    result = choices[-1]
    for i in reversed(range(len(choices) - 1)):
        result = jnp.where(group == i, choices[i], result)
    return result


def split_tiles(tall):
    turned = [tall] + [pltpu.roll(tall, 32 * a, 1) for a in range(1, 4)]
    return [
        pick([turned[(m - u) % 4][24 * h + 8 * m : 24 * h + 8 * m + 8] for m in range(3)])
        for h in range(tall.shape[0] // 24)
        for u in range(4)
    ]


def join_tiles(tiles):
    tall = jnp.concatenate(tiles, 0)
    turned = [tall] + [pltpu.roll(tall, 32 * a, 1) for a in range(1, 4)]
    return jnp.concatenate(
        [
            pick([turned[(u - m) % 4][8 * (4 * h + u) : 8 * (4 * h + u) + 8] for u in range(4)])
            for h in range(len(tiles) // 4)
            for m in range(3)
        ],
        0,
    )


def swap_groups(parts):
    rows = parts[0].shape[0]
    tall = jnp.concatenate([p[:, 128 * m : 128 * m + 128] for p in parts for m in range(2)], 0)
    turned = [tall] + [pltpu.roll(tall, 32 * a, 1) for a in range(1, 4)]
    group = lax.broadcasted_iota(jnp.int32, (rows, 128), 1) // 32
    result = []
    for j in range(8):
        m, g = j // 4, j % 4
        tiles = []
        for t in range(2):
            tile = None
            for u in range(4):
                at = (2 * (4 * t + u) + m) * rows
                piece = turned[(u - g) % 4][at : at + rows]
                tile = piece if tile is None else jnp.where(group == u, piece, tile)
            tiles.append(tile)
        result.append(jnp.concatenate(tiles, 1))
    return result


def body(
    feats_in, owner_in, place_in, nbr_in, w_in_in, w_mid_in, sel_in, ec_in, eh_in, cm_in,
    grid_out, point_out,
    feats, owner, place, nbr, w_in, w_mid, sel, ec, eh, cm, sem_in, index,
    send_a, recv_a, send_b, recv_b, x_one, c_one, h_send, h_recv, x_two, face_one, face_two, w_all, w_send_two, w_recv_two,
    w_one, w_two, lot_p, hi_p, lot_s, hi_s, pad_one, pad_two, ret_a, ret_v,
    sem_z, sem_j, sem_x, sem_p, sem_f, sem_g, sem_w, sem_ret,
):
    s = lax.axis_index("space")
    q = lax.axis_index("chan")
    core = s % 2
    z = (s // 2) % DEPTH
    row = s // (2 * DEPTH)
    plane = row * 2 + core
    spaces = 64

    def far_peer(d, e):
        other = (plane + e + PLANE) % PLANE
        return {"space": ((other // 2) * DEPTH + (z + d + DEPTH) % DEPTH) * 2 + other % 2, "chan": q}

    def x_peer(d):
        return {"space": s, "chan": (q + d) % CHAN}

    def s_peer(d):
        return {"space": (s + d + spaces) % spaces, "chan": q}

    started = []

    def send(src, dst, sems, at, peer):
        copy = pltpu.make_async_remote_copy(
            src_ref=src, dst_ref=dst, send_sem=sems.at[(0, *at)], recv_sem=sems.at[(1, *at)], device_id=peer, device_id_type=MESH
        )
        copy.start()
        started.append(copy)
        return copy

    fetches = [
        pltpu.make_async_copy(src, dst, sem_in.at[i])
        for i, (src, dst) in enumerate(
            (
                (owner_in, owner), (place_in, place), (feats_in, feats), (w_in_in, w_in), (w_mid_in, w_mid),
                (nbr_in, nbr), (sel_in, sel), (ec_in, ec), (eh_in, eh), (cm_in, cm),
            )
        )
    ]
    for copy in fetches:
        copy.start()
    peers = (
        [far_peer(0, e) for e in FAR_FIRST]
        + [far_peer(d, 0) for d in FAR_FIRST]
        + [s_peer(1), s_peer(-1)]
        + [x_peer(d) for d in range(1, CHAN)]
    )
    barrier = pltpu.get_barrier_semaphore()
    for peer in peers:
        pl.semaphore_signal(barrier, inc=1, device_id=peer, device_id_type=MESH)

    for copy in fetches[:3]:
        copy.wait()

    own = owner[...]
    where_to = place[...]
    match = jnp.where(lax.broadcasted_iota(jnp.int32, (64, 1024), 0) == own, 1.0, 0.0)
    tall = jnp.concatenate([match[:, 256 * i : 256 * i + 256] for i in range(4)], 0)
    before = jnp.where(
        lax.broadcasted_iota(jnp.int32, (256, 256), 0) < lax.broadcasted_iota(jnp.int32, (256, 256), 1), 1.0, 0.0
    )
    earlier = dot(tall.astype(BF16), before.astype(BF16))
    carry = jnp.zeros((64, 1), F32)
    ranks = []
    for i in range(4):
        mine = tall[64 * i : 64 * i + 64]
        ranks.append(jnp.sum(mine * (earlier[64 * i : 64 * i + 64] + carry), axis=0, keepdims=True))
        carry = carry + jnp.sum(mine, axis=1, keepdims=True)
    rank = jnp.concatenate(ranks, 1)
    to_z = ((own // 2) - z) & 7
    to_plane = ((own // (2 * DEPTH)) * 2 + (own & 1) - plane) & 7
    hi = (to_plane * 2 + to_z // 4).astype(F32)
    lo = ((to_z & 3) * CAP).astype(F32) + rank
    hot = one_hot(lo, 128)
    lot_p[...] = hot
    hi_p[...] = jnp.broadcast_to(hi, (8, 1024))
    extra = lax.broadcasted_iota(jnp.int32, (8, 1024), 0)
    extra = jnp.where(
        extra == 0, (where_to // 128).astype(F32), jnp.where(extra == 1, (where_to % 128).astype(F32), 0.0)
    )
    full = jnp.concatenate([feats[...].astype(F32), extra], 0)
    hi_wide = jnp.broadcast_to(hi, (24, 1024))
    spread = jnp.concatenate([jnp.where(hi_wide == float(h), full, 0.0).astype(BF16) for h in range(16)], 0)
    packed = dot_lanes(spread, hot)
    for h in range(16):
        send_a[h // 2, :, 128 * (h % 2) : 128 * (h % 2) + 128] = packed[24 * h : 24 * h + 24].astype(BF16)

    pl.semaphore_wait(barrier, len(peers))

    first = [send(send_a.at[e], recv_a.at[e], sem_j, (e,), far_peer(0, e)) for e in FAR_FIRST]
    for copy in fetches[3:]:
        copy.wait()

    lane = lax.broadcasted_iota(jnp.int32, (1, 128), 1)
    weight_moves = [send(w_in, w_all.at[d], sem_w, (0, d), x_peer(d)) for d in range(1, CHAN)]
    zero = jnp.zeros((24, 32), F32)
    for i in range(3):
        slabs = [jnp.concatenate([w_mid[9 * i + jl].astype(F32), zero], 1) for jl in range(TAPS)]
        for k in range(CHAN):
            tiles = []
            for group in (range(0, 5), range(5, 9)):
                tile = jnp.zeros((24, 128), F32)
                for u, jl in enumerate(group):
                    moved = pltpu.roll(slabs[jl], (24 * u - 24 * k) % 128, 1)
                    tile = jnp.where((lane >= 24 * u) & (lane < 24 * u + 24), moved, tile)
                tiles.append(tile)
            w_send_two[k, i] = jnp.concatenate(tiles, 1).astype(BF16)
    for d in range(1, CHAN):
        weight_moves.append(send(w_send_two.at[(q + d) % CHAN], w_recv_two.at[d], sem_w, (1, d), x_peer(d)))

    for copy in first:
        copy.wait_recv()
    parts = [send_a[0].astype(F32)] + [recv_a[e].astype(F32) for e in range(1, PLANE)]
    for d, part in enumerate(swap_groups(parts)):
        send_b[d] = part.astype(BF16)
    second = {d: send(send_b.at[d], recv_b.at[d], sem_z, (d,), far_peer(d, 0)) for d in FAR_FIRST}

    none = 36
    for b in range(BRICKS):
        for f in range(6):
            local = nbr[b, f] - BRICKS * s + BRICKS
            there = (nbr[b, f] >= 0) & (local >= 0) & (local < 3 * BRICKS)
            base = (local >> 2) * 12 + f // 2
            index[0, 6 * b + f] = jnp.where(there, base + 3 * (local & 3), none)
            index[1, 6 * b + f] = jnp.where(there, base + 3 * ((q - local) & 3), none)

    cells = jnp.zeros((256, 128), F32)
    for d in (0, 1, 7, 2, 6, 3, 5, 4):
        at = slice(256 * d, 256 * d + 256)
        if d:
            second[d].wait_recv()
        slots = (recv_b if d else send_b)[d].astype(F32)
        hi = slots[16:17]
        hot = one_hot(slots[17:18], 128)
        lot_s[:, at] = hot
        hi_s[:, at] = jnp.broadcast_to(hi, (8, 256))
        hi_wide = jnp.broadcast_to(hi, (16, 256))
        spread = [jnp.where(hi_wide == float(h), slots[0:16], 0.0).astype(BF16) for h in range(16)]
        cells = cells + dot_lanes(jnp.concatenate(spread, 0), hot)
    for h in range(16):
        x_one[h // 4, :, 128 * (h % 4) : 128 * (h % 4) + 128] = cells[16 * h : 16 * h + 16].astype(BF16)

    def rim(face, b, p, relative):
        low, high = (face[index[relative, 6 * b + f]].astype(F32) for f in (2 * p, 2 * p + 1))
        return jnp.where(lax.broadcasted_iota(jnp.int32, low.shape, 1) < 64, low, high)

    def tap_sum(full, count, row_of):
        total = None
        for jl in range(TAPS):
            term = full[row_of(jl) : row_of(jl) + count]
            term = jnp.concatenate([term[:, 128 * x : 128 * x + 128] for x in range(8)], 0)
            shift = 10 * (jl // 3) + jl % 3
            if shift:
                term = pltpu.roll(term, 128 - shift, 1)
            total = term if total is None else total + term
        return total

    def pack_planes(layer, count):
        return [
            jnp.concatenate(
                [layer[count * (2 * p) : count * (2 * p + 1)], layer[count * (2 * p + 1) : count * (2 * p + 2)]], 1
            )
            for p in range(4)
        ]

    rims = dot(jnp.concatenate([x_one[b] for b in range(BRICKS)], 0), sel[...])
    for b in range(BRICKS):
        for p in range(3):
            face_one[12 + 3 * b + p] = rims[16 * b : 16 * b + 16, 128 * p : 128 * p + 128].astype(BF16)
    face_one[none] = jnp.zeros((16, 128), BF16)
    face_two[none] = jnp.zeros((ALL, 128), BF16)
    beside = [
        send(face_one.at[12:24], face_one.at[24 * e : 24 * e + 12], sem_f, (3, e), s_peer(1 - 2 * e)) for e in (0, 1)
    ]
    centers = [send(x_one.at[(q + d) % CHAN], c_one.at[d], sem_x, (0, d), x_peer(d)) for d in (2, 1, 3)]
    for copy in weight_moves:
        copy.wait_recv()
    zero = jnp.zeros((192, 32), F32)
    for jl in range(TAPS):
        pieces = [(w_in if r == 0 else w_all.at[r])[9 * i + jl].astype(F32) for i in range(3) for r in range(CHAN)]
        tall = jnp.concatenate([jnp.concatenate(pieces, 0), zero], 1)
        w_one[ALL * jl : ALL * jl + ALL, 0:192] = tall.T[0:ALL].astype(BF16)
    w_recv_two[0] = w_send_two[q]
    pieces = [w_recv_two[(q - k + CHAN) % CHAN, i].astype(F32) for i in range(3) for k in range(CHAN)]
    turned = jnp.concatenate(pieces + [jnp.zeros((ALL, 256), F32)], 0).T[:ROWS]
    out_id = lax.broadcasted_iota(jnp.int32, (ROWS, 384), 0) - tap_row(4)
    in_id = lax.broadcasted_iota(jnp.int32, (ROWS, 384), 1) - 3 * ALL - OUT * q
    same = (out_id == in_id) & (out_id >= 0) & (out_id < OUT)
    w_two[...] = jnp.where(same, 1.0, turned).astype(BF16)

    for copy in beside:
        copy.wait_recv()
    for b in range(BRICKS):
        for p in range(3):
            h_send[b, p] = rim(face_one, b, p, 0).astype(BF16)
    halos = [send(h_send.at[(q + d) % CHAN], h_recv.at[d], sem_x, (1, d), x_peer(d)) for d in (2, 1, 3)]
    for copy in centers:
        copy.wait_recv()
    parts = [x_one[q].astype(F32)] + [c_one[r].astype(F32) for r in range(1, CHAN)]
    tiles = [part[:, 128 * p : 128 * p + 128] for part in parts for p in range(4)]
    inner = dot(jnp.concatenate(tiles, 0).astype(BF16), ec[...])
    for copy in halos:
        copy.wait_recv()
    edges = [jnp.concatenate([h_send[q, p]] + [h_recv[r, p] for r in range(1, CHAN)], 0) for p in range(3)]
    ends = dot(edges[0], ec[...]).astype(BF16)
    outer = dot(jnp.concatenate(edges[1:], 1), eh[...])
    pad_one[:, 0:128] = ends[:, 0:128]
    pad_one[:, 1152:1280] = ends[:, 128:256]
    for p in range(4):
        mid = jnp.concatenate([inner[(4 * r + p) * 16 : (4 * r + p + 1) * 16] for r in range(CHAN)], 0)
        pad_one[:, 128 + 256 * p : 384 + 256 * p] = (mid + outer[:, 256 * p : 256 * p + 256]).astype(BF16)
    deep = jnp.concatenate([pad_one[:, 128 * i : 128 * i + 1024] for i in range(3)], 0)
    layer = tap_sum(dot(w_one[:, 0:192], deep), ALL, lambda jl: ALL * jl)
    layer = jnp.maximum(layer, 0.0).astype(BF16).astype(F32)
    cells = dot(jnp.concatenate(pack_planes(layer, ALL), 0).astype(BF16), cm[...])
    for p in range(4):
        x_two[0, :, 128 * p : 128 * p + 128] = cells[ALL * p : ALL * p + ALL].astype(BF16)

    def piece(slot, t):
        return x_two.at[slot, 16 * t : 16 * t + 16]

    right, left = {}, {}
    for t in range(6):
        right[t] = send(piece(0, t), piece(1, t), sem_p, (0, t), x_peer(1))
        u = (t + 3) % 6
        left[u] = send(piece(0, u), piece(3, u), sem_p, (1, u), x_peer(3))
    face_moves = []

    def send_faces(r, at, sems, which):
        for e in (0, 1):
            src = face_two.at[12 + 3 * r : 15 + 3 * r, at]
            dst = face_two.at[24 * e + 3 * r : 24 * e + 3 * r + 3, at]
            face_moves.append(send(src, dst, sems, (*which, e), s_peer(1 - 2 * e)))

    def faces(r):
        rims = dot(x_two[r], sel[...])
        for p in range(3):
            face_two[12 + 3 * r + p] = rims[:, 128 * p : 128 * p + 128].astype(BF16)
        send_faces(r, slice(0, ALL), sem_f, (r if r < 2 else 2,))

    faces(0)
    relay = {}
    for t in range(3):
        right[t].wait_recv()
        relay[t] = send(piece(1, t), piece(2, t), sem_p, (2, t), x_peer(1))
        left[3 + t].wait_recv()
        relay[3 + t] = send(piece(3, 3 + t), piece(2, 3 + t), sem_p, (2, 3 + t), x_peer(3))
    for t in range(3, 6):
        right[t].wait_recv()
    faces(1)
    for t in range(3):
        left[t].wait_recv()
    faces(3)
    for t in range(3):
        relay[t].wait_recv()
        relay[3 + t].wait_recv()
        rows = [slice(16 * u, 16 * u + 16) for u in (t, 3 + t)]
        rims = dot(jnp.concatenate([x_two[2, at] for at in rows], 0), sel[...])
        for half, at in enumerate(rows):
            for p in range(3):
                face_two[18 + p, at] = rims[16 * half : 16 * half + 16, 128 * p : 128 * p + 128].astype(BF16)
            send_faces(2, at, sem_g, (t, half))
    bricks = [x_two[(q - b + CHAN) % CHAN] for b in range(BRICKS)]
    tiles = [brick[:, 128 * p : 128 * p + 128] for brick in bricks for p in range(4)]
    inner = dot(jnp.concatenate(tiles, 0), ec[...])
    for copy in face_moves:
        copy.wait_recv()
    edges = [
        jnp.concatenate([rim(face_two, b, p, 1).astype(BF16) for b in range(BRICKS)], 0) for p in range(3)
    ]
    ends = dot(edges[0], ec[...]).astype(BF16)
    outer = dot(jnp.concatenate(edges[1:], 1), eh[...])
    layers = []
    for b in range(BRICKS):
        pad_two[b, :, 0:128] = ends[ALL * b : ALL * b + ALL, 0:128]
        pad_two[b, :, 1152:1280] = ends[ALL * b : ALL * b + ALL, 128:256]
        for p in range(4):
            mid = inner[(4 * b + p) * ALL : (4 * b + p + 1) * ALL]
            mid = mid + outer[ALL * b : ALL * b + ALL, 256 * p : 256 * p + 256]
            pad_two[b, :, 128 + 256 * p : 384 + 256 * p] = mid.astype(BF16)
        deep = jnp.concatenate([pad_two[b, :, 128 * i : 128 * i + 1024] for i in (0, 1, 2, 1)], 0)
        layer = tap_sum(dot(w_two[...], deep), OUT, tap_row)
        layers += pack_planes(jnp.maximum(layer, 0.0), OUT)
    closed = dot(jnp.concatenate(layers, 0).astype(BF16), cm[...])
    cells = closed.astype(BF16)

    back = {}
    for d in [*FAR_FIRST, 0]:
        at = slice(256 * d, 256 * d + 256)
        found = dot(cells, lot_s[:, at])
        hi_wide = jnp.broadcast_to(hi_s[0:1, at], (OUT, 256))
        value = found[0:OUT]
        for h in range(1, 16):
            value = jnp.where(hi_wide == float(h), found[OUT * h : OUT * h + OUT], value)
        tiles = split_tiles(jnp.concatenate([value[:, 0:128], value[:, 128:256]], 0))
        for e in range(PLANE):
            (ret_a if d or e else ret_v)[DEPTH * e + d] = tiles[e].astype(BF16)
        for e in [*FAR_FIRST, 0]:
            if d or e:
                at = DEPTH * e + d
                back[at] = send(ret_a.at[at], ret_v.at[at], sem_ret, (at,), far_peer(-d, -e))
    for p in range(4):
        tiles = [closed[OUT * (4 * b + p) : OUT * (4 * b + p) + OUT] for b in range(BRICKS)]
        grid_out[:, :, 128 * p : 128 * p + 128] = jnp.stack(tiles, 1).astype(BF16)
    for copy in started:
        copy.wait_send()
    hi_wide = jnp.broadcast_to(hi_p[0:1], (OUT, 1024))
    value = jnp.zeros((OUT, 1024), F32)
    for near in ((0, 1, 7), (2, 6), (3, 5, 4)):
        ids = [DEPTH * e + d for e in near for d in range(DEPTH)]
        for at in ids:
            if at:
                back[at].wait_recv()
        lines = join_tiles([ret_v[at].astype(F32) for at in ids])
        found = dot(lines.astype(BF16), lot_p[...])
        for i, h in enumerate(2 * e + half for e in near for half in (0, 1)):
            value = jnp.where(hi_wide == float(h), found[OUT * i : OUT * i + OUT], value)
    point_out[...] = value.astype(BF16)


def deliver(grid, values, grid_out, point_out, sems):
    copies = [pltpu.make_async_copy(a, b, sems.at[i]) for i, (a, b) in enumerate(((grid, grid_out), (values, point_out)))]
    for copy in copies:
        copy.start()
    for copy in copies:
        copy.wait()


def per_device(point_feats, point_owner, point_place, neighbors, weight_in, weight_mid):
    anywhere = pl.BlockSpec(memory_space=pl.ANY)
    constants = [jnp.asarray(c(), BF16) for c in (face_picker, plane_spread, rim_spread, plane_pack)]
    points = point_feats.shape[1]
    grid, values = pl.pallas_call(
        body,
        out_shape=(
            pltpu.VMEM((OUT, BRICKS, CELLS), BF16),
            pltpu.VMEM((OUT, points), BF16),
        ),
        in_specs=[anywhere] * 10,
        out_specs=(pl.BlockSpec(memory_space=pltpu.VMEM), pl.BlockSpec(memory_space=pltpu.VMEM)),
        scratch_shapes=[
            pltpu.VMEM((16, points), BF16),
            pltpu.VMEM((1, points), jnp.int32),
            pltpu.VMEM((1, points), jnp.int32),
            pltpu.SMEM((4, 6), jnp.int32),
            pltpu.VMEM((27, 16, 96), BF16),
            pltpu.VMEM((27, 24, 96), BF16),
            *[pltpu.VMEM(c.shape, BF16) for c in constants],
            pltpu.SemaphoreType.DMA((10,)),
            pltpu.SMEM((2, 24), jnp.int32),
            pltpu.VMEM((8, 24, 256), BF16),
            pltpu.VMEM((8, 24, 256), BF16),
            pltpu.VMEM((8, 24, 256), BF16),
            pltpu.VMEM((8, 24, 256), BF16),
            pltpu.VMEM((4, 16, CELLS), BF16),
            pltpu.VMEM((4, 16, CELLS), BF16),
            pltpu.VMEM((4, 3, 16, 128), BF16),
            pltpu.VMEM((4, 3, 16, 128), BF16),
            pltpu.VMEM((4, ALL, CELLS), BF16),
            pltpu.VMEM((37, 16, 128), BF16),
            pltpu.VMEM((37, ALL, 128), BF16),
            pltpu.VMEM((4, 27, 16, 96), BF16),
            pltpu.VMEM((4, 3, 24, 256), BF16),
            pltpu.VMEM((4, 3, 24, 256), BF16),
            pltpu.VMEM((TAPS * ALL, 256), BF16),
            pltpu.VMEM((ROWS, 384), BF16),
            pltpu.VMEM((128, points), BF16),
            pltpu.VMEM((8, points), F32),
            pltpu.VMEM((128, VOX), BF16),
            pltpu.VMEM((8, VOX), F32),
            pltpu.VMEM((64, 1280), BF16),
            pltpu.VMEM((4, ALL, 1280), BF16),
            pltpu.VMEM((64, 8, 128), BF16),
            pltpu.VMEM((64, 8, 128), BF16),
            pltpu.SemaphoreType.DMA((2, 8)),
            pltpu.SemaphoreType.DMA((2, 8)),
            pltpu.SemaphoreType.DMA((2, 2, 4)),
            pltpu.SemaphoreType.DMA((2, 3, 6)),
            pltpu.SemaphoreType.DMA((2, 4, 2)),
            pltpu.SemaphoreType.DMA((2, 3, 2, 2)),
            pltpu.SemaphoreType.DMA((2, 2, 4)),
            pltpu.SemaphoreType.DMA((2, 64)),
        ],
        compiler_params=pltpu.CompilerParams(collective_id=0, has_side_effects=True),
    )(
        point_feats,
        point_owner.reshape(1, points),
        point_place.reshape(1, points),
        neighbors,
        jnp.transpose(weight_in, (1, 0, 2)),
        jnp.transpose(weight_mid, (1, 0, 2)),
        *constants,
    )
    grid, values = (pltpu.with_memory_space_constraint(a, pltpu.VMEM) for a in (grid, values))
    return pl.pallas_call(
        deliver,
        out_shape=(
            jax.ShapeDtypeStruct((OUT, BRICKS, CELLS), BF16),
            jax.ShapeDtypeStruct((OUT, points), BF16),
        ),
        in_specs=[pl.BlockSpec(memory_space=pltpu.VMEM)] * 2,
        out_specs=(anywhere, anywhere),
        scratch_shapes=[pltpu.SemaphoreType.DMA((2,))],
    )(grid, values)


def solution(mesh):
    return jax.shard_map(
        per_device,
        mesh=mesh,
        in_specs=(
            P("chan", "space"),
            P("space", None),
            P("space"),
            P("space", None),
            P("chan", None, None),
            P("chan", None, None),
        ),
        out_specs=(P("chan", "space", None), P("chan", "space")),
        check_vma=False,
    )
```

```python
import functools

import jax
import jax.numpy as jnp
import numpy as np
from jax import lax
from jax.experimental import pallas as pl
from jax.experimental.pallas import tpu as pltpu
from jax.sharding import PartitionSpec as P

DEPTH = 8
PLANE = 8
CHAN = 4
CAP = 32
CELLS = 512
BRICKS = 4
VOX = BRICKS * CELLS
OUT = 24
TAPS = 9
F32 = jnp.float32
BF16 = jnp.bfloat16
MESH = pl.DeviceIdType.MESH


def tap_row(jl):
    return OUT * jl + (8 if jl >= 5 else 0)


ROWS = 224
ALL = 96
FAR_FIRST = (4, 3, 5, 2, 6, 1, 7)


def face_picker():
    sel = np.zeros((CELLS, 384), np.float32)
    for u in range(8):
        for w in range(8):
            for p in range(3):
                for half, end in ((0, 7), (1, 0)):
                    x, y, z = ((end, u, w), (u, end, w), (u, w, end))[p]
                    sel[(8 * x + y) * 8 + z, 128 * p + 64 * half + 8 * u + w] = 1
    return sel


def plane_spread():
    ec = np.zeros((128, 256), np.float32)
    for x in range(2):
        for y in range(8):
            for z in range(8):
                ec[64 * x + 8 * y + z, 128 * x + 10 * (y + 1) + z + 1] = 1
    return ec


def rim_spread():
    eh = np.zeros((256, 1024), np.float32)
    for x in range(8):
        for w in range(8):
            eh[8 * x + w, 128 * x + w + 1] = 1
            eh[64 + 8 * x + w, 128 * x + 90 + w + 1] = 1
            eh[128 + 8 * x + w, 128 * x + 10 * (w + 1)] = 1
            eh[192 + 8 * x + w, 128 * x + 10 * (w + 1) + 9] = 1
    return eh


def plane_pack():
    cm = np.zeros((256, 128), np.float32)
    for x in range(2):
        for y in range(8):
            for z in range(8):
                cm[128 * x + 10 * y + z, 64 * x + 8 * y + z] = 1
    return cm


def dot(a, b):
    return jnp.dot(a, b, preferred_element_type=F32)


def dot_lanes(a, b):
    return lax.dot_general(a, b, (((1,), (1,)), ((), ())), preferred_element_type=F32)


def one_hot(row, count):
    ids = lax.broadcasted_iota(jnp.int32, (count, row.shape[1]), 0).astype(F32)
    return jnp.where(ids == row, 1.0, 0.0).astype(BF16)


def pick(choices):
    group = lax.broadcasted_iota(jnp.int32, (8, 128), 1) // 32
    result = choices[-1]
    for i in reversed(range(len(choices) - 1)):
        result = jnp.where(group == i, choices[i], result)
    return result


def split_tiles(tall):
    turned = [tall] + [pltpu.roll(tall, 32 * a, 1) for a in range(1, 4)]
    return [
        pick([turned[(m - u) % 4][24 * h + 8 * m : 24 * h + 8 * m + 8] for m in range(3)])
        for h in range(tall.shape[0] // 24)
        for u in range(4)
    ]


def join_tiles(tiles):
    tall = jnp.concatenate(tiles, 0)
    turned = [tall] + [pltpu.roll(tall, 32 * a, 1) for a in range(1, 4)]
    return jnp.concatenate(
        [
            pick([turned[(u - m) % 4][8 * (4 * h + u) : 8 * (4 * h + u) + 8] for u in range(4)])
            for h in range(len(tiles) // 4)
            for m in range(3)
        ],
        0,
    )


def swap_groups(parts):
    rows = parts[0].shape[0]
    tall = jnp.concatenate([p[:, 128 * m : 128 * m + 128] for p in parts for m in range(2)], 0)
    turned = [tall] + [pltpu.roll(tall, 32 * a, 1) for a in range(1, 4)]
    group = lax.broadcasted_iota(jnp.int32, (rows, 128), 1) // 32
    result = []
    for j in range(8):
        m, g = j // 4, j % 4
        tiles = []
        for t in range(2):
            tile = None
            for u in range(4):
                at = (2 * (4 * t + u) + m) * rows
                piece = turned[(u - g) % 4][at : at + rows]
                tile = piece if tile is None else jnp.where(group == u, piece, tile)
            tiles.append(tile)
        result.append(jnp.concatenate(tiles, 1))
    return result


def body(
    feats_in, owner_in, place_in, nbr_in, w_in_in, w_mid_in, sel_in, ec_in, eh_in, cm_in,
    grid_out, point_out,
    feats, owner, place, nbr, w_in, w_mid, sel, ec, eh, cm, sem_in, index,
    send_a, recv_a, send_b, recv_b, x_one, c_one, h_send, h_recv, x_two, face_one, face_two, w_all, w_send_two, w_recv_two,
    w_one, w_two, lot_p, hi_p, lot_s, hi_s, pad_one, pad_two, ret_a, ret_v,
    sem_z, sem_j, sem_x, sem_p, sem_f, sem_g, sem_w, sem_ret,
):
    s = lax.axis_index("space")
    q = lax.axis_index("chan")
    core = s % 2
    z = (s // 2) % DEPTH
    row = s // (2 * DEPTH)
    plane = row * 2 + core
    spaces = 64

    def far_peer(d, e):
        other = (plane + e + PLANE) % PLANE
        return {"space": ((other // 2) * DEPTH + (z + d + DEPTH) % DEPTH) * 2 + other % 2, "chan": q}

    def x_peer(d):
        return {"space": s, "chan": (q + d) % CHAN}

    def s_peer(d):
        return {"space": (s + d + spaces) % spaces, "chan": q}

    started = []

    def send(src, dst, sems, at, peer):
        copy = pltpu.make_async_remote_copy(
            src_ref=src, dst_ref=dst, send_sem=sems.at[(0, *at)], recv_sem=sems.at[(1, *at)], device_id=peer, device_id_type=MESH
        )
        copy.start()
        started.append(copy)
        return copy

    fetches = [
        pltpu.make_async_copy(src, dst, sem_in.at[i])
        for i, (src, dst) in enumerate(
            (
                (owner_in, owner), (place_in, place), (feats_in, feats), (w_in_in, w_in), (w_mid_in, w_mid),
                (nbr_in, nbr), (sel_in, sel), (ec_in, ec), (eh_in, eh), (cm_in, cm),
            )
        )
    ]
    for copy in fetches:
        copy.start()
    peers = (
        [far_peer(0, e) for e in FAR_FIRST]
        + [far_peer(d, 0) for d in FAR_FIRST]
        + [s_peer(1), s_peer(-1)]
        + [x_peer(d) for d in range(1, CHAN)]
    )
    barrier = pltpu.get_barrier_semaphore()
    for peer in peers:
        pl.semaphore_signal(barrier, inc=1, device_id=peer, device_id_type=MESH)

    for copy in fetches[:3]:
        copy.wait()

    own = owner[...]
    where_to = place[...]
    match = jnp.where(lax.broadcasted_iota(jnp.int32, (64, 1024), 0) == own, 1.0, 0.0)
    tall = jnp.concatenate([match[:, 256 * i : 256 * i + 256] for i in range(4)], 0)
    before = jnp.where(
        lax.broadcasted_iota(jnp.int32, (256, 256), 0) < lax.broadcasted_iota(jnp.int32, (256, 256), 1), 1.0, 0.0
    )
    earlier = dot(tall.astype(BF16), before.astype(BF16))
    carry = jnp.zeros((64, 1), F32)
    ranks = []
    for i in range(4):
        mine = tall[64 * i : 64 * i + 64]
        ranks.append(jnp.sum(mine * (earlier[64 * i : 64 * i + 64] + carry), axis=0, keepdims=True))
        carry = carry + jnp.sum(mine, axis=1, keepdims=True)
    rank = jnp.concatenate(ranks, 1)
    to_z = ((own // 2) - z) & 7
    to_plane = ((own // (2 * DEPTH)) * 2 + (own & 1) - plane) & 7
    hi = (to_plane * 2 + to_z // 4).astype(F32)
    lo = ((to_z & 3) * CAP).astype(F32) + rank
    hot = one_hot(lo, 128)
    lot_p[...] = hot
    hi_p[...] = jnp.broadcast_to(hi, (8, 1024))
    extra = lax.broadcasted_iota(jnp.int32, (8, 1024), 0)
    extra = jnp.where(
        extra == 0, (where_to // 128).astype(F32), jnp.where(extra == 1, (where_to % 128).astype(F32), 0.0)
    )
    full = jnp.concatenate([feats[...].astype(F32), extra], 0)
    hi_wide = jnp.broadcast_to(hi, (24, 1024))
    spread = jnp.concatenate([jnp.where(hi_wide == float(h), full, 0.0).astype(BF16) for h in range(16)], 0)
    packed = dot_lanes(spread, hot)
    for h in range(16):
        send_a[h // 2, :, 128 * (h % 2) : 128 * (h % 2) + 128] = packed[24 * h : 24 * h + 24].astype(BF16)

    pl.semaphore_wait(barrier, len(peers))

    first = [send(send_a.at[e], recv_a.at[e], sem_j, (e,), far_peer(0, e)) for e in FAR_FIRST]
    for copy in fetches[3:]:
        copy.wait()

    lane = lax.broadcasted_iota(jnp.int32, (1, 128), 1)
    weight_moves = [send(w_in, w_all.at[d], sem_w, (0, d), x_peer(d)) for d in range(1, CHAN)]
    zero = jnp.zeros((24, 32), F32)
    for i in range(3):
        slabs = [jnp.concatenate([w_mid[9 * i + jl].astype(F32), zero], 1) for jl in range(TAPS)]
        for k in range(CHAN):
            tiles = []
            for group in (range(0, 5), range(5, 9)):
                tile = jnp.zeros((24, 128), F32)
                for u, jl in enumerate(group):
                    moved = pltpu.roll(slabs[jl], (24 * u - 24 * k) % 128, 1)
                    tile = jnp.where((lane >= 24 * u) & (lane < 24 * u + 24), moved, tile)
                tiles.append(tile)
            w_send_two[k, i] = jnp.concatenate(tiles, 1).astype(BF16)
    for d in range(1, CHAN):
        weight_moves.append(send(w_send_two.at[(q + d) % CHAN], w_recv_two.at[d], sem_w, (1, d), x_peer(d)))

    for copy in first:
        copy.wait_recv()
    parts = [send_a[0].astype(F32)] + [recv_a[e].astype(F32) for e in range(1, PLANE)]
    for d, part in enumerate(swap_groups(parts)):
        send_b[d] = part.astype(BF16)
    second = {d: send(send_b.at[d], recv_b.at[d], sem_z, (d,), far_peer(d, 0)) for d in FAR_FIRST}

    none = 36
    for b in range(BRICKS):
        for f in range(6):
            local = nbr[b, f] - BRICKS * s + BRICKS
            there = (nbr[b, f] >= 0) & (local >= 0) & (local < 3 * BRICKS)
            base = (local >> 2) * 12 + f // 2
            index[0, 6 * b + f] = jnp.where(there, base + 3 * (local & 3), none)
            index[1, 6 * b + f] = jnp.where(there, base + 3 * ((q - local) & 3), none)

    cells = jnp.zeros((256, 128), F32)
    for d in (0, 1, 7, 2, 6, 3, 5, 4):
        at = slice(256 * d, 256 * d + 256)
        if d:
            second[d].wait_recv()
        slots = (recv_b if d else send_b)[d].astype(F32)
        hi = slots[16:17]
        hot = one_hot(slots[17:18], 128)
        lot_s[:, at] = hot
        hi_s[:, at] = jnp.broadcast_to(hi, (8, 256))
        hi_wide = jnp.broadcast_to(hi, (16, 256))
        spread = [jnp.where(hi_wide == float(h), slots[0:16], 0.0).astype(BF16) for h in range(16)]
        cells = cells + dot_lanes(jnp.concatenate(spread, 0), hot)
    for h in range(16):
        x_one[h // 4, :, 128 * (h % 4) : 128 * (h % 4) + 128] = cells[16 * h : 16 * h + 16].astype(BF16)

    def rim(face, b, p, relative):
        low, high = (face[index[relative, 6 * b + f]].astype(F32) for f in (2 * p, 2 * p + 1))
        return jnp.where(lax.broadcasted_iota(jnp.int32, low.shape, 1) < 64, low, high)

    def tap_sum(full, count, taps):
        total = None
        for at, shift in taps:
            term = full[at : at + count]
            term = jnp.concatenate([term[:, 128 * x : 128 * x + 128] for x in range(8)], 0)
            if shift:
                term = pltpu.roll(term, 128 - shift, 1)
            total = term if total is None else total + term
        return total

    def pack_planes(layer, count):
        return [
            jnp.concatenate(
                [layer[count * (2 * p) : count * (2 * p + 1)], layer[count * (2 * p + 1) : count * (2 * p + 2)]], 1
            )
            for p in range(4)
        ]

    rims = dot(jnp.concatenate([x_one[b] for b in range(BRICKS)], 0), sel[...])
    for b in range(BRICKS):
        for p in range(3):
            face_one[12 + 3 * b + p] = rims[16 * b : 16 * b + 16, 128 * p : 128 * p + 128].astype(BF16)
    face_one[none] = jnp.zeros((16, 128), BF16)
    face_two[none] = jnp.zeros((ALL, 128), BF16)
    beside = [
        send(face_one.at[12:24], face_one.at[24 * e : 24 * e + 12], sem_f, (3, e), s_peer(1 - 2 * e)) for e in (0, 1)
    ]
    centers = [send(x_one.at[(q + d) % CHAN], c_one.at[d], sem_x, (0, d), x_peer(d)) for d in (2, 1, 3)]
    for copy in weight_moves:
        copy.wait_recv()
    zero = jnp.zeros((9 * 64, 32), F32)
    for l in range(3):
        pieces = [(w_in if r == 0 else w_all.at[r])[3 * ij + l].astype(F32) for ij in range(9) for r in range(CHAN)]
        tall = jnp.concatenate([jnp.concatenate(pieces, 0), zero], 1)
        w_one[ALL * l : ALL * l + ALL, 0 : 9 * 64] = tall.T[0:ALL].astype(BF16)
    w_recv_two[0] = w_send_two[q]
    pieces = [w_recv_two[(q - k + CHAN) % CHAN, i].astype(F32) for i in range(3) for k in range(CHAN)]
    turned = jnp.concatenate(pieces + [jnp.zeros((ALL, 256), F32)], 0).T[:ROWS]
    out_id = lax.broadcasted_iota(jnp.int32, (ROWS, 384), 0) - tap_row(4)
    in_id = lax.broadcasted_iota(jnp.int32, (ROWS, 384), 1) - 3 * ALL - OUT * q
    same = (out_id == in_id) & (out_id >= 0) & (out_id < OUT)
    w_two[...] = jnp.where(same, 1.0, turned).astype(BF16)

    for copy in beside:
        copy.wait_recv()
    for b in range(BRICKS):
        for p in range(3):
            h_send[b, p] = rim(face_one, b, p, 0).astype(BF16)
    halos = [send(h_send.at[(q + d) % CHAN], h_recv.at[d], sem_x, (1, d), x_peer(d)) for d in (2, 1, 3)]
    for copy in centers:
        copy.wait_recv()
    parts = [x_one[q].astype(F32)] + [c_one[r].astype(F32) for r in range(1, CHAN)]
    tiles = [part[:, 128 * p : 128 * p + 128] for part in parts for p in range(4)]
    inner = dot(jnp.concatenate(tiles, 0).astype(BF16), ec[...])
    for copy in halos:
        copy.wait_recv()
    edges = [jnp.concatenate([h_send[q, p]] + [h_recv[r, p] for r in range(1, CHAN)], 0) for p in range(3)]
    ends = dot(edges[0], ec[...]).astype(BF16)
    outer = dot(jnp.concatenate(edges[1:], 1), eh[...])
    planes = [ends[:, 0:128]]
    for p in range(4):
        mid = jnp.concatenate([inner[(4 * r + p) * 16 : (4 * r + p + 1) * 16] for r in range(CHAN)], 0)
        mid = (mid + outer[:, 256 * p : 256 * p + 256]).astype(BF16)
        planes += [mid[:, 0:128], mid[:, 128:256]]
    planes.append(ends[:, 128:256])
    for x, part in enumerate(planes):
        for j in range(3):
            pad_one[j, :, 128 * x : 128 * x + 128] = pltpu.roll(part, 128 - 10 * j, 1) if j else part
    deep = jnp.concatenate([pad_one[j, :, 128 * i : 128 * i + 1024] for i in range(3) for j in range(3)], 0)
    layer = tap_sum(dot(w_one[:, 0 : 9 * 64], deep), ALL, [(ALL * l, l) for l in range(3)])
    layer = jnp.maximum(layer, 0.0).astype(BF16).astype(F32)
    cells = dot(jnp.concatenate(pack_planes(layer, ALL), 0).astype(BF16), cm[...])
    for p in range(4):
        x_two[0, :, 128 * p : 128 * p + 128] = cells[ALL * p : ALL * p + ALL].astype(BF16)

    def piece(slot, t):
        return x_two.at[slot, 16 * t : 16 * t + 16]

    right, left = {}, {}
    for t in range(6):
        right[t] = send(piece(0, t), piece(1, t), sem_p, (0, t), x_peer(1))
        u = (t + 3) % 6
        left[u] = send(piece(0, u), piece(3, u), sem_p, (1, u), x_peer(3))
    face_moves = []

    def send_faces(r, at, sems, which):
        for e in (0, 1):
            src = face_two.at[12 + 3 * r : 15 + 3 * r, at]
            dst = face_two.at[24 * e + 3 * r : 24 * e + 3 * r + 3, at]
            face_moves.append(send(src, dst, sems, (*which, e), s_peer(1 - 2 * e)))

    def faces(r):
        rims = dot(x_two[r], sel[...])
        for p in range(3):
            face_two[12 + 3 * r + p] = rims[:, 128 * p : 128 * p + 128].astype(BF16)
        send_faces(r, slice(0, ALL), sem_f, (r if r < 2 else 2,))

    faces(0)
    relay = {}
    for t in range(3):
        right[t].wait_recv()
        relay[t] = send(piece(1, t), piece(2, t), sem_p, (2, t), x_peer(1))
        left[3 + t].wait_recv()
        relay[3 + t] = send(piece(3, 3 + t), piece(2, 3 + t), sem_p, (2, 3 + t), x_peer(3))
    for t in range(3, 6):
        right[t].wait_recv()
    faces(1)
    for t in range(3):
        left[t].wait_recv()
    faces(3)
    for t in range(3):
        relay[t].wait_recv()
        relay[3 + t].wait_recv()
        rows = [slice(16 * u, 16 * u + 16) for u in (t, 3 + t)]
        rims = dot(jnp.concatenate([x_two[2, at] for at in rows], 0), sel[...])
        for half, at in enumerate(rows):
            for p in range(3):
                face_two[18 + p, at] = rims[16 * half : 16 * half + 16, 128 * p : 128 * p + 128].astype(BF16)
            send_faces(2, at, sem_g, (t, half))
    bricks = [x_two[(q - b + CHAN) % CHAN] for b in range(BRICKS)]
    tiles = [brick[:, 128 * p : 128 * p + 128] for brick in bricks for p in range(4)]
    inner = dot(jnp.concatenate(tiles, 0), ec[...])
    for copy in face_moves:
        copy.wait_recv()
    edges = [
        jnp.concatenate([rim(face_two, b, p, 1).astype(BF16) for b in range(BRICKS)], 0) for p in range(3)
    ]
    ends = dot(edges[0], ec[...]).astype(BF16)
    outer = dot(jnp.concatenate(edges[1:], 1), eh[...])
    layers = []
    for b in range(BRICKS):
        pad_two[b, :, 0:128] = ends[ALL * b : ALL * b + ALL, 0:128]
        pad_two[b, :, 1152:1280] = ends[ALL * b : ALL * b + ALL, 128:256]
        for p in range(4):
            mid = inner[(4 * b + p) * ALL : (4 * b + p + 1) * ALL]
            mid = mid + outer[ALL * b : ALL * b + ALL, 256 * p : 256 * p + 256]
            pad_two[b, :, 128 + 256 * p : 384 + 256 * p] = mid.astype(BF16)
        deep = jnp.concatenate([pad_two[b, :, 128 * i : 128 * i + 1024] for i in (0, 1, 2, 1)], 0)
        layer = tap_sum(dot(w_two[...], deep), OUT, [(tap_row(jl), 10 * (jl // 3) + jl % 3) for jl in range(TAPS)])
        layers += pack_planes(jnp.maximum(layer, 0.0), OUT)
    closed = dot(jnp.concatenate(layers, 0).astype(BF16), cm[...])
    cells = closed.astype(BF16)

    back = {}
    for d in [*FAR_FIRST, 0]:
        at = slice(256 * d, 256 * d + 256)
        found = dot(cells, lot_s[:, at])
        hi_wide = jnp.broadcast_to(hi_s[0:1, at], (OUT, 256))
        value = found[0:OUT]
        for h in range(1, 16):
            value = jnp.where(hi_wide == float(h), found[OUT * h : OUT * h + OUT], value)
        tiles = split_tiles(jnp.concatenate([value[:, 0:128], value[:, 128:256]], 0))
        for e in range(PLANE):
            (ret_a if d or e else ret_v)[DEPTH * e + d] = tiles[e].astype(BF16)
        for e in [*FAR_FIRST, 0]:
            if d or e:
                at = DEPTH * e + d
                back[at] = send(ret_a.at[at], ret_v.at[at], sem_ret, (at,), far_peer(-d, -e))
    for p in range(4):
        tiles = [closed[OUT * (4 * b + p) : OUT * (4 * b + p) + OUT] for b in range(BRICKS)]
        grid_out[:, :, 128 * p : 128 * p + 128] = jnp.stack(tiles, 1).astype(BF16)
    for copy in started:
        copy.wait_send()
    hi_wide = jnp.broadcast_to(hi_p[0:1], (OUT, 1024))
    value = jnp.zeros((OUT, 1024), F32)
    for near in ((0, 1, 7), (2, 6), (3, 5, 4)):
        ids = [DEPTH * e + d for e in near for d in range(DEPTH)]
        for at in ids:
            if at:
                back[at].wait_recv()
        lines = join_tiles([ret_v[at].astype(F32) for at in ids])
        found = dot(lines.astype(BF16), lot_p[...])
        for i, h in enumerate(2 * e + half for e in near for half in (0, 1)):
            value = jnp.where(hi_wide == float(h), found[OUT * i : OUT * i + OUT], value)
    point_out[...] = value.astype(BF16)


def deliver(grid, values, grid_out, point_out, sems):
    copies = [pltpu.make_async_copy(a, b, sems.at[i]) for i, (a, b) in enumerate(((grid, grid_out), (values, point_out)))]
    for copy in copies:
        copy.start()
    for copy in copies:
        copy.wait()


def per_device(point_feats, point_owner, point_place, neighbors, weight_in, weight_mid):
    anywhere = pl.BlockSpec(memory_space=pl.ANY)
    constants = [jnp.asarray(c(), BF16) for c in (face_picker, plane_spread, rim_spread, plane_pack)]
    points = point_feats.shape[1]
    grid, values = pl.pallas_call(
        body,
        out_shape=(
            pltpu.VMEM((OUT, BRICKS, CELLS), BF16),
            pltpu.VMEM((OUT, points), BF16),
        ),
        in_specs=[anywhere] * 10,
        out_specs=(pl.BlockSpec(memory_space=pltpu.VMEM), pl.BlockSpec(memory_space=pltpu.VMEM)),
        scratch_shapes=[
            pltpu.VMEM((16, points), BF16),
            pltpu.VMEM((1, points), jnp.int32),
            pltpu.VMEM((1, points), jnp.int32),
            pltpu.SMEM((4, 6), jnp.int32),
            pltpu.VMEM((27, 16, 96), BF16),
            pltpu.VMEM((27, 24, 96), BF16),
            *[pltpu.VMEM(c.shape, BF16) for c in constants],
            pltpu.SemaphoreType.DMA((10,)),
            pltpu.SMEM((2, 24), jnp.int32),
            pltpu.VMEM((8, 24, 256), BF16),
            pltpu.VMEM((8, 24, 256), BF16),
            pltpu.VMEM((8, 24, 256), BF16),
            pltpu.VMEM((8, 24, 256), BF16),
            pltpu.VMEM((4, 16, CELLS), BF16),
            pltpu.VMEM((4, 16, CELLS), BF16),
            pltpu.VMEM((4, 3, 16, 128), BF16),
            pltpu.VMEM((4, 3, 16, 128), BF16),
            pltpu.VMEM((4, ALL, CELLS), BF16),
            pltpu.VMEM((37, 16, 128), BF16),
            pltpu.VMEM((37, ALL, 128), BF16),
            pltpu.VMEM((4, 27, 16, 96), BF16),
            pltpu.VMEM((4, 3, 24, 256), BF16),
            pltpu.VMEM((4, 3, 24, 256), BF16),
            pltpu.VMEM((3 * ALL, 640), BF16),
            pltpu.VMEM((ROWS, 384), BF16),
            pltpu.VMEM((128, points), BF16),
            pltpu.VMEM((8, points), F32),
            pltpu.VMEM((128, VOX), BF16),
            pltpu.VMEM((8, VOX), F32),
            pltpu.VMEM((3, 64, 1280), BF16),
            pltpu.VMEM((4, ALL, 1280), BF16),
            pltpu.VMEM((64, 8, 128), BF16),
            pltpu.VMEM((64, 8, 128), BF16),
            pltpu.SemaphoreType.DMA((2, 8)),
            pltpu.SemaphoreType.DMA((2, 8)),
            pltpu.SemaphoreType.DMA((2, 2, 4)),
            pltpu.SemaphoreType.DMA((2, 3, 6)),
            pltpu.SemaphoreType.DMA((2, 4, 2)),
            pltpu.SemaphoreType.DMA((2, 3, 2, 2)),
            pltpu.SemaphoreType.DMA((2, 2, 4)),
            pltpu.SemaphoreType.DMA((2, 64)),
        ],
        compiler_params=pltpu.CompilerParams(collective_id=0, has_side_effects=True),
    )(
        point_feats,
        point_owner.reshape(1, points),
        point_place.reshape(1, points),
        neighbors,
        jnp.transpose(weight_in, (1, 0, 2)),
        jnp.transpose(weight_mid, (1, 0, 2)),
        *constants,
    )
    grid, values = (pltpu.with_memory_space_constraint(a, pltpu.VMEM) for a in (grid, values))
    return pl.pallas_call(
        deliver,
        out_shape=(
            jax.ShapeDtypeStruct((OUT, BRICKS, CELLS), BF16),
            jax.ShapeDtypeStruct((OUT, points), BF16),
        ),
        in_specs=[pl.BlockSpec(memory_space=pltpu.VMEM)] * 2,
        out_specs=(anywhere, anywhere),
        scratch_shapes=[pltpu.SemaphoreType.DMA((2,))],
    )(grid, values)


def solution(mesh):
    return jax.shard_map(
        per_device,
        mesh=mesh,
        in_specs=(
            P("chan", "space"),
            P("space", None),
            P("space"),
            P("space", None),
            P("chan", None, None),
            P("chan", None, None),
        ),
        out_specs=(P("chan", "space", None), P("chan", "space")),
        check_vma=False,
    )
```

```python
import functools

import jax
import jax.numpy as jnp
import numpy as np
from jax import lax
from jax.experimental import pallas as pl
from jax.experimental.pallas import tpu as pltpu
from jax.sharding import PartitionSpec as P

DEPTH = 8
PLANE = 8
CHAN = 4
CAP = 32
CELLS = 512
BRICKS = 4
VOX = BRICKS * CELLS
OUT = 24
TAPS = 9
F32 = jnp.float32
BF16 = jnp.bfloat16
MESH = pl.DeviceIdType.MESH


def tap_row(jl):
    return OUT * jl + (8 if jl >= 5 else 0)


ROWS = 224
ALL = 96
FAR_FIRST = (4, 3, 5, 2, 6, 1, 7)


def face_picker():
    sel = np.zeros((CELLS, 384), np.float32)
    for u in range(8):
        for w in range(8):
            for p in range(3):
                for half, end in ((0, 7), (1, 0)):
                    x, y, z = ((end, u, w), (u, end, w), (u, w, end))[p]
                    sel[(8 * x + y) * 8 + z, 128 * p + 64 * half + 8 * u + w] = 1
    return sel


def plane_spread():
    ec = np.zeros((128, 256), np.float32)
    for x in range(2):
        for y in range(8):
            for z in range(8):
                ec[64 * x + 8 * y + z, 128 * x + 10 * (y + 1) + z + 1] = 1
    return ec


def rim_spread():
    eh = np.zeros((256, 1024), np.float32)
    for x in range(8):
        for w in range(8):
            eh[8 * x + w, 128 * x + w + 1] = 1
            eh[64 + 8 * x + w, 128 * x + 90 + w + 1] = 1
            eh[128 + 8 * x + w, 128 * x + 10 * (w + 1)] = 1
            eh[192 + 8 * x + w, 128 * x + 10 * (w + 1) + 9] = 1
    return eh


def plane_pack():
    cm = np.zeros((256, 128), np.float32)
    for x in range(2):
        for y in range(8):
            for z in range(8):
                cm[128 * x + 10 * y + z, 64 * x + 8 * y + z] = 1
    return cm


def dot(a, b):
    return jnp.dot(a, b, preferred_element_type=F32)


def dot_lanes(a, b):
    return lax.dot_general(a, b, (((1,), (1,)), ((), ())), preferred_element_type=F32)


def one_hot(row, count):
    ids = lax.broadcasted_iota(jnp.int32, (count, row.shape[1]), 0).astype(F32)
    return jnp.where(ids == row, 1.0, 0.0).astype(BF16)


def pick(choices):
    group = lax.broadcasted_iota(jnp.int32, (8, 128), 1) // 32
    result = choices[-1]
    for i in reversed(range(len(choices) - 1)):
        result = jnp.where(group == i, choices[i], result)
    return result


def split_tiles(tall):
    turned = [tall] + [pltpu.roll(tall, 32 * a, 1) for a in range(1, 4)]
    return [
        pick([turned[(m - u) % 4][24 * h + 8 * m : 24 * h + 8 * m + 8] for m in range(3)])
        for h in range(tall.shape[0] // 24)
        for u in range(4)
    ]


def join_tiles(tiles):
    tall = jnp.concatenate(tiles, 0)
    turned = [tall] + [pltpu.roll(tall, 32 * a, 1) for a in range(1, 4)]
    return jnp.concatenate(
        [
            pick([turned[(u - m) % 4][8 * (4 * h + u) : 8 * (4 * h + u) + 8] for u in range(4)])
            for h in range(len(tiles) // 4)
            for m in range(3)
        ],
        0,
    )


def swap_groups(parts):
    rows = parts[0].shape[0]
    tall = jnp.concatenate([p[:, 128 * m : 128 * m + 128] for p in parts for m in range(2)], 0)
    turned = [tall] + [pltpu.roll(tall, 32 * a, 1) for a in range(1, 4)]
    group = lax.broadcasted_iota(jnp.int32, (rows, 128), 1) // 32
    result = []
    for j in range(8):
        m, g = j // 4, j % 4
        tiles = []
        for t in range(2):
            tile = None
            for u in range(4):
                at = (2 * (4 * t + u) + m) * rows
                piece = turned[(u - g) % 4][at : at + rows]
                tile = piece if tile is None else jnp.where(group == u, piece, tile)
            tiles.append(tile)
        result.append(jnp.concatenate(tiles, 1))
    return result


def body(
    feats_in, owner_in, place_in, nbr_in, w_in_in, w_mid_in, sel_in, ec_in, eh_in, cm_in,
    grid_out, point_out,
    feats, owner, place, nbr, w_in, w_mid, sel, ec, eh, cm, sem_in, index,
    send_a, recv_a, send_b, recv_b, x_one, c_one, h_send, h_recv, x_two, face_one, face_two, w_all, w_send_two, w_recv_two,
    w_one, w_two, lot_p, hi_p, lot_s, hi_s, pad_one, pad_two, ret_a, ret_v, taken,
    sent, got, got_z, got_p, got_ret,
):
    s = lax.axis_index("space")
    q = lax.axis_index("chan")
    core = s % 2
    z = (s // 2) % DEPTH
    row = s // (2 * DEPTH)
    plane = row * 2 + core
    spaces = 64

    def far_peer(d, e):
        other = (plane + e + PLANE) % PLANE
        return {"space": ((other // 2) * DEPTH + (z + d + DEPTH) % DEPTH) * 2 + other % 2, "chan": q}

    def x_peer(d):
        return {"space": s, "chan": (q + d) % CHAN}

    def s_peer(d):
        return {"space": (s + d + spaces) % spaces, "chan": q}

    def send(src, dst, sent, got, peer):
        copy = pltpu.make_async_remote_copy(
            src_ref=src, dst_ref=dst, send_sem=sent, recv_sem=got, device_id=peer, device_id_type=MESH
        )
        copy.start()
        return copy

    def drain(ref, sem):
        pltpu.make_async_copy(ref, ref, sem).wait()

    fetches = [
        pltpu.make_async_copy(src, dst, sem_in.at[i])
        for i, (src, dst) in enumerate(
            (
                (owner_in, owner), (place_in, place), (feats_in, feats), (w_in_in, w_in), (w_mid_in, w_mid),
                (nbr_in, nbr), (sel_in, sel), (ec_in, ec), (eh_in, eh), (cm_in, cm),
            )
        )
    ]
    for copy in fetches:
        copy.start()
    peers = (
        [far_peer(0, e) for e in FAR_FIRST]
        + [far_peer(d, 0) for d in FAR_FIRST]
        + [s_peer(1), s_peer(-1)]
        + [x_peer(d) for d in range(1, CHAN)]
    )
    barrier = pltpu.get_barrier_semaphore()
    for peer in peers:
        pl.semaphore_signal(barrier, inc=1, device_id=peer, device_id_type=MESH)

    for copy in fetches[:3]:
        copy.wait()

    own = owner[...]
    where_to = place[...]
    match = jnp.where(lax.broadcasted_iota(jnp.int32, (64, 1024), 0) == own, 1.0, 0.0)
    tall = jnp.concatenate([match[:, 256 * i : 256 * i + 256] for i in range(4)], 0)
    before = jnp.where(
        lax.broadcasted_iota(jnp.int32, (256, 256), 0) < lax.broadcasted_iota(jnp.int32, (256, 256), 1), 1.0, 0.0
    )
    earlier = dot(tall.astype(BF16), before.astype(BF16))
    carry = jnp.zeros((64, 1), F32)
    ranks = []
    for i in range(4):
        mine = tall[64 * i : 64 * i + 64]
        ranks.append(jnp.sum(mine * (earlier[64 * i : 64 * i + 64] + carry), axis=0, keepdims=True))
        carry = carry + jnp.sum(mine, axis=1, keepdims=True)
    rank = jnp.concatenate(ranks, 1)
    to_z = ((own // 2) - z) & 7
    to_plane = ((own // (2 * DEPTH)) * 2 + (own & 1) - plane) & 7
    hi = (to_plane * 2 + to_z // 4).astype(F32)
    lo = ((to_z & 3) * CAP).astype(F32) + rank
    hot = one_hot(lo, 128)
    lot_p[...] = hot
    hi_p[...] = jnp.broadcast_to(hi, (8, 1024))
    extra = lax.broadcasted_iota(jnp.int32, (8, 1024), 0)
    extra = jnp.where(
        extra == 0, (where_to // 128).astype(F32), jnp.where(extra == 1, (where_to % 128).astype(F32), 0.0)
    )
    full = jnp.concatenate([feats[...].astype(F32), extra], 0)
    hi_wide = jnp.broadcast_to(hi, (24, 1024))
    spread = jnp.concatenate([jnp.where(hi_wide == float(h), full, 0.0).astype(BF16) for h in range(16)], 0)
    packed = dot_lanes(spread, hot)
    for h in range(16):
        send_a[h // 2, :, 128 * (h % 2) : 128 * (h % 2) + 128] = packed[24 * h : 24 * h + 24].astype(BF16)

    pl.semaphore_wait(barrier, len(peers))

    for e in FAR_FIRST:
        send(send_a.at[e], recv_a.at[e], sent.at[0], got.at[0], far_peer(0, e))
    for copy in fetches[3:]:
        copy.wait()

    lane = lax.broadcasted_iota(jnp.int32, (1, 128), 1)
    for d in range(1, CHAN):
        send(w_in, w_all.at[d], sent.at[2], got.at[1], x_peer(d))
    zero = jnp.zeros((24, 32), F32)
    for i in range(3):
        slabs = [jnp.concatenate([w_mid[9 * i + jl].astype(F32), zero], 1) for jl in range(TAPS)]
        for k in range(CHAN):
            tiles = []
            for group in (range(0, 5), range(5, 9)):
                tile = jnp.zeros((24, 128), F32)
                for u, jl in enumerate(group):
                    moved = pltpu.roll(slabs[jl], (24 * u - 24 * k) % 128, 1)
                    tile = jnp.where((lane >= 24 * u) & (lane < 24 * u + 24), moved, tile)
                tiles.append(tile)
            w_send_two[k, i] = jnp.concatenate(tiles, 1).astype(BF16)
    for d in range(1, CHAN):
        send(w_send_two.at[(q + d) % CHAN], w_recv_two.at[d], sent.at[3], got.at[2], x_peer(d))

    drain(recv_a.at[1:8], got.at[0])
    parts = [send_a[0].astype(F32)] + [recv_a[e].astype(F32) for e in range(1, PLANE)]
    for d, part in enumerate(swap_groups(parts)):
        send_b[d] = part.astype(BF16)
    second = {d: send(send_b.at[d], recv_b.at[d], sent.at[1], got_z.at[d], far_peer(d, 0)) for d in FAR_FIRST}

    none = 36
    for b in range(BRICKS):
        for f in range(6):
            local = nbr[b, f] - BRICKS * s + BRICKS
            there = (nbr[b, f] >= 0) & (local >= 0) & (local < 3 * BRICKS)
            base = (local >> 2) * 12 + f // 2
            index[0, 6 * b + f] = jnp.where(there, base + 3 * (local & 3), none)
            index[1, 6 * b + f] = jnp.where(there, base + 3 * ((q - local) & 3), none)

    cells = jnp.zeros((256, 128), F32)
    for d in (0, 1, 7, 2, 6, 3, 5, 4):
        at = slice(256 * d, 256 * d + 256)
        if d:
            second[d].wait_recv()
        slots = (recv_b if d else send_b)[d].astype(F32)
        hi = slots[16:17]
        hot = one_hot(slots[17:18], 128)
        lot_s[:, at] = hot
        hi_s[:, at] = jnp.broadcast_to(hi, (8, 256))
        hi_wide = jnp.broadcast_to(hi, (16, 256))
        spread = [jnp.where(hi_wide == float(h), slots[0:16], 0.0).astype(BF16) for h in range(16)]
        cells = cells + dot_lanes(jnp.concatenate(spread, 0), hot)
    for h in range(16):
        x_one[h // 4, :, 128 * (h % 4) : 128 * (h % 4) + 128] = cells[16 * h : 16 * h + 16].astype(BF16)

    def rim(face, b, p, relative):
        low, high = (face[index[relative, 6 * b + f]].astype(F32) for f in (2 * p, 2 * p + 1))
        return jnp.where(lax.broadcasted_iota(jnp.int32, low.shape, 1) < 64, low, high)

    def tap_sum(full, count, taps):
        total = None
        for at, shift in taps:
            term = full[at : at + count]
            term = jnp.concatenate([term[:, 128 * x : 128 * x + 128] for x in range(8)], 0)
            if shift:
                term = pltpu.roll(term, 128 - shift, 1)
            total = term if total is None else total + term
        return total

    def pack_planes(layer, count):
        return [
            jnp.concatenate(
                [layer[count * (2 * p) : count * (2 * p + 1)], layer[count * (2 * p + 1) : count * (2 * p + 2)]], 1
            )
            for p in range(4)
        ]

    rims = dot(jnp.concatenate([x_one[b] for b in range(BRICKS)], 0), sel[...])
    for b in range(BRICKS):
        for p in range(3):
            face_one[12 + 3 * b + p] = rims[16 * b : 16 * b + 16, 128 * p : 128 * p + 128].astype(BF16)
    face_one[none] = jnp.zeros((16, 128), BF16)
    face_two[none] = jnp.zeros((ALL, 128), BF16)
    for e in (0, 1):
        send(face_one.at[12:24], face_one.at[24 * e : 24 * e + 12], sent.at[4], got.at[3], s_peer(1 - 2 * e))
    for d in (2, 1, 3):
        send(x_one.at[(q + d) % CHAN], c_one.at[d], sent.at[5], got.at[4], x_peer(d))
    drain(w_all.at[1:4], got.at[1])
    drain(w_recv_two.at[1:4], got.at[2])
    zero = jnp.zeros((9 * 64, 32), F32)
    for l in range(3):
        pieces = [(w_in if r == 0 else w_all.at[r])[3 * ij + l].astype(F32) for ij in range(9) for r in range(CHAN)]
        tall = jnp.concatenate([jnp.concatenate(pieces, 0), zero], 1)
        w_one[ALL * l : ALL * l + ALL, 0 : 9 * 64] = tall.T[0:ALL].astype(BF16)
    w_recv_two[0] = w_send_two[q]
    pieces = [w_recv_two[(q - k + CHAN) % CHAN, i].astype(F32) for i in range(3) for k in range(CHAN)]
    turned = jnp.concatenate(pieces + [jnp.zeros((ALL, 256), F32)], 0).T[:ROWS]
    out_id = lax.broadcasted_iota(jnp.int32, (ROWS, 384), 0) - tap_row(4)
    in_id = lax.broadcasted_iota(jnp.int32, (ROWS, 384), 1) - 3 * ALL - OUT * q
    same = (out_id == in_id) & (out_id >= 0) & (out_id < OUT)
    w_two[...] = jnp.where(same, 1.0, turned).astype(BF16)

    drain(face_one.at[0:24], got.at[3])
    for b in range(BRICKS):
        for p in range(3):
            h_send[b, p] = rim(face_one, b, p, 0).astype(BF16)
    for d in (2, 1, 3):
        send(h_send.at[(q + d) % CHAN], h_recv.at[d], sent.at[6], got.at[5], x_peer(d))
    drain(c_one.at[1:4], got.at[4])
    parts = [x_one[q].astype(F32)] + [c_one[r].astype(F32) for r in range(1, CHAN)]
    tiles = [part[:, 128 * p : 128 * p + 128] for part in parts for p in range(4)]
    inner = dot(jnp.concatenate(tiles, 0).astype(BF16), ec[...])
    drain(h_recv.at[1:4], got.at[5])
    edges = [jnp.concatenate([h_send[q, p]] + [h_recv[r, p] for r in range(1, CHAN)], 0) for p in range(3)]
    ends = dot(edges[0], ec[...]).astype(BF16)
    outer = dot(jnp.concatenate(edges[1:], 1), eh[...])
    planes = [ends[:, 0:128]]
    for p in range(4):
        mid = jnp.concatenate([inner[(4 * r + p) * 16 : (4 * r + p + 1) * 16] for r in range(CHAN)], 0)
        mid = (mid + outer[:, 256 * p : 256 * p + 256]).astype(BF16)
        planes += [mid[:, 0:128], mid[:, 128:256]]
    planes.append(ends[:, 128:256])
    for x, part in enumerate(planes):
        for j in range(3):
            pad_one[j, :, 128 * x : 128 * x + 128] = pltpu.roll(part, 128 - 10 * j, 1) if j else part
    deep = jnp.concatenate([pad_one[j, :, 128 * i : 128 * i + 1024] for i in range(3) for j in range(3)], 0)
    layer = tap_sum(dot(w_one[:, 0 : 9 * 64], deep), ALL, [(ALL * l, l) for l in range(3)])
    layer = jnp.maximum(layer, 0.0).astype(BF16).astype(F32)
    cells = dot(jnp.concatenate(pack_planes(layer, ALL), 0).astype(BF16), cm[...])
    for p in range(4):
        x_two[0, :, 128 * p : 128 * p + 128] = cells[ALL * p : ALL * p + ALL].astype(BF16)

    def piece(slot, t):
        return x_two.at[slot, 16 * t : 16 * t + 16]

    right, left = {}, {}
    for t in range(6):
        right[t] = send(piece(0, t), piece(1, t), sent.at[7], got_p.at[t if t < 3 else 6], x_peer(1))
        u = (t + 3) % 6
        left[u] = send(piece(0, u), piece(3, u), sent.at[7], got_p.at[u if u >= 3 else 7], x_peer(3))

    def send_faces(r, at):
        for e in (0, 1):
            src = face_two.at[12 + 3 * r : 15 + 3 * r, at]
            dst = face_two.at[24 * e + 3 * r : 24 * e + 3 * r + 3, at]
            send(src, dst, sent.at[8], got.at[6], s_peer(1 - 2 * e))

    def faces(r):
        rims = dot(x_two[r], sel[...])
        for p in range(3):
            face_two[12 + 3 * r + p] = rims[:, 128 * p : 128 * p + 128].astype(BF16)
        send_faces(r, slice(0, ALL))

    faces(0)
    for t in range(3):
        right[t].wait_recv()
        send(piece(1, t), piece(2, t), sent.at[7], got_p.at[8 + t], x_peer(1))
        left[3 + t].wait_recv()
        send(piece(3, 3 + t), piece(2, 3 + t), sent.at[7], got_p.at[8 + t], x_peer(3))
    drain(x_two.at[1, 48:96], got_p.at[6])
    faces(1)
    drain(x_two.at[3, 0:48], got_p.at[7])
    faces(3)
    for t in range(3):
        drain(x_two.at[2, 0:32], got_p.at[8 + t])
        rows = [slice(16 * u, 16 * u + 16) for u in (t, 3 + t)]
        rims = dot(jnp.concatenate([x_two[2, at] for at in rows], 0), sel[...])
        for half, at in enumerate(rows):
            for p in range(3):
                face_two[18 + p, at] = rims[16 * half : 16 * half + 16, 128 * p : 128 * p + 128].astype(BF16)
            send_faces(2, at)
    bricks = [x_two[(q - b + CHAN) % CHAN] for b in range(BRICKS)]
    tiles = [brick[:, 128 * p : 128 * p + 128] for brick in bricks for p in range(4)]
    inner = dot(jnp.concatenate(tiles, 0), ec[...])
    drain(face_two.at[0:24], got.at[6])
    edges = [
        jnp.concatenate([rim(face_two, b, p, 1).astype(BF16) for b in range(BRICKS)], 0) for p in range(3)
    ]
    ends = dot(edges[0], ec[...]).astype(BF16)
    outer = dot(jnp.concatenate(edges[1:], 1), eh[...])
    layers = []
    for b in range(BRICKS):
        pad_two[b, :, 0:128] = ends[ALL * b : ALL * b + ALL, 0:128]
        pad_two[b, :, 1152:1280] = ends[ALL * b : ALL * b + ALL, 128:256]
        for p in range(4):
            mid = inner[(4 * b + p) * ALL : (4 * b + p + 1) * ALL]
            mid = mid + outer[ALL * b : ALL * b + ALL, 256 * p : 256 * p + 256]
            pad_two[b, :, 128 + 256 * p : 384 + 256 * p] = mid.astype(BF16)
        deep = jnp.concatenate([pad_two[b, :, 128 * i : 128 * i + 1024] for i in (0, 1, 2, 1)], 0)
        layer = tap_sum(dot(w_two[...], deep), OUT, [(tap_row(jl), 10 * (jl // 3) + jl % 3) for jl in range(TAPS)])
        layers += pack_planes(jnp.maximum(layer, 0.0), OUT)
    closed = dot(jnp.concatenate(layers, 0).astype(BF16), cm[...])
    cells = closed.astype(BF16)

    for d in [*FAR_FIRST, 0]:
        at = slice(256 * d, 256 * d + 256)
        found = dot(cells, lot_s[:, at])
        hi_wide = jnp.broadcast_to(hi_s[0:1, at], (OUT, 256))
        value = found[0:OUT]
        for h in range(1, 16):
            value = jnp.where(hi_wide == float(h), found[OUT * h : OUT * h + OUT], value)
        tiles = split_tiles(jnp.concatenate([value[:, 0:128], value[:, 128:256]], 0))
        for e in range(PLANE):
            (ret_a if d or e else ret_v)[DEPTH * e + d] = tiles[e].astype(BF16)
        for e in [*FAR_FIRST, 0]:
            if d or e:
                at = DEPTH * e + d
                stage = 0 if e in (0, 1, 7) else 1 if e in (2, 6) else 2
                send(ret_a.at[at], ret_v.at[at], sent.at[9], got_ret.at[stage], far_peer(-d, -e))
    for p in range(4):
        tiles = [closed[OUT * (4 * b + p) : OUT * (4 * b + p) + OUT] for b in range(BRICKS)]
        grid_out[:, :, 128 * p : 128 * p + 128] = jnp.stack(tiles, 1).astype(BF16)
    for i, ref in enumerate(
        (
            send_a.at[1:8], send_b.at[1:8], w_all.at[1:4], w_send_two.at[1:4], face_one.at[0:24], x_one.at[1:4],
            h_send.at[1:4], x_two.at[0:3], face_two.at[0:24], ret_a.at[1:64],
        )
    ):
        drain(ref, sent.at[i])
    hi_wide = jnp.broadcast_to(hi_p[0:1], (OUT, 1024))
    for stage, near in enumerate(((0, 1, 7), (2, 6), (3, 5, 4))):
        ids = [DEPTH * e + d for e in near for d in range(DEPTH)]
        drain(ret_v.at[1 if stage == 0 else 0 : len(ids)], got_ret.at[stage])
        lines = join_tiles([ret_v[at].astype(F32) for at in ids])
        found = dot(lines.astype(BF16), lot_p[...])
        value = taken[...] if 0 not in near else jnp.zeros((OUT, 1024), F32)
        for i, h in enumerate(2 * e + half for e in near for half in (0, 1)):
            value = jnp.where(hi_wide == float(h), found[OUT * i : OUT * i + OUT], value)
        taken[...] = value
    point_out[...] = value.astype(BF16)


def deliver(grid, values, grid_out, point_out, sems):
    copies = [pltpu.make_async_copy(a, b, sems.at[i]) for i, (a, b) in enumerate(((grid, grid_out), (values, point_out)))]
    for copy in copies:
        copy.start()
    for copy in copies:
        copy.wait()


def per_device(point_feats, point_owner, point_place, neighbors, weight_in, weight_mid):
    anywhere = pl.BlockSpec(memory_space=pl.ANY)
    constants = [jnp.asarray(c(), BF16) for c in (face_picker, plane_spread, rim_spread, plane_pack)]
    points = point_feats.shape[1]
    grid, values = pl.pallas_call(
        body,
        out_shape=(
            pltpu.VMEM((OUT, BRICKS, CELLS), BF16),
            pltpu.VMEM((OUT, points), BF16),
        ),
        in_specs=[anywhere] * 10,
        out_specs=(pl.BlockSpec(memory_space=pltpu.VMEM), pl.BlockSpec(memory_space=pltpu.VMEM)),
        scratch_shapes=[
            pltpu.VMEM((16, points), BF16),
            pltpu.VMEM((1, points), jnp.int32),
            pltpu.VMEM((1, points), jnp.int32),
            pltpu.SMEM((4, 6), jnp.int32),
            pltpu.VMEM((27, 16, 96), BF16),
            pltpu.VMEM((27, 24, 96), BF16),
            *[pltpu.VMEM(c.shape, BF16) for c in constants],
            pltpu.SemaphoreType.DMA((10,)),
            pltpu.SMEM((2, 24), jnp.int32),
            pltpu.VMEM((8, 24, 256), BF16),
            pltpu.VMEM((8, 24, 256), BF16),
            pltpu.VMEM((8, 24, 256), BF16),
            pltpu.VMEM((8, 24, 256), BF16),
            pltpu.VMEM((4, 16, CELLS), BF16),
            pltpu.VMEM((4, 16, CELLS), BF16),
            pltpu.VMEM((4, 3, 16, 128), BF16),
            pltpu.VMEM((4, 3, 16, 128), BF16),
            pltpu.VMEM((4, ALL, CELLS), BF16),
            pltpu.VMEM((37, 16, 128), BF16),
            pltpu.VMEM((37, ALL, 128), BF16),
            pltpu.VMEM((4, 27, 16, 96), BF16),
            pltpu.VMEM((4, 3, 24, 256), BF16),
            pltpu.VMEM((4, 3, 24, 256), BF16),
            pltpu.VMEM((3 * ALL, 640), BF16),
            pltpu.VMEM((ROWS, 384), BF16),
            pltpu.VMEM((128, points), BF16),
            pltpu.VMEM((8, points), F32),
            pltpu.VMEM((128, VOX), BF16),
            pltpu.VMEM((8, VOX), F32),
            pltpu.VMEM((3, 64, 1280), BF16),
            pltpu.VMEM((4, ALL, 1280), BF16),
            pltpu.VMEM((64, 8, 128), BF16),
            pltpu.VMEM((64, 8, 128), BF16),
            pltpu.VMEM((OUT, points), F32),
            pltpu.SemaphoreType.DMA((10,)),
            pltpu.SemaphoreType.DMA((7,)),
            pltpu.SemaphoreType.DMA((8,)),
            pltpu.SemaphoreType.DMA((11,)),
            pltpu.SemaphoreType.DMA((3,)),
        ],
        compiler_params=pltpu.CompilerParams(collective_id=0, has_side_effects=True),
    )(
        point_feats,
        point_owner.reshape(1, points),
        point_place.reshape(1, points),
        neighbors,
        jnp.transpose(weight_in, (1, 0, 2)),
        jnp.transpose(weight_mid, (1, 0, 2)),
        *constants,
    )
    grid, values = (pltpu.with_memory_space_constraint(a, pltpu.VMEM) for a in (grid, values))
    return pl.pallas_call(
        deliver,
        out_shape=(
            jax.ShapeDtypeStruct((OUT, BRICKS, CELLS), BF16),
            jax.ShapeDtypeStruct((OUT, points), BF16),
        ),
        in_specs=[pl.BlockSpec(memory_space=pltpu.VMEM)] * 2,
        out_specs=(anywhere, anywhere),
        scratch_shapes=[pltpu.SemaphoreType.DMA((2,))],
    )(grid, values)


def solution(mesh):
    return jax.shard_map(
        per_device,
        mesh=mesh,
        in_specs=(
            P("chan", "space"),
            P("space", None),
            P("space"),
            P("space", None),
            P("chan", None, None),
            P("chan", None, None),
        ),
        out_specs=(P("chan", "space", None), P("chan", "space")),
        check_vma=False,
    )
```

```python
import functools

import jax
import jax.numpy as jnp
import numpy as np
from jax import lax
from jax.experimental import pallas as pl
from jax.experimental.pallas import tpu as pltpu
from jax.sharding import PartitionSpec as P

DEPTH = 8
PLANE = 8
CHAN = 4
CAP = 32
CELLS = 512
BRICKS = 4
VOX = BRICKS * CELLS
OUT = 24
TAPS = 9
F32 = jnp.float32
BF16 = jnp.bfloat16
MESH = pl.DeviceIdType.MESH


def tap_row(jl):
    return OUT * jl + (8 if jl >= 5 else 0)


ROWS = 224
ALL = 96
FAR_FIRST = (4, 3, 5, 2, 6, 1, 7)


def face_picker():
    sel = np.zeros((CELLS, 384), np.float32)
    for u in range(8):
        for w in range(8):
            for p in range(3):
                for half, end in ((0, 7), (1, 0)):
                    x, y, z = ((end, u, w), (u, end, w), (u, w, end))[p]
                    sel[(8 * x + y) * 8 + z, 128 * p + 64 * half + 8 * u + w] = 1
    return sel


def plane_spread():
    ec = np.zeros((128, 256), np.float32)
    for x in range(2):
        for y in range(8):
            for z in range(8):
                ec[64 * x + 8 * y + z, 128 * x + 10 * (y + 1) + z + 1] = 1
    return ec


def rim_spread():
    eh = np.zeros((256, 1024), np.float32)
    for x in range(8):
        for w in range(8):
            eh[8 * x + w, 128 * x + w + 1] = 1
            eh[64 + 8 * x + w, 128 * x + 90 + w + 1] = 1
            eh[128 + 8 * x + w, 128 * x + 10 * (w + 1)] = 1
            eh[192 + 8 * x + w, 128 * x + 10 * (w + 1) + 9] = 1
    return eh


def plane_pack():
    cm = np.zeros((256, 128), np.float32)
    for x in range(2):
        for y in range(8):
            for z in range(8):
                cm[128 * x + 10 * y + z, 64 * x + 8 * y + z] = 1
    return cm


def dot(a, b):
    return jnp.dot(a, b, preferred_element_type=F32)


def dot_lanes(a, b):
    return lax.dot_general(a, b, (((1,), (1,)), ((), ())), preferred_element_type=F32)


def one_hot(row, count):
    ids = lax.broadcasted_iota(jnp.int32, (count, row.shape[1]), 0).astype(F32)
    return jnp.where(ids == row, 1.0, 0.0).astype(BF16)


def pick(choices):
    group = lax.broadcasted_iota(jnp.int32, (8, 128), 1) // 32
    result = choices[-1]
    for i in reversed(range(len(choices) - 1)):
        result = jnp.where(group == i, choices[i], result)
    return result


def split_tiles(tall):
    turned = [tall] + [pltpu.roll(tall, 32 * a, 1) for a in range(1, 4)]
    return [
        pick([turned[(m - u) % 4][24 * h + 8 * m : 24 * h + 8 * m + 8] for m in range(3)])
        for h in range(tall.shape[0] // 24)
        for u in range(4)
    ]


def join_tiles(tiles):
    tall = jnp.concatenate(tiles, 0)
    turned = [tall] + [pltpu.roll(tall, 32 * a, 1) for a in range(1, 4)]
    return jnp.concatenate(
        [
            pick([turned[(u - m) % 4][8 * (4 * h + u) : 8 * (4 * h + u) + 8] for u in range(4)])
            for h in range(len(tiles) // 4)
            for m in range(3)
        ],
        0,
    )


def swap_groups(parts):
    rows = parts[0].shape[0]
    tall = jnp.concatenate([p[:, 128 * m : 128 * m + 128] for p in parts for m in range(2)], 0)
    turned = [tall] + [pltpu.roll(tall, 32 * a, 1) for a in range(1, 4)]
    group = lax.broadcasted_iota(jnp.int32, (rows, 128), 1) // 32
    result = []
    for j in range(8):
        m, g = j // 4, j % 4
        tiles = []
        for t in range(2):
            tile = None
            for u in range(4):
                at = (2 * (4 * t + u) + m) * rows
                piece = turned[(u - g) % 4][at : at + rows]
                tile = piece if tile is None else jnp.where(group == u, piece, tile)
            tiles.append(tile)
        result.append(jnp.concatenate(tiles, 1))
    return result


def body(
    feats_in, owner_in, place_in, nbr_in, w_in_in, w_mid_in, sel_in, ec_in, eh_in, cm_in,
    grid_out, point_out,
    feats, owner, place, nbr, w_in, w_mid, sel, ec, eh, cm, sem_in, index,
    send_a, recv_a, send_b, recv_b, x_one, c_one, h_send, h_recv, x_two, face_one, face_two, w_all, w_send_two, w_recv_two,
    w_one, w_two, lot_p, hi_p, lot_s, hi_s, pad_one, pad_two, ret_a, ret_v, taken,
    sent, got, got_z, got_p, got_ret,
):
    s = lax.axis_index("space")
    q = lax.axis_index("chan")
    core = s % 2
    z = (s // 2) % DEPTH
    row = s // (2 * DEPTH)
    plane = row * 2 + core
    spaces = 64

    def far_peer(d, e):
        other = (plane + e + PLANE) % PLANE
        return {"space": ((other // 2) * DEPTH + (z + d + DEPTH) % DEPTH) * 2 + other % 2, "chan": q}

    def x_peer(d):
        return {"space": s, "chan": (q + d) % CHAN}

    def s_peer(d):
        return {"space": (s + d + spaces) % spaces, "chan": q}

    def send(src, dst, sent, got, peer):
        copy = pltpu.make_async_remote_copy(
            src_ref=src, dst_ref=dst, send_sem=sent, recv_sem=got, device_id=peer, device_id_type=MESH
        )
        copy.start()
        return copy

    def drain(ref, sem):
        pltpu.make_async_copy(ref, ref, sem).wait()

    fetches = [
        pltpu.make_async_copy(src, dst, sem_in.at[i])
        for i, (src, dst) in enumerate(
            (
                (owner_in, owner), (place_in, place), (feats_in, feats), (w_in_in, w_in), (w_mid_in, w_mid),
                (nbr_in, nbr), (sel_in, sel), (ec_in, ec), (eh_in, eh), (cm_in, cm),
            )
        )
    ]
    for copy in fetches:
        copy.start()
    peers = (
        [far_peer(0, e) for e in FAR_FIRST]
        + [far_peer(d, 0) for d in FAR_FIRST]
        + [s_peer(1), s_peer(-1)]
        + [x_peer(d) for d in range(1, CHAN)]
    )
    barrier = pltpu.get_barrier_semaphore()
    for peer in peers:
        pl.semaphore_signal(barrier, inc=1, device_id=peer, device_id_type=MESH)

    for copy in fetches[:3]:
        copy.wait()

    own = owner[...]
    where_to = place[...]
    match = jnp.where(lax.broadcasted_iota(jnp.int32, (64, 1024), 0) == own, 1.0, 0.0)
    tall = jnp.concatenate([match[:, 256 * i : 256 * i + 256] for i in range(4)], 0)
    before = jnp.where(
        lax.broadcasted_iota(jnp.int32, (256, 256), 0) < lax.broadcasted_iota(jnp.int32, (256, 256), 1), 1.0, 0.0
    )
    earlier = dot(tall.astype(BF16), before.astype(BF16))
    carry = jnp.zeros((64, 1), F32)
    ranks = []
    for i in range(4):
        mine = tall[64 * i : 64 * i + 64]
        ranks.append(jnp.sum(mine * (earlier[64 * i : 64 * i + 64] + carry), axis=0, keepdims=True))
        carry = carry + jnp.sum(mine, axis=1, keepdims=True)
    rank = jnp.concatenate(ranks, 1)
    to_z = ((own // 2) - z) & 7
    to_plane = ((own // (2 * DEPTH)) * 2 + (own & 1) - plane) & 7
    hi = (to_plane * 2 + to_z // 4).astype(F32)
    lo = ((to_z & 3) * CAP).astype(F32) + rank
    hot = one_hot(lo, 128)
    lot_p[...] = hot
    hi_p[...] = jnp.broadcast_to(hi, (8, 1024))
    extra = lax.broadcasted_iota(jnp.int32, (8, 1024), 0)
    extra = jnp.where(
        extra == 0, (where_to // 128).astype(F32), jnp.where(extra == 1, (where_to % 128).astype(F32), 0.0)
    )
    full = jnp.concatenate([feats[...].astype(F32), extra], 0)
    hi_wide = jnp.broadcast_to(hi, (24, 1024))
    spread = jnp.concatenate([jnp.where(hi_wide == float(h), full, 0.0).astype(BF16) for h in range(16)], 0)
    packed = dot_lanes(spread, hot)
    for h in range(16):
        send_a[h // 2, :, 128 * (h % 2) : 128 * (h % 2) + 128] = packed[24 * h : 24 * h + 24].astype(BF16)

    pl.semaphore_wait(barrier, len(peers))

    for e in FAR_FIRST:
        send(send_a.at[e], recv_a.at[e], sent.at[0], got.at[0], far_peer(0, e))
    for copy in fetches[3:]:
        copy.wait()

    lane = lax.broadcasted_iota(jnp.int32, (1, 128), 1)
    for d in range(1, CHAN):
        send(w_in, w_all.at[d], sent.at[1], got.at[1], x_peer(d))
    zero = jnp.zeros((24, 32), F32)
    for i in range(3):
        slabs = [jnp.concatenate([w_mid[9 * i + jl].astype(F32), zero], 1) for jl in range(TAPS)]
        for k in range(CHAN):
            tiles = []
            for group in (range(0, 5), range(5, 9)):
                tile = jnp.zeros((24, 128), F32)
                for u, jl in enumerate(group):
                    moved = pltpu.roll(slabs[jl], (24 * u - 24 * k) % 128, 1)
                    tile = jnp.where((lane >= 24 * u) & (lane < 24 * u + 24), moved, tile)
                tiles.append(tile)
            w_send_two[k, i] = jnp.concatenate(tiles, 1).astype(BF16)
    for d in range(1, CHAN):
        send(w_send_two.at[(q + d) % CHAN], w_recv_two.at[d], sent.at[0], got.at[2], x_peer(d))

    drain(recv_a.at[1:8], got.at[0])
    parts = [send_a[0].astype(F32)] + [recv_a[e].astype(F32) for e in range(1, PLANE)]
    for d, part in enumerate(swap_groups(parts)):
        send_b[d] = part.astype(BF16)
    second = {d: send(send_b.at[d], recv_b.at[d], sent.at[0], got_z.at[d - 1], far_peer(d, 0)) for d in FAR_FIRST}

    none = 36
    for b in range(BRICKS):
        for f in range(6):
            local = nbr[b, f] - BRICKS * s + BRICKS
            there = (nbr[b, f] >= 0) & (local >= 0) & (local < 3 * BRICKS)
            base = (local >> 2) * 12 + f // 2
            index[0, 6 * b + f] = jnp.where(there, base + 3 * (local & 3), none)
            index[1, 6 * b + f] = jnp.where(there, base + 3 * ((q - local) & 3), none)

    cells = jnp.zeros((256, 128), F32)
    for d in (0, 1, 7, 2, 6, 3, 5, 4):
        at = slice(256 * d, 256 * d + 256)
        if d:
            second[d].wait_recv()
        slots = (recv_b if d else send_b)[d].astype(F32)
        hi = slots[16:17]
        hot = one_hot(slots[17:18], 128)
        lot_s[:, at] = hot
        hi_s[:, at] = jnp.broadcast_to(hi, (8, 256))
        hi_wide = jnp.broadcast_to(hi, (16, 256))
        spread = [jnp.where(hi_wide == float(h), slots[0:16], 0.0).astype(BF16) for h in range(16)]
        cells = cells + dot_lanes(jnp.concatenate(spread, 0), hot)
    for h in range(16):
        x_one[h // 4, :, 128 * (h % 4) : 128 * (h % 4) + 128] = cells[16 * h : 16 * h + 16].astype(BF16)

    def rim(face, b, p, relative):
        low, high = (face[index[relative, 6 * b + f]].astype(F32) for f in (2 * p, 2 * p + 1))
        return jnp.where(lax.broadcasted_iota(jnp.int32, low.shape, 1) < 64, low, high)

    def tap_sum(full, count, taps):
        total = None
        for at, shift in taps:
            term = full[at : at + count]
            term = jnp.concatenate([term[:, 128 * x : 128 * x + 128] for x in range(8)], 0)
            if shift:
                term = pltpu.roll(term, 128 - shift, 1)
            total = term if total is None else total + term
        return total

    def pack_planes(layer, count):
        return [
            jnp.concatenate(
                [layer[count * (2 * p) : count * (2 * p + 1)], layer[count * (2 * p + 1) : count * (2 * p + 2)]], 1
            )
            for p in range(4)
        ]

    rims = dot(jnp.concatenate([x_one[b] for b in range(BRICKS)], 0), sel[...])
    for b in range(BRICKS):
        for p in range(3):
            face_one[12 + 3 * b + p] = rims[16 * b : 16 * b + 16, 128 * p : 128 * p + 128].astype(BF16)
    face_one[none] = jnp.zeros((16, 128), BF16)
    face_two[none] = jnp.zeros((ALL, 128), BF16)
    for e in (0, 1):
        send(face_one.at[12:24], face_one.at[24 * e : 24 * e + 12], sent.at[0], got.at[3], s_peer(1 - 2 * e))
    for d in (2, 1, 3):
        send(x_one.at[(q + d) % CHAN], c_one.at[d], sent.at[0], got.at[4], x_peer(d))
    drain(w_all.at[1:4], got.at[1])
    drain(w_recv_two.at[1:4], got.at[2])
    zero = jnp.zeros((9 * 64, 32), F32)
    for l in range(3):
        pieces = [(w_in if r == 0 else w_all.at[r])[3 * ij + l].astype(F32) for ij in range(9) for r in range(CHAN)]
        tall = jnp.concatenate([jnp.concatenate(pieces, 0), zero], 1)
        w_one[ALL * l : ALL * l + ALL, 0 : 9 * 64] = tall.T[0:ALL].astype(BF16)
    w_recv_two[0] = w_send_two[q]
    pieces = [w_recv_two[(q - k + CHAN) % CHAN, i].astype(F32) for i in range(3) for k in range(CHAN)]
    turned = jnp.concatenate(pieces + [jnp.zeros((ALL, 256), F32)], 0).T[:ROWS]
    out_id = lax.broadcasted_iota(jnp.int32, (ROWS, 384), 0) - tap_row(4)
    in_id = lax.broadcasted_iota(jnp.int32, (ROWS, 384), 1) - 3 * ALL - OUT * q
    same = (out_id == in_id) & (out_id >= 0) & (out_id < OUT)
    w_two[...] = jnp.where(same, 1.0, turned).astype(BF16)

    drain(face_one.at[0:24], got.at[3])
    for b in range(BRICKS):
        for p in range(3):
            h_send[b, p] = rim(face_one, b, p, 0).astype(BF16)
    for d in (2, 1, 3):
        send(h_send.at[(q + d) % CHAN], h_recv.at[d], sent.at[0], got.at[5], x_peer(d))
    drain(c_one.at[1:4], got.at[4])
    parts = [x_one[q].astype(F32)] + [c_one[r].astype(F32) for r in range(1, CHAN)]
    tiles = [part[:, 128 * p : 128 * p + 128] for part in parts for p in range(4)]
    inner = dot(jnp.concatenate(tiles, 0).astype(BF16), ec[...])
    drain(h_recv.at[1:4], got.at[5])
    edges = [jnp.concatenate([h_send[q, p]] + [h_recv[r, p] for r in range(1, CHAN)], 0) for p in range(3)]
    ends = dot(edges[0], ec[...]).astype(BF16)
    outer = dot(jnp.concatenate(edges[1:], 1), eh[...])
    planes = [ends[:, 0:128]]
    for p in range(4):
        mid = jnp.concatenate([inner[(4 * r + p) * 16 : (4 * r + p + 1) * 16] for r in range(CHAN)], 0)
        mid = (mid + outer[:, 256 * p : 256 * p + 256]).astype(BF16)
        planes += [mid[:, 0:128], mid[:, 128:256]]
    planes.append(ends[:, 128:256])
    for x, part in enumerate(planes):
        for j in range(3):
            pad_one[j, :, 128 * x : 128 * x + 128] = pltpu.roll(part, 128 - 10 * j, 1) if j else part
    deep = jnp.concatenate([pad_one[j, :, 128 * i : 128 * i + 1024] for i in range(3) for j in range(3)], 0)
    layer = tap_sum(dot(w_one[:, 0 : 9 * 64], deep), ALL, [(ALL * l, l) for l in range(3)])
    layer = jnp.maximum(layer, 0.0).astype(BF16).astype(F32)
    cells = dot(jnp.concatenate(pack_planes(layer, ALL), 0).astype(BF16), cm[...])
    for p in range(4):
        x_two[0, :, 128 * p : 128 * p + 128] = cells[ALL * p : ALL * p + ALL].astype(BF16)

    def piece(slot, t):
        return x_two.at[slot, 16 * t : 16 * t + 16]

    right, left = {}, {}
    for t in range(6):
        right[t] = send(piece(0, t), piece(1, t), sent.at[0], got_p.at[t if t < 3 else 6], x_peer(1))
        u = (t + 3) % 6
        left[u] = send(piece(0, u), piece(3, u), sent.at[0], got_p.at[u if u >= 3 else 7], x_peer(3))

    def send_faces(r, at):
        for e in (0, 1):
            src = face_two.at[12 + 3 * r : 15 + 3 * r, at]
            dst = face_two.at[24 * e + 3 * r : 24 * e + 3 * r + 3, at]
            send(src, dst, sent.at[2], got.at[6], s_peer(1 - 2 * e))

    def faces(r):
        rims = dot(x_two[r], sel[...])
        for p in range(3):
            face_two[12 + 3 * r + p] = rims[:, 128 * p : 128 * p + 128].astype(BF16)
        send_faces(r, slice(0, ALL))

    faces(0)
    for t in range(3):
        right[t].wait_recv()
        send(piece(1, t), piece(2, t), sent.at[0], got_p.at[8 + t], x_peer(1))
        left[3 + t].wait_recv()
        send(piece(3, 3 + t), piece(2, 3 + t), sent.at[0], got_p.at[8 + t], x_peer(3))
    drain(x_two.at[1, 48:96], got_p.at[6])
    faces(1)
    drain(x_two.at[3, 0:48], got_p.at[7])
    faces(3)
    for t in range(3):
        drain(x_two.at[2, 0:32], got_p.at[8 + t])
        rows = [slice(16 * u, 16 * u + 16) for u in (t, 3 + t)]
        rims = dot(jnp.concatenate([x_two[2, at] for at in rows], 0), sel[...])
        for half, at in enumerate(rows):
            for p in range(3):
                face_two[18 + p, at] = rims[16 * half : 16 * half + 16, 128 * p : 128 * p + 128].astype(BF16)
            send_faces(2, at)
    bricks = [x_two[(q - b + CHAN) % CHAN] for b in range(BRICKS)]
    tiles = [brick[:, 128 * p : 128 * p + 128] for brick in bricks for p in range(4)]
    inner = dot(jnp.concatenate(tiles, 0), ec[...])
    drain(face_two.at[0:24], got.at[6])
    edges = [
        jnp.concatenate([rim(face_two, b, p, 1).astype(BF16) for b in range(BRICKS)], 0) for p in range(3)
    ]
    ends = dot(edges[0], ec[...]).astype(BF16)
    outer = dot(jnp.concatenate(edges[1:], 1), eh[...])
    layers = []
    for b in range(BRICKS):
        pad_two[b, :, 0:128] = ends[ALL * b : ALL * b + ALL, 0:128]
        pad_two[b, :, 1152:1280] = ends[ALL * b : ALL * b + ALL, 128:256]
        for p in range(4):
            mid = inner[(4 * b + p) * ALL : (4 * b + p + 1) * ALL]
            mid = mid + outer[ALL * b : ALL * b + ALL, 256 * p : 256 * p + 256]
            pad_two[b, :, 128 + 256 * p : 384 + 256 * p] = mid.astype(BF16)
        deep = jnp.concatenate([pad_two[b, :, 128 * i : 128 * i + 1024] for i in (0, 1, 2, 1)], 0)
        layer = tap_sum(dot(w_two[...], deep), OUT, [(tap_row(jl), 10 * (jl // 3) + jl % 3) for jl in range(TAPS)])
        layers += pack_planes(jnp.maximum(layer, 0.0), OUT)
    closed = dot(jnp.concatenate(layers, 0).astype(BF16), cm[...])
    cells = closed.astype(BF16)

    for d in [*FAR_FIRST, 0]:
        at = slice(256 * d, 256 * d + 256)
        found = dot(cells, lot_s[:, at])
        hi_wide = jnp.broadcast_to(hi_s[0:1, at], (OUT, 256))
        value = found[0:OUT]
        for h in range(1, 16):
            value = jnp.where(hi_wide == float(h), found[OUT * h : OUT * h + OUT], value)
        tiles = split_tiles(jnp.concatenate([value[:, 0:128], value[:, 128:256]], 0))
        for e in range(PLANE):
            (ret_a if d or e else ret_v)[DEPTH * e + d] = tiles[e].astype(BF16)
        for e in [*FAR_FIRST, 0]:
            if d or e:
                at = DEPTH * e + d
                stage = 0 if e in (0, 1, 7) else 1 if e in (2, 6) else 2
                send(ret_a.at[at], ret_v.at[at], sent.at[3], got_ret.at[stage], far_peer(-d, -e))
    for p in range(4):
        tiles = [closed[OUT * (4 * b + p) : OUT * (4 * b + p) + OUT] for b in range(BRICKS)]
        grid_out[:, :, 128 * p : 128 * p + 128] = jnp.stack(tiles, 1).astype(BF16)
    for i, ref in enumerate((face_two.at[0:31], w_all.at[1:4], face_two.at[0:24], ret_a.at[1:64])):
        drain(ref, sent.at[i])
    hi_wide = jnp.broadcast_to(hi_p[0:1], (OUT, 1024))
    for stage, near in enumerate(((0, 1, 7), (2, 6), (3, 5, 4))):
        ids = [DEPTH * e + d for e in near for d in range(DEPTH)]
        drain(ret_v.at[1 if stage == 0 else 0 : len(ids)], got_ret.at[stage])
        lines = join_tiles([ret_v[at].astype(F32) for at in ids])
        found = dot(lines.astype(BF16), lot_p[...])
        value = taken[...] if 0 not in near else jnp.zeros((OUT, 1024), F32)
        for i, h in enumerate(2 * e + half for e in near for half in (0, 1)):
            value = jnp.where(hi_wide == float(h), found[OUT * i : OUT * i + OUT], value)
        taken[...] = value
    point_out[...] = value.astype(BF16)


def deliver(grid, values, grid_out, point_out, sems):
    copies = [pltpu.make_async_copy(a, b, sems.at[i]) for i, (a, b) in enumerate(((grid, grid_out), (values, point_out)))]
    for copy in copies:
        copy.start()
    for copy in copies:
        copy.wait()


def per_device(point_feats, point_owner, point_place, neighbors, weight_in, weight_mid):
    anywhere = pl.BlockSpec(memory_space=pl.ANY)
    constants = [jnp.asarray(c(), BF16) for c in (face_picker, plane_spread, rim_spread, plane_pack)]
    points = point_feats.shape[1]
    grid, values = pl.pallas_call(
        body,
        out_shape=(
            pltpu.VMEM((OUT, BRICKS, CELLS), BF16),
            pltpu.VMEM((OUT, points), BF16),
        ),
        in_specs=[anywhere] * 10,
        out_specs=(pl.BlockSpec(memory_space=pltpu.VMEM), pl.BlockSpec(memory_space=pltpu.VMEM)),
        scratch_shapes=[
            pltpu.VMEM((16, points), BF16),
            pltpu.VMEM((1, points), jnp.int32),
            pltpu.VMEM((1, points), jnp.int32),
            pltpu.SMEM((4, 6), jnp.int32),
            pltpu.VMEM((27, 16, 96), BF16),
            pltpu.VMEM((27, 24, 96), BF16),
            *[pltpu.VMEM(c.shape, BF16) for c in constants],
            pltpu.SemaphoreType.DMA((10,)),
            pltpu.SMEM((2, 24), jnp.int32),
            pltpu.VMEM((8, 24, 256), BF16),
            pltpu.VMEM((8, 24, 256), BF16),
            pltpu.VMEM((8, 24, 256), BF16),
            pltpu.VMEM((8, 24, 256), BF16),
            pltpu.VMEM((4, 16, CELLS), BF16),
            pltpu.VMEM((4, 16, CELLS), BF16),
            pltpu.VMEM((4, 3, 16, 128), BF16),
            pltpu.VMEM((4, 3, 16, 128), BF16),
            pltpu.VMEM((4, ALL, CELLS), BF16),
            pltpu.VMEM((37, 16, 128), BF16),
            pltpu.VMEM((37, ALL, 128), BF16),
            pltpu.VMEM((4, 27, 16, 96), BF16),
            pltpu.VMEM((4, 3, 24, 256), BF16),
            pltpu.VMEM((4, 3, 24, 256), BF16),
            pltpu.VMEM((3 * ALL, 640), BF16),
            pltpu.VMEM((ROWS, 384), BF16),
            pltpu.VMEM((128, points), BF16),
            pltpu.VMEM((8, points), F32),
            pltpu.VMEM((128, VOX), BF16),
            pltpu.VMEM((8, VOX), F32),
            pltpu.VMEM((3, 64, 1280), BF16),
            pltpu.VMEM((4, ALL, 1280), BF16),
            pltpu.VMEM((64, 8, 128), BF16),
            pltpu.VMEM((64, 8, 128), BF16),
            pltpu.VMEM((OUT, points), F32),
            pltpu.SemaphoreType.DMA((4,)),
            pltpu.SemaphoreType.DMA((7,)),
            pltpu.SemaphoreType.DMA((7,)),
            pltpu.SemaphoreType.DMA((11,)),
            pltpu.SemaphoreType.DMA((3,)),
        ],
        compiler_params=pltpu.CompilerParams(collective_id=0, has_side_effects=True),
    )(
        point_feats,
        point_owner.reshape(1, points),
        point_place.reshape(1, points),
        neighbors,
        jnp.transpose(weight_in, (1, 0, 2)),
        jnp.transpose(weight_mid, (1, 0, 2)),
        *constants,
    )
    grid, values = (pltpu.with_memory_space_constraint(a, pltpu.VMEM) for a in (grid, values))
    return pl.pallas_call(
        deliver,
        out_shape=(
            jax.ShapeDtypeStruct((OUT, BRICKS, CELLS), BF16),
            jax.ShapeDtypeStruct((OUT, points), BF16),
        ),
        in_specs=[pl.BlockSpec(memory_space=pltpu.VMEM)] * 2,
        out_specs=(anywhere, anywhere),
        scratch_shapes=[pltpu.SemaphoreType.DMA((2,))],
    )(grid, values)


def solution(mesh):
    return jax.shard_map(
        per_device,
        mesh=mesh,
        in_specs=(
            P("chan", "space"),
            P("space", None),
            P("space"),
            P("space", None),
            P("chan", None, None),
            P("chan", None, None),
        ),
        out_specs=(P("chan", "space", None), P("chan", "space")),
        check_vma=False,
    )
```

```python
import functools

import jax
import jax.numpy as jnp
import numpy as np
from jax import lax
from jax.experimental import pallas as pl
from jax.experimental.pallas import tpu as pltpu
from jax.sharding import PartitionSpec as P

DEPTH = 8
PLANE = 8
CHAN = 4
CAP = 32
CELLS = 512
BRICKS = 4
VOX = BRICKS * CELLS
OUT = 24
TAPS = 9
F32 = jnp.float32
BF16 = jnp.bfloat16
MESH = pl.DeviceIdType.MESH


def tap_row(jl):
    return OUT * jl + (8 if jl >= 5 else 0)


ROWS = 224
ALL = 96
FAR_FIRST = (4, 3, 5, 2, 6, 1, 7)


def face_picker():
    sel = np.zeros((CELLS, 384), np.float32)
    for u in range(8):
        for w in range(8):
            for p in range(3):
                for half, end in ((0, 7), (1, 0)):
                    x, y, z = ((end, u, w), (u, end, w), (u, w, end))[p]
                    sel[(8 * x + y) * 8 + z, 128 * p + 64 * half + 8 * u + w] = 1
    return sel


def plane_spread():
    ec = np.zeros((128, 256), np.float32)
    for x in range(2):
        for y in range(8):
            for z in range(8):
                ec[64 * x + 8 * y + z, 128 * x + 10 * (y + 1) + z + 1] = 1
    return ec


def rim_spread():
    eh = np.zeros((256, 1024), np.float32)
    for x in range(8):
        for w in range(8):
            eh[8 * x + w, 128 * x + w + 1] = 1
            eh[64 + 8 * x + w, 128 * x + 90 + w + 1] = 1
            eh[128 + 8 * x + w, 128 * x + 10 * (w + 1)] = 1
            eh[192 + 8 * x + w, 128 * x + 10 * (w + 1) + 9] = 1
    return eh


def plane_pack():
    cm = np.zeros((256, 128), np.float32)
    for x in range(2):
        for y in range(8):
            for z in range(8):
                cm[128 * x + 10 * y + z, 64 * x + 8 * y + z] = 1
    return cm


def dot(a, b):
    return jnp.dot(a, b, preferred_element_type=F32)


def dot_lanes(a, b):
    return lax.dot_general(a, b, (((1,), (1,)), ((), ())), preferred_element_type=F32)


def one_hot(row, count):
    ids = lax.broadcasted_iota(jnp.int32, (count, row.shape[1]), 0).astype(F32)
    return jnp.where(ids == row, 1.0, 0.0).astype(BF16)


def pick(choices):
    group = lax.broadcasted_iota(jnp.int32, (8, 128), 1) // 32
    result = choices[-1]
    for i in reversed(range(len(choices) - 1)):
        result = jnp.where(group == i, choices[i], result)
    return result


def split_tiles(tall):
    turned = [tall] + [pltpu.roll(tall, 32 * a, 1) for a in range(1, 4)]
    return [
        pick([turned[(m - u) % 4][24 * h + 8 * m : 24 * h + 8 * m + 8] for m in range(3)])
        for h in range(tall.shape[0] // 24)
        for u in range(4)
    ]


def join_tiles(tiles):
    tall = jnp.concatenate(tiles, 0)
    turned = [tall] + [pltpu.roll(tall, 32 * a, 1) for a in range(1, 4)]
    return jnp.concatenate(
        [
            pick([turned[(u - m) % 4][8 * (4 * h + u) : 8 * (4 * h + u) + 8] for u in range(4)])
            for h in range(len(tiles) // 4)
            for m in range(3)
        ],
        0,
    )


def swap_groups(parts):
    rows = parts[0].shape[0]
    tall = jnp.concatenate([p[:, 128 * m : 128 * m + 128] for p in parts for m in range(2)], 0)
    turned = [tall] + [pltpu.roll(tall, 32 * a, 1) for a in range(1, 4)]
    group = lax.broadcasted_iota(jnp.int32, (rows, 128), 1) // 32
    result = []
    for j in range(8):
        m, g = j // 4, j % 4
        tiles = []
        for t in range(2):
            tile = None
            for u in range(4):
                at = (2 * (4 * t + u) + m) * rows
                piece = turned[(u - g) % 4][at : at + rows]
                tile = piece if tile is None else jnp.where(group == u, piece, tile)
            tiles.append(tile)
        result.append(jnp.concatenate(tiles, 1))
    return result


def body(
    feats_in, owner_in, place_in, nbr_in, w_in_in, w_mid_in, sel_in, ec_in, eh_in, cm_in,
    grid_out, point_out,
    feats, owner, place, nbr, w_in, w_mid, sel, ec, eh, cm, sem_in, index,
    send_a, recv_a, send_b, recv_b, x_one, c_one, h_send, h_recv, x_two, face_one, face_two, w_all, w_send_two, w_recv_two,
    w_one, w_two, lot_p, hi_p, lot_s, hi_s, pad_one, pad_two, ret_a, ret_v, taken,
    sent, got, got_z, got_p, got_ret,
):
    s = lax.axis_index("space")
    q = lax.axis_index("chan")
    core = s % 2
    z = (s // 2) % DEPTH
    row = s // (2 * DEPTH)
    plane = row * 2 + core
    spaces = 64

    def far_peer(d, e):
        other = (plane + e + PLANE) % PLANE
        return {"space": ((other // 2) * DEPTH + (z + d + DEPTH) % DEPTH) * 2 + other % 2, "chan": q}

    def x_peer(d):
        return {"space": s, "chan": (q + d) % CHAN}

    def s_peer(d):
        return {"space": (s + d + spaces) % spaces, "chan": q}

    def send(src, dst, sent, got, peer):
        copy = pltpu.make_async_remote_copy(
            src_ref=src, dst_ref=dst, send_sem=sent, recv_sem=got, device_id=peer, device_id_type=MESH
        )
        copy.start()
        return copy

    def drain(ref, sem):
        pltpu.make_async_copy(ref, ref, sem).wait()

    fetches = [
        pltpu.make_async_copy(src, dst, sem_in.at[(0, 0, 0, 1, 2, 3, 4, 5, 6, 5)[i]])
        for i, (src, dst) in enumerate(
            (
                (owner_in, owner), (place_in, place), (feats_in, feats), (w_in_in, w_in), (w_mid_in, w_mid),
                (nbr_in, nbr), (sel_in, sel), (ec_in, ec), (eh_in, eh), (cm_in, cm),
            )
        )
    ]
    for copy in fetches:
        copy.start()
    peers = (
        [far_peer(0, e) for e in FAR_FIRST]
        + [far_peer(d, 0) for d in FAR_FIRST]
        + [s_peer(1), s_peer(-1)]
        + [x_peer(d) for d in range(1, CHAN)]
    )
    barrier = pltpu.get_barrier_semaphore()
    for peer in peers:
        pl.semaphore_signal(barrier, inc=1, device_id=peer, device_id_type=MESH)

    drain(x_two.at[0, 0:40], sem_in.at[0])

    own = owner[...]
    where_to = place[...]
    match = jnp.where(lax.broadcasted_iota(jnp.int32, (64, 1024), 0) == own, 1.0, 0.0)
    tall = jnp.concatenate([match[:, 256 * i : 256 * i + 256] for i in range(4)], 0)
    before = jnp.where(
        lax.broadcasted_iota(jnp.int32, (256, 256), 0) < lax.broadcasted_iota(jnp.int32, (256, 256), 1), 1.0, 0.0
    )
    earlier = dot(tall.astype(BF16), before.astype(BF16))
    carry = jnp.zeros((64, 1), F32)
    ranks = []
    for i in range(4):
        mine = tall[64 * i : 64 * i + 64]
        ranks.append(jnp.sum(mine * (earlier[64 * i : 64 * i + 64] + carry), axis=0, keepdims=True))
        carry = carry + jnp.sum(mine, axis=1, keepdims=True)
    rank = jnp.concatenate(ranks, 1)
    to_z = ((own // 2) - z) & 7
    to_plane = ((own // (2 * DEPTH)) * 2 + (own & 1) - plane) & 7
    hi = (to_plane * 2 + to_z // 4).astype(F32)
    lo = ((to_z & 3) * CAP).astype(F32) + rank
    hot = one_hot(lo, 128)
    lot_p[...] = hot
    hi_p[...] = jnp.broadcast_to(hi, (8, 1024))
    extra = lax.broadcasted_iota(jnp.int32, (8, 1024), 0)
    extra = jnp.where(
        extra == 0, (where_to // 128).astype(F32), jnp.where(extra == 1, (where_to % 128).astype(F32), 0.0)
    )
    full = jnp.concatenate([feats[...].astype(F32), extra], 0)
    hi_wide = jnp.broadcast_to(hi, (24, 1024))
    spread = jnp.concatenate([jnp.where(hi_wide == float(h), full, 0.0).astype(BF16) for h in range(16)], 0)
    packed = dot_lanes(spread, hot)
    for h in range(16):
        send_a[h // 2, :, 128 * (h % 2) : 128 * (h % 2) + 128] = packed[24 * h : 24 * h + 24].astype(BF16)

    pl.semaphore_wait(barrier, len(peers))

    for e in FAR_FIRST:
        send(send_a.at[e], recv_a.at[e], sent.at[0], got.at[0], far_peer(0, e))
    for i in (3, 4, 5, 6, 8):
        fetches[i].wait()
    drain(ret_v, sem_in.at[5])

    lane = lax.broadcasted_iota(jnp.int32, (1, 128), 1)
    for d in range(1, CHAN):
        send(w_in, w_all.at[d], sent.at[1], got.at[1], x_peer(d))
    zero = jnp.zeros((24, 32), F32)
    for i in range(3):
        slabs = [jnp.concatenate([w_mid[9 * i + jl].astype(F32), zero], 1) for jl in range(TAPS)]
        for k in range(CHAN):
            tiles = []
            for group in (range(0, 5), range(5, 9)):
                tile = jnp.zeros((24, 128), F32)
                for u, jl in enumerate(group):
                    moved = pltpu.roll(slabs[jl], (24 * u - 24 * k) % 128, 1)
                    tile = jnp.where((lane >= 24 * u) & (lane < 24 * u + 24), moved, tile)
                tiles.append(tile)
            w_send_two[k, i] = jnp.concatenate(tiles, 1).astype(BF16)
    for d in range(1, CHAN):
        send(w_send_two.at[(q + d) % CHAN], w_recv_two.at[d], sent.at[0], got.at[2], x_peer(d))

    drain(recv_a.at[1:8], got.at[0])
    parts = [send_a[0].astype(F32)] + [recv_a[e].astype(F32) for e in range(1, PLANE)]
    for d, part in enumerate(swap_groups(parts)):
        send_b[d] = part.astype(BF16)
    second = {d: send(send_b.at[d], recv_b.at[d], sent.at[0], got_z.at[d - 1], far_peer(d, 0)) for d in FAR_FIRST}

    none = 36
    for b in range(BRICKS):
        for f in range(6):
            local = nbr[b, f] - BRICKS * s + BRICKS
            there = (nbr[b, f] >= 0) & (local >= 0) & (local < 3 * BRICKS)
            base = (local >> 2) * 12 + f // 2
            index[0, 6 * b + f] = jnp.where(there, base + 3 * (local & 3), none)
            index[1, 6 * b + f] = jnp.where(there, base + 3 * ((q - local) & 3), none)

    cells = jnp.zeros((256, 128), F32)
    for d in (0, 1, 7, 2, 6, 3, 5, 4):
        at = slice(256 * d, 256 * d + 256)
        if d:
            second[d].wait_recv()
        slots = (recv_b if d else send_b)[d].astype(F32)
        hi = slots[16:17]
        hot = one_hot(slots[17:18], 128)
        lot_s[:, at] = hot
        hi_s[:, at] = jnp.broadcast_to(hi, (8, 256))
        hi_wide = jnp.broadcast_to(hi, (16, 256))
        spread = [jnp.where(hi_wide == float(h), slots[0:16], 0.0).astype(BF16) for h in range(16)]
        cells = cells + dot_lanes(jnp.concatenate(spread, 0), hot)
    for h in range(16):
        x_one[h // 4, :, 128 * (h % 4) : 128 * (h % 4) + 128] = cells[16 * h : 16 * h + 16].astype(BF16)

    def rim(face, b, p, relative):
        low, high = (face[index[relative, 6 * b + f]].astype(F32) for f in (2 * p, 2 * p + 1))
        return jnp.where(lax.broadcasted_iota(jnp.int32, low.shape, 1) < 64, low, high)

    def tap_sum(full, count, taps):
        total = None
        for at, shift in taps:
            term = full[at : at + count]
            term = jnp.concatenate([term[:, 128 * x : 128 * x + 128] for x in range(8)], 0)
            if shift:
                term = pltpu.roll(term, 128 - shift, 1)
            total = term if total is None else total + term
        return total

    def pack_planes(layer, count):
        return [
            jnp.concatenate(
                [layer[count * (2 * p) : count * (2 * p + 1)], layer[count * (2 * p + 1) : count * (2 * p + 2)]], 1
            )
            for p in range(4)
        ]

    rims = dot(jnp.concatenate([x_one[b] for b in range(BRICKS)], 0), sel[...])
    for b in range(BRICKS):
        for p in range(3):
            face_one[12 + 3 * b + p] = rims[16 * b : 16 * b + 16, 128 * p : 128 * p + 128].astype(BF16)
    face_one[none] = jnp.zeros((16, 128), BF16)
    face_two[none] = jnp.zeros((ALL, 128), BF16)
    for e in (0, 1):
        send(face_one.at[12:24], face_one.at[24 * e : 24 * e + 12], sent.at[0], got.at[3], s_peer(1 - 2 * e))
    for d in (2, 1, 3):
        send(x_one.at[(q + d) % CHAN], c_one.at[d], sent.at[0], got.at[4], x_peer(d))
    drain(w_all.at[1:4], got.at[1])
    drain(w_recv_two.at[1:4], got.at[2])
    zero = jnp.zeros((9 * 64, 32), F32)
    for l in range(3):
        pieces = [(w_in if r == 0 else w_all.at[r])[3 * ij + l].astype(F32) for ij in range(9) for r in range(CHAN)]
        tall = jnp.concatenate([jnp.concatenate(pieces, 0), zero], 1)
        w_one[ALL * l : ALL * l + ALL, 0 : 9 * 64] = tall.T[0:ALL].astype(BF16)
    w_recv_two[0] = w_send_two[q]
    pieces = [w_recv_two[(q - k + CHAN) % CHAN, i].astype(F32) for i in range(3) for k in range(CHAN)]
    turned = jnp.concatenate(pieces + [jnp.zeros((ALL, 256), F32)], 0).T[:ROWS]
    out_id = lax.broadcasted_iota(jnp.int32, (ROWS, 384), 0) - tap_row(4)
    in_id = lax.broadcasted_iota(jnp.int32, (ROWS, 384), 1) - 3 * ALL - OUT * q
    same = (out_id == in_id) & (out_id >= 0) & (out_id < OUT)
    w_two[...] = jnp.where(same, 1.0, turned).astype(BF16)

    drain(face_one.at[0:24], got.at[3])
    for b in range(BRICKS):
        for p in range(3):
            h_send[b, p] = rim(face_one, b, p, 0).astype(BF16)
    for d in (2, 1, 3):
        send(h_send.at[(q + d) % CHAN], h_recv.at[d], sent.at[0], got.at[5], x_peer(d))
    drain(c_one.at[1:4], got.at[4])
    parts = [x_one[q].astype(F32)] + [c_one[r].astype(F32) for r in range(1, CHAN)]
    tiles = [part[:, 128 * p : 128 * p + 128] for part in parts for p in range(4)]
    inner = dot(jnp.concatenate(tiles, 0).astype(BF16), ec[...])
    drain(h_recv.at[1:4], got.at[5])
    edges = [jnp.concatenate([h_send[q, p]] + [h_recv[r, p] for r in range(1, CHAN)], 0) for p in range(3)]
    ends = dot(edges[0], ec[...]).astype(BF16)
    outer = dot(jnp.concatenate(edges[1:], 1), eh[...])
    planes = [ends[:, 0:128]]
    for p in range(4):
        mid = jnp.concatenate([inner[(4 * r + p) * 16 : (4 * r + p + 1) * 16] for r in range(CHAN)], 0)
        mid = (mid + outer[:, 256 * p : 256 * p + 256]).astype(BF16)
        planes += [mid[:, 0:128], mid[:, 128:256]]
    planes.append(ends[:, 128:256])
    for x, part in enumerate(planes):
        for j in range(3):
            pad_one[j, :, 128 * x : 128 * x + 128] = pltpu.roll(part, 128 - 10 * j, 1) if j else part
    deep = jnp.concatenate([pad_one[j, :, 128 * i : 128 * i + 1024] for i in range(3) for j in range(3)], 0)
    layer = tap_sum(dot(w_one[:, 0 : 9 * 64], deep), ALL, [(ALL * l, l) for l in range(3)])
    layer = jnp.maximum(layer, 0.0).astype(BF16).astype(F32)
    cells = dot(jnp.concatenate(pack_planes(layer, ALL), 0).astype(BF16), cm[...])
    for p in range(4):
        x_two[0, :, 128 * p : 128 * p + 128] = cells[ALL * p : ALL * p + ALL].astype(BF16)

    def piece(slot, t):
        return x_two.at[slot, 16 * t : 16 * t + 16]

    right, left = {}, {}
    for t in range(6):
        right[t] = send(piece(0, t), piece(1, t), sent.at[0], got_p.at[t if t < 3 else 6], x_peer(1))
        u = (t + 3) % 6
        left[u] = send(piece(0, u), piece(3, u), sent.at[0], got_p.at[u if u >= 3 else 7], x_peer(3))

    def send_faces(r, at):
        for e in (0, 1):
            src = face_two.at[12 + 3 * r : 15 + 3 * r, at]
            dst = face_two.at[24 * e + 3 * r : 24 * e + 3 * r + 3, at]
            send(src, dst, sent.at[2], got.at[6], s_peer(1 - 2 * e))

    def faces(r):
        rims = dot(x_two[r], sel[...])
        for p in range(3):
            face_two[12 + 3 * r + p] = rims[:, 128 * p : 128 * p + 128].astype(BF16)
        send_faces(r, slice(0, ALL))

    faces(0)
    for t in range(3):
        right[t].wait_recv()
        send(piece(1, t), piece(2, t), sent.at[0], got_p.at[8 + t], x_peer(1))
        left[3 + t].wait_recv()
        send(piece(3, 3 + t), piece(2, 3 + t), sent.at[0], got_p.at[8 + t], x_peer(3))
    drain(x_two.at[1, 48:96], got_p.at[6])
    faces(1)
    drain(x_two.at[3, 0:48], got_p.at[7])
    faces(3)
    for t in range(3):
        drain(x_two.at[2, 0:32], got_p.at[8 + t])
        rows = [slice(16 * u, 16 * u + 16) for u in (t, 3 + t)]
        rims = dot(jnp.concatenate([x_two[2, at] for at in rows], 0), sel[...])
        for half, at in enumerate(rows):
            for p in range(3):
                face_two[18 + p, at] = rims[16 * half : 16 * half + 16, 128 * p : 128 * p + 128].astype(BF16)
            send_faces(2, at)
    bricks = [x_two[(q - b + CHAN) % CHAN] for b in range(BRICKS)]
    tiles = [brick[:, 128 * p : 128 * p + 128] for brick in bricks for p in range(4)]
    inner = dot(jnp.concatenate(tiles, 0), ec[...])
    drain(face_two.at[0:24], got.at[6])
    edges = [
        jnp.concatenate([rim(face_two, b, p, 1).astype(BF16) for b in range(BRICKS)], 0) for p in range(3)
    ]
    ends = dot(edges[0], ec[...]).astype(BF16)
    outer = dot(jnp.concatenate(edges[1:], 1), eh[...])
    layers = []
    for b in range(BRICKS):
        pad_two[b, :, 0:128] = ends[ALL * b : ALL * b + ALL, 0:128]
        pad_two[b, :, 1152:1280] = ends[ALL * b : ALL * b + ALL, 128:256]
        for p in range(4):
            mid = inner[(4 * b + p) * ALL : (4 * b + p + 1) * ALL]
            mid = mid + outer[ALL * b : ALL * b + ALL, 256 * p : 256 * p + 256]
            pad_two[b, :, 128 + 256 * p : 384 + 256 * p] = mid.astype(BF16)
        deep = jnp.concatenate([pad_two[b, :, 128 * i : 128 * i + 1024] for i in (0, 1, 2, 1)], 0)
        layer = tap_sum(dot(w_two[...], deep), OUT, [(tap_row(jl), 10 * (jl // 3) + jl % 3) for jl in range(TAPS)])
        layers += pack_planes(jnp.maximum(layer, 0.0), OUT)
    closed = dot(jnp.concatenate(layers, 0).astype(BF16), cm[...])
    cells = closed.astype(BF16)

    for d in [*FAR_FIRST, 0]:
        at = slice(256 * d, 256 * d + 256)
        found = dot(cells, lot_s[:, at])
        hi_wide = jnp.broadcast_to(hi_s[0:1, at], (OUT, 256))
        value = found[0:OUT]
        for h in range(1, 16):
            value = jnp.where(hi_wide == float(h), found[OUT * h : OUT * h + OUT], value)
        tiles = split_tiles(jnp.concatenate([value[:, 0:128], value[:, 128:256]], 0))
        for e in range(PLANE):
            (ret_a if d or e else ret_v)[DEPTH * e + d] = tiles[e].astype(BF16)
        for e in [*FAR_FIRST, 0]:
            if d or e:
                at = DEPTH * e + d
                stage = 0 if e in (0, 1, 7) else 1 if e in (2, 6) else 2
                send(ret_a.at[at], ret_v.at[at], sent.at[3], got_ret.at[stage], far_peer(-d, -e))
    for p in range(4):
        tiles = [closed[OUT * (4 * b + p) : OUT * (4 * b + p) + OUT] for b in range(BRICKS)]
        grid_out[:, :, 128 * p : 128 * p + 128] = jnp.stack(tiles, 1).astype(BF16)
    for i, ref in enumerate((face_two.at[0:31], w_all.at[1:4], face_two.at[0:24], ret_a.at[1:64])):
        drain(ref, sent.at[i])
    hi_wide = jnp.broadcast_to(hi_p[0:1], (OUT, 1024))
    for stage, near in enumerate(((0, 1, 7), (2, 6), (3, 5, 4))):
        ids = [DEPTH * e + d for e in near for d in range(DEPTH)]
        drain(ret_v.at[1 if stage == 0 else 0 : len(ids)], got_ret.at[stage])
        lines = join_tiles([ret_v[at].astype(F32) for at in ids])
        found = dot(lines.astype(BF16), lot_p[...])
        value = taken[...] if 0 not in near else jnp.zeros((OUT, 1024), F32)
        for i, h in enumerate(2 * e + half for e in near for half in (0, 1)):
            value = jnp.where(hi_wide == float(h), found[OUT * i : OUT * i + OUT], value)
        taken[...] = value
    point_out[...] = value.astype(BF16)


def deliver(grid, values, grid_out, point_out, sems):
    copies = [pltpu.make_async_copy(a, b, sems.at[i]) for i, (a, b) in enumerate(((grid, grid_out), (values, point_out)))]
    for copy in copies:
        copy.start()
    for copy in copies:
        copy.wait()


def per_device(point_feats, point_owner, point_place, neighbors, weight_in, weight_mid):
    anywhere = pl.BlockSpec(memory_space=pl.ANY)
    constants = [jnp.asarray(c(), BF16) for c in (face_picker, plane_spread, rim_spread, plane_pack)]
    points = point_feats.shape[1]
    grid, values = pl.pallas_call(
        body,
        out_shape=(
            pltpu.VMEM((OUT, BRICKS, CELLS), BF16),
            pltpu.VMEM((OUT, points), BF16),
        ),
        in_specs=[anywhere] * 10,
        out_specs=(pl.BlockSpec(memory_space=pltpu.VMEM), pl.BlockSpec(memory_space=pltpu.VMEM)),
        scratch_shapes=[
            pltpu.VMEM((16, points), BF16),
            pltpu.VMEM((1, points), jnp.int32),
            pltpu.VMEM((1, points), jnp.int32),
            pltpu.SMEM((4, 6), jnp.int32),
            pltpu.VMEM((27, 16, 96), BF16),
            pltpu.VMEM((27, 24, 96), BF16),
            *[pltpu.VMEM(c.shape, BF16) for c in constants],
            pltpu.SemaphoreType.DMA((7,)),
            pltpu.SMEM((2, 24), jnp.int32),
            pltpu.VMEM((8, 24, 256), BF16),
            pltpu.VMEM((8, 24, 256), BF16),
            pltpu.VMEM((8, 24, 256), BF16),
            pltpu.VMEM((8, 24, 256), BF16),
            pltpu.VMEM((4, 16, CELLS), BF16),
            pltpu.VMEM((4, 16, CELLS), BF16),
            pltpu.VMEM((4, 3, 16, 128), BF16),
            pltpu.VMEM((4, 3, 16, 128), BF16),
            pltpu.VMEM((4, ALL, CELLS), BF16),
            pltpu.VMEM((37, 16, 128), BF16),
            pltpu.VMEM((37, ALL, 128), BF16),
            pltpu.VMEM((4, 27, 16, 96), BF16),
            pltpu.VMEM((4, 3, 24, 256), BF16),
            pltpu.VMEM((4, 3, 24, 256), BF16),
            pltpu.VMEM((3 * ALL, 640), BF16),
            pltpu.VMEM((ROWS, 384), BF16),
            pltpu.VMEM((128, points), BF16),
            pltpu.VMEM((8, points), F32),
            pltpu.VMEM((128, VOX), BF16),
            pltpu.VMEM((8, VOX), F32),
            pltpu.VMEM((3, 64, 1280), BF16),
            pltpu.VMEM((4, ALL, 1280), BF16),
            pltpu.VMEM((64, 8, 128), BF16),
            pltpu.VMEM((64, 8, 128), BF16),
            pltpu.VMEM((OUT, points), F32),
            pltpu.SemaphoreType.DMA((4,)),
            pltpu.SemaphoreType.DMA((7,)),
            pltpu.SemaphoreType.DMA((7,)),
            pltpu.SemaphoreType.DMA((11,)),
            pltpu.SemaphoreType.DMA((3,)),
        ],
        compiler_params=pltpu.CompilerParams(collective_id=0, has_side_effects=True),
    )(
        point_feats,
        point_owner.reshape(1, points),
        point_place.reshape(1, points),
        neighbors,
        jnp.transpose(weight_in, (1, 0, 2)),
        jnp.transpose(weight_mid, (1, 0, 2)),
        *constants,
    )
    grid, values = (pltpu.with_memory_space_constraint(a, pltpu.VMEM) for a in (grid, values))
    return pl.pallas_call(
        deliver,
        out_shape=(
            jax.ShapeDtypeStruct((OUT, BRICKS, CELLS), BF16),
            jax.ShapeDtypeStruct((OUT, points), BF16),
        ),
        in_specs=[pl.BlockSpec(memory_space=pltpu.VMEM)] * 2,
        out_specs=(anywhere, anywhere),
        scratch_shapes=[pltpu.SemaphoreType.DMA((2,))],
    )(grid, values)


def solution(mesh):
    return jax.shard_map(
        per_device,
        mesh=mesh,
        in_specs=(
            P("chan", "space"),
            P("space", None),
            P("space"),
            P("space", None),
            P("chan", None, None),
            P("chan", None, None),
        ),
        out_specs=(P("chan", "space", None), P("chan", "space")),
        check_vma=False,
    )
```
